32 devices in a mesh: section: 2 (over core), dp: 8 (over z, x), seq: 2 (over y).
Axes of the slice: x: 2, y: 2, z: 4, core: 2. Of those that a mesh axis runs over, the one named last changes fastest.
Arguments:
- tokens: bfloat16 [4, 8, 1024, 768], P(None, 'dp', 'seq'), may hold values from -6 to 6
- segments: int32 [4, 8, 1024], P(None, 'dp'), may hold values from 0 to 4, as said below
- cotangent: bfloat16 [4, 8, 1024, 768], P(None, 'dp', 'seq'), may hold values from -6 to 6
- joint_weight: bfloat16 [2, 768, 2304], P('section'), may hold values from -0.21875 to 0.21875
- joint_bias: float32 [2, 2304], P('section'), may hold values from -2 to 2
- output_weight: bfloat16 [2, 768, 768], P('section'), may hold values from -0.21875 to 0.21875
- output_bias: float32 [2, 768], P('section'), may hold values from -2 to 2
- up_weight: bfloat16 [2, 768, 3072], P('section'), may hold values from -0.21875 to 0.21875
- up_bias: float32 [2, 3072], P('section'), may hold values from -2 to 2
- down_weight: bfloat16 [2, 3072, 768], P('section'), may hold values from -0.109375 to 0.109375
- down_bias: float32 [2, 768], P('section'), may hold values from -2 to 2
- first_gain: float32 [2, 768], P('section'), may hold values from 0.25 to 1.75
- inner_gain: float32 [2, 768], P('section'), may hold values from 0.25 to 1.75
- second_gain: float32 [2, 768], P('section'), may hold values from 0.25 to 1.75
- hidden_gain: float32 [2, 3072], P('section'), may hold values from 0.25 to 1.75
Outputs:
- hiddens: bfloat16 [2, 4, 8, 1024, 768], P('section', None, 'dp', 'seq')
- input_gradients: float32 [2, 4, 8, 1024, 768], P('section', None, 'dp', 'seq')
- joint_weight_gradient: float32 [2, 768, 2304], P('section', None, ('dp', 'seq'))
- joint_bias_gradient: float32 [2, 2304], P('section', ('dp', 'seq'))
- output_weight_gradient: float32 [2, 768, 768], P('section', None, ('dp', 'seq'))
- output_bias_gradient: float32 [2, 768], P('section', ('dp', 'seq'))
- up_weight_gradient: float32 [2, 768, 3072], P('section', None, ('dp', 'seq'))
- up_bias_gradient: float32 [2, 3072], P('section', ('dp', 'seq'))
- down_weight_gradient: float32 [2, 3072, 768], P('section', None, ('dp', 'seq'))
- down_bias_gradient: float32 [2, 768], P('section', ('dp', 'seq'))
- first_gain_gradient: float32 [2, 768], P('section', ('dp', 'seq'))
- inner_gain_gradient: float32 [2, 768], P('section', ('dp', 'seq'))
- second_gain_gradient: float32 [2, 768], P('section', ('dp', 'seq'))
- hidden_gain_gradient: float32 [2, 3072], P('section', ('dp', 'seq'))
The draws below stay inside these ranges and needn't reach their ends.
Inputs may be any that keep to these rules, and one draw needn't show every extreme that they name: `segments`: along a row the ids never fall, and the row starts with id 0.
All inputs are finite; a program needn't handle non-finite values.
Results may differ from the reference program's by a relative error of at most 0.015.
Values may be sent and summed in bfloat16 or wider, within the bound.
A program may use at most 512 MiB of HBM per device.

```python
import jax
import jax.numpy as jnp
from jax import lax

D = 768
HEAD_DIM = 64
FF = 3072
ROW_LEN = 1024
MICRO = 4
PIECE = 512
ROWS = 8


def draw_segments(key, part):
    keys = jax.random.split(jax.random.fold_in(key, 7), 4)
    shape = (MICRO, ROWS, 1)
    early_one = jax.random.randint(keys[0], shape, 1, PIECE)
    early_two = jax.random.randint(keys[1], shape, 1, PIECE)
    late_one = jax.random.randint(keys[2], shape, ROW_LEN - PIECE + 1, ROW_LEN)
    late_two = jax.random.randint(keys[3], shape, ROW_LEN - PIECE + 1, ROW_LEN)
    place = jnp.arange(ROW_LEN, dtype=jnp.int32)[None, None, :]
    total = (place >= early_one).astype(jnp.int32) + (place >= early_two).astype(jnp.int32)
    total = total + (place >= late_one).astype(jnp.int32) + (place >= late_two).astype(jnp.int32)
    return total.astype(jnp.int32)


def steps_of(key, extent, pieces, least, largest):
    def one(position, blocks):
        draws = jax.random.uniform(jax.random.fold_in(jax.random.fold_in(key, 6), position), (blocks,), jnp.float32, least / len(pieces), largest / len(pieces))
        return jnp.repeat(jnp.exp(draws), extent[position] // blocks).reshape((-1,) + (1,) * (len(extent) - position - 1))

    factor_of = one(*pieces[0])
    for cut in pieces[1:]:
        factor_of = factor_of * one(*cut)
    return factor_of


def scatter_about(key, dims, scale, bound, shards=(), kind=jnp.bfloat16):
    entries = jax.random.normal(key, dims, jnp.float32) * scale
    if len(shards) > 0:
        entries = steps_of(key, dims, shards, -0.22, 0.18) * entries
    return jnp.clip(entries, min=-bound, max=bound).astype(kind)


def setup_inputs(seed: int = 0) -> dict:
    streams_of = jax.random.split(jax.random.key(seed), 16)
    tokens = scatter_about(streams_of[0], (MICRO, ROWS, ROW_LEN, D), 1.0, 6.0, ((1, 8), (2, 2)))
    segments = draw_segments(jax.random.fold_in(streams_of[15], 71), 0)
    cotangent = scatter_about(streams_of[2], (MICRO, ROWS, ROW_LEN, D), 1.0, 6.0, ((1, 8), (2, 2)))
    joint_weight = scatter_about(streams_of[3], (2, D, 3 * D), D ** -0.5, 0.21875, ((0, 2),))
    joint_bias = scatter_about(streams_of[4], (2, 3 * D), 0.5, 2.0, ((0, 2),), jnp.float32)
    output_weight = scatter_about(streams_of[5], (2, D, D), D ** -0.5, 0.21875, ((0, 2),))
    output_bias = scatter_about(streams_of[6], (2, D), 0.5, 2.0, ((0, 2),), jnp.float32)
    up_weight = scatter_about(streams_of[7], (2, D, FF), D ** -0.5, 0.21875, ((0, 2),))
    up_bias = scatter_about(streams_of[8], (2, FF), 0.5, 2.0, ((0, 2),), jnp.float32)
    down_weight = scatter_about(streams_of[9], (2, FF, D), FF ** -0.5, 0.109375, ((0, 2),))
    down_bias = scatter_about(streams_of[10], (2, D), 0.5, 2.0, ((0, 2),), jnp.float32)
    first_gain = jnp.clip(1.0 + 0.15 * jax.random.normal(streams_of[11], (2, D), jnp.float32), 0.25, 1.75)
    inner_gain = jnp.clip(1.0 + 0.15 * jax.random.normal(streams_of[12], (2, D), jnp.float32), 0.25, 1.75)
    second_gain = jnp.clip(1.0 + 0.15 * jax.random.normal(streams_of[13], (2, D), jnp.float32), 0.25, 1.75)
    hidden_gain = jnp.clip(1.0 + 0.15 * jax.random.normal(streams_of[14], (2, FF), jnp.float32), 0.25, 1.75)
    return {"tokens": tokens, "segments": segments, "cotangent": cotangent, "joint_weight": joint_weight, "joint_bias": joint_bias, "output_weight": output_weight, "output_bias": output_bias, "up_weight": up_weight, "up_bias": up_bias, "down_weight": down_weight, "down_bias": down_bias, "first_gain": first_gain, "inner_gain": inner_gain, "second_gain": second_gain, "hidden_gain": hidden_gain}


EPSILON = 1e-05
MASKED = -1e+30

@jax.custom_vjp
def low(v):
    return lax.optimization_barrier(v.astype(jnp.bfloat16)).astype(jnp.float32)

@jax.custom_vjp
def low_back(v):
    return v

def low_keep(v):
    return (low(v), None)

def low_pass(kept, grad):
    return (grad,)

def back_keep(v):
    return (v, None)

def back_low(kept, grad):
    return (low(grad),)
low.defvjp(low_keep, low_pass)
low_back.defvjp(back_keep, back_low)

def layer_norm(value, gain):
    centered = value - lax.optimization_barrier(jnp.mean(value, axis=-1, keepdims=True))
    spread = lax.optimization_barrier(jnp.mean(centered * centered, axis=-1, keepdims=True))
    return centered * lax.rsqrt(spread + EPSILON) * gain

def rotate(value, cosine, sine):
    middle = value.shape[-1] // 2
    first, second = (value[..., :middle], value[..., middle:])
    return jnp.concatenate([first * cosine - second * sine, second * cosine + first * sine], axis=-1)

def product(left, right):
    return jnp.dot(left, right, precision=lax.Precision.HIGHEST, preferred_element_type=jnp.float32)

def layer_row(weights, state, labels):
    joint_weight, joint_bias, output_weight, output_bias, up_weight, up_bias, down_weight, down_bias, first_gain, inner_gain, second_gain, hidden_gain = weights
    length = state.shape[0]
    head_count = D // HEAD_DIM
    starts = lax.optimization_barrier(jnp.sum((labels[None, :] < labels[:, None]).astype(jnp.int32), axis=1))
    places = (jnp.arange(length, dtype=jnp.int32) - starts).astype(jnp.float32)
    inverse_rate = 1.0 / 10000.0 ** (jnp.arange(HEAD_DIM // 2, dtype=jnp.float32) * 2.0 / HEAD_DIM)
    angle = places[:, None, None] * inverse_rate
    cosine = jnp.cos(angle)
    sine = jnp.sin(angle)
    normed = low(layer_norm(state, first_gain))
    joint = low_back(product(normed, joint_weight) + joint_bias)
    query = low(rotate(joint[:, :D].reshape(length, head_count, HEAD_DIM), cosine, sine))
    key = low(rotate(joint[:, D:2 * D].reshape(length, head_count, HEAD_DIM), cosine, sine))
    value = low(joint[:, 2 * D:].reshape(length, head_count, HEAD_DIM))
    scores = low_back(jnp.einsum('qhd,khd->hqk', query, key, precision=lax.Precision.HIGHEST) * HEAD_DIM ** (-0.5))
    match = labels[:, None] == labels[None, :]
    scores = jnp.where(match[None], scores, MASKED)
    shares = low(jax.nn.softmax(scores, axis=-1))
    attended = low_back(jnp.einsum('hqk,khd->qhd', shares, value, precision=lax.Precision.HIGHEST).reshape(length, D))
    inner = low(layer_norm(attended, inner_gain))
    mixed = state + low_back(product(inner, output_weight) + output_bias)
    normed_two = low(layer_norm(mixed, second_gain))
    before = low_back(product(normed_two, up_weight) + up_bias)
    hidden = low(layer_norm(jax.nn.gelu(before, approximate=False), hidden_gain))
    return mixed + low_back(product(hidden, down_weight) + down_bias)

def reference(tokens, segments, cotangent, joint_weight, joint_bias, output_weight, output_bias, up_weight, up_bias, down_weight, down_bias, first_gain, inner_gain, second_gain, hidden_gain):
    every = (joint_weight, joint_bias, output_weight, output_bias, up_weight, up_bias, down_weight, down_bias, first_gain, inner_gain, second_gain, hidden_gain)
    every = tuple((item.astype(jnp.float32) for item in every))
    count = MICRO * ROWS
    states = tokens.astype(jnp.float32).reshape(count, ROW_LEN, D)
    labels = segments.reshape(count, ROW_LEN).astype(jnp.int32)
    outer = cotangent.astype(jnp.float32).reshape(count, ROW_LEN, D)
    layer_one = tuple((item[0] for item in every))
    layer_two = tuple((item[1] for item in every))
    checked = jax.checkpoint(layer_row)

    def forward(inputs, weights):
        return lax.map(lambda pair: checked(weights, pair[0], pair[1]), (inputs, labels))
    out_one, pull_one = jax.vjp(forward, states, layer_one)
    middle = low(out_one)
    final, pull_two = jax.vjp(forward, middle, layer_two)
    back_middle, grads_two = pull_two(outer)
    back_input, grads_one = pull_one(low(back_middle))
    shape = (2, MICRO, ROWS, ROW_LEN, D)
    hiddens = jnp.stack([middle, final]).astype(jnp.bfloat16).reshape(shape)
    input_gradients = jnp.stack([back_input, back_middle]).reshape(shape)
    grads = tuple((jnp.stack([first, second]) for first, second in zip(grads_one, grads_two)))
    return (hiddens, input_gradients, grads[0], grads[1], grads[2], grads[3], grads[4], grads[5], grads[6], grads[7], grads[8], grads[9], grads[10], grads[11])
```

```python
import functools
import math

import jax
import jax.numpy as jnp
from jax import lax
from jax.experimental import pallas as pl
from jax.experimental.pallas import tpu as pltpu
from jax.sharding import PartitionSpec as P

HEAD_DIM = 64


EPSILON = 1e-05
MASKED = -1e30


def passed_along(value, axis, by):
    devices = lax.axis_size(axis)
    pairs = [(i, i + by) for i in range(devices) if 0 <= i + by < devices]
    return lax.ppermute(value, axis, pairs)


def layer_norm(value, gain):
    centered = value - jnp.mean(value, axis=-1, keepdims=True)
    spread = jnp.mean(centered * centered, axis=-1, keepdims=True)
    return centered * lax.rsqrt(spread + EPSILON) * gain


def feed_norm(before, gain):
    return layer_norm(jax.nn.gelu(before, approximate=False), gain)


def rotate(value, cosine, sine):
    middle = value.shape[-1] // 2
    first, second = (value[..., :middle], value[..., middle:])
    return jnp.concatenate(
        [first * cosine - second * sine, second * cosine + first * sine], axis=-1
    )


def rotate_back(incoming, cosine, sine):
    middle = incoming.shape[-1] // 2
    first, second = (incoming[..., :middle], incoming[..., middle:])
    return jnp.concatenate(
        [first * cosine + second * sine, second * cosine - first * sine], axis=-1
    )


def layer_forward(state, labels, weights, part):
    (
        joint_weight,
        joint_bias,
        output_weight,
        output_bias,
        up_weight,
        up_bias,
        down_weight,
        down_bias,
        first_gain,
        inner_gain,
        second_gain,
        hidden_gain,
    ) = weights
    row_count, piece_len, model_width = state.shape
    head_count = model_width // HEAD_DIM
    shape_heads = (row_count, piece_len, head_count, HEAD_DIM)
    offset = part * piece_len
    local_labels = lax.dynamic_slice_in_dim(labels, offset, piece_len, 1)
    starts = jnp.sum((labels[:, None, :] < local_labels[:, :, None]).astype(jnp.int32), axis=-1)
    places = offset + jnp.arange(piece_len, dtype=jnp.int32)[None, :] - starts
    inverse_rate = 1.0 / 10000.0 ** (jnp.arange(HEAD_DIM // 2, dtype=jnp.float32) * 2.0 / HEAD_DIM)
    angle = places.astype(jnp.float32)[:, :, None, None] * inverse_rate
    cosine = jnp.cos(angle)
    sine = jnp.sin(angle)
    normed = layer_norm(state, first_gain).astype(jnp.bfloat16)
    joint = jnp.dot(normed, joint_weight, preferred_element_type=jnp.float32) + joint_bias
    query = rotate(joint[..., :model_width].reshape(shape_heads), cosine, sine).astype(jnp.bfloat16)
    key = rotate(
        joint[..., model_width : 2 * model_width].reshape(shape_heads), cosine, sine
    ).astype(jnp.bfloat16)
    value = joint[..., 2 * model_width :].reshape(shape_heads).astype(jnp.bfloat16)
    keys_all, values_all = (
        lax.all_gather(key, "seq", axis=1, tiled=True),
        lax.all_gather(value, "seq", axis=1, tiled=True),
    )
    match = local_labels[:, None, :, None] == labels[:, None, None, :]
    scores = jnp.einsum(
        "rqhd,rkhd->rhqk", query, keys_all, preferred_element_type=jnp.float32
    ) * HEAD_DIM ** (-0.5)
    scores = jnp.where(match, scores, MASKED)
    peak = jnp.max(scores, axis=-1, keepdims=True)
    raised = jnp.exp(scores - peak)
    total_raised = jnp.sum(raised, axis=-1, keepdims=True)
    shares = raised / total_raised
    log_total = peak + jnp.log(total_raised)
    attended = jnp.einsum(
        "rhqk,rkhd->rqhd",
        shares.astype(jnp.bfloat16),
        values_all,
        preferred_element_type=jnp.float32,
    ).reshape(row_count, piece_len, model_width)
    inner = layer_norm(attended, inner_gain).astype(jnp.bfloat16)
    mixed = state + jnp.dot(inner, output_weight, preferred_element_type=jnp.float32) + output_bias
    normed_two = layer_norm(mixed, second_gain).astype(jnp.bfloat16)
    before = jnp.dot(normed_two, up_weight, preferred_element_type=jnp.float32) + up_bias
    hidden = feed_norm(before, hidden_gain).astype(jnp.bfloat16)
    result = mixed + jnp.dot(hidden, down_weight, preferred_element_type=jnp.float32) + down_bias
    kept = (
        state,
        normed,
        query,
        keys_all,
        values_all,
        cosine,
        sine,
        match,
        shares,
        attended,
        inner,
        mixed,
        normed_two,
        before,
        hidden,
        log_total,
        labels,
    )
    return (result, kept)


def feed_backward(kept, slope_out, weights, totals):
    (
        state,
        normed,
        query,
        keys_all,
        values_all,
        cosine,
        sine,
        match,
        shares,
        attended,
        inner,
        mixed,
        normed_two,
        before,
        hidden,
        log_total,
        labels,
    ) = kept
    (
        joint_weight,
        joint_bias,
        output_weight,
        output_bias,
        up_weight,
        up_bias,
        down_weight,
        down_bias,
        first_gain,
        inner_gain,
        second_gain,
        hidden_gain,
    ) = weights
    slope_low = slope_out.astype(jnp.bfloat16)
    totals[6] = totals[6] + jnp.einsum(
        "rcf,rcd->fd", hidden, slope_low, preferred_element_type=jnp.float32
    )
    totals[7] = totals[7] + jnp.sum(slope_low.astype(jnp.float32), axis=(0, 1))
    slope_hidden = jnp.einsum(
        "rcd,fd->rcf", slope_low, down_weight, preferred_element_type=jnp.float32
    )
    unused, puller = jax.vjp(feed_norm, before, hidden_gain)
    slope_before, slope_gain = puller(slope_hidden)
    totals[11] = totals[11] + slope_gain
    before_low = slope_before.astype(jnp.bfloat16)
    totals[4] = totals[4] + jnp.einsum(
        "rcd,rcf->df", normed_two, before_low, preferred_element_type=jnp.float32
    )
    totals[5] = totals[5] + jnp.sum(before_low.astype(jnp.float32), axis=(0, 1))
    slope_normed = jnp.einsum(
        "rcf,df->rcd", before_low, up_weight, preferred_element_type=jnp.float32
    )
    unused, puller = jax.vjp(layer_norm, mixed, second_gain)
    slope_mixed, slope_gain = puller(slope_normed)
    totals[10] = totals[10] + slope_gain
    return (slope_out + slope_mixed, totals)


def attend_backward(kept, slope_mixed, weights, totals):
    (
        state,
        normed,
        query,
        keys_all,
        values_all,
        cosine,
        sine,
        match,
        shares,
        attended,
        inner,
        mixed,
        normed_two,
        before,
        hidden,
        log_total,
        labels,
    ) = kept
    (
        joint_weight,
        joint_bias,
        output_weight,
        output_bias,
        up_weight,
        up_bias,
        down_weight,
        down_bias,
        first_gain,
        inner_gain,
        second_gain,
        hidden_gain,
    ) = weights
    row_count, piece_len, model_width = state.shape
    head_count = model_width // HEAD_DIM
    scale = HEAD_DIM ** (-0.5)
    slope_low = slope_mixed.astype(jnp.bfloat16)
    totals[2] = totals[2] + jnp.einsum(
        "rcd,rce->de", inner, slope_low, preferred_element_type=jnp.float32
    )
    totals[3] = totals[3] + jnp.sum(slope_low.astype(jnp.float32), axis=(0, 1))
    slope_inner = jnp.einsum(
        "rce,de->rcd", slope_low, output_weight, preferred_element_type=jnp.float32
    )
    unused, puller = jax.vjp(layer_norm, attended, inner_gain)
    slope_attended, slope_gain = puller(slope_inner)
    totals[9] = totals[9] + slope_gain
    slope_heads = slope_attended.astype(jnp.bfloat16).reshape(
        row_count, piece_len, head_count, HEAD_DIM
    )
    slope_shares = jnp.einsum(
        "rqhd,rkhd->rhqk", slope_heads, values_all, preferred_element_type=jnp.float32
    )
    weighted = jnp.sum(shares * slope_shares, axis=-1, keepdims=True)
    slope_scores = (shares * (slope_shares - weighted)).astype(jnp.bfloat16)
    slope_query = (
        jnp.einsum("rhqk,rkhd->rqhd", slope_scores, keys_all, preferred_element_type=jnp.float32)
        * scale
    )
    shares_low = shares.astype(jnp.bfloat16)
    key_part = (
        jnp.einsum("rhqk,rqhd->krhd", slope_scores, query, preferred_element_type=jnp.float32)
        * scale
    )
    value_part = jnp.einsum(
        "rhqk,rqhd->krhd", shares_low, slope_heads, preferred_element_type=jnp.float32
    )
    summed = lax.psum_scatter(
        jnp.concatenate([key_part, value_part], axis=-1).astype(jnp.bfloat16),
        "seq",
        scatter_dimension=0,
        tiled=True,
    ).astype(jnp.float32)
    summed = jnp.transpose(summed, (1, 0, 2, 3))
    key_raw = summed[..., :HEAD_DIM]
    slope_value = summed[..., HEAD_DIM:]
    slope_key = rotate_back(key_raw, cosine, sine)
    slope_query = rotate_back(slope_query, cosine, sine)
    flat = (row_count, piece_len, model_width)
    slope_joint = jnp.concatenate(
        [slope_query.reshape(flat), slope_key.reshape(flat), slope_value.reshape(flat)], axis=-1
    ).astype(jnp.bfloat16)
    totals[0] = totals[0] + jnp.einsum(
        "rcd,rce->de", normed, slope_joint, preferred_element_type=jnp.float32
    )
    totals[1] = totals[1] + jnp.sum(slope_joint.astype(jnp.float32), axis=(0, 1))
    slope_normed = jnp.einsum(
        "rce,de->rcd", slope_joint, joint_weight, preferred_element_type=jnp.float32
    )
    unused, puller = jax.vjp(layer_norm, state, first_gain)
    slope_state, slope_gain = puller(slope_normed)
    totals[8] = totals[8] + slope_gain
    return (slope_mixed + slope_state, totals)


def lift(vector):
    return vector.reshape(1, vector.shape[0])


def shards(
    tokens,
    segments,
    cotangent,
    joint_weight,
    joint_bias,
    output_weight,
    output_bias,
    up_weight,
    up_bias,
    down_weight,
    down_bias,
    first_gain,
    inner_gain,
    second_gain,
    hidden_gain,
):
    weights = tuple(
        (
            item[0]
            for item in (
                joint_weight,
                joint_bias,
                output_weight,
                output_bias,
                up_weight,
                up_bias,
                down_weight,
                down_bias,
                first_gain,
                inner_gain,
                second_gain,
                hidden_gain,
            )
        )
    )
    micro, row_count, piece_len, model_width = tokens.shape
    leading = lax.axis_index("section") == 0
    part = lax.axis_index("seq")
    received = jnp.zeros((row_count, piece_len, model_width), jnp.bfloat16)
    saved = []
    results = []
    for moment in range(micro + 1):
        labels = jnp.where(leading, segments[min(moment, micro - 1)], segments[max(moment - 1, 0)])
        source = jnp.where(leading, tokens[min(moment, micro - 1)], received)
        state = source.astype(jnp.float32)
        result, kept = layer_forward(state, labels, weights, part)
        sent = result.astype(jnp.bfloat16)
        results.append(sent)
        saved.append((state, labels))
        if moment < micro:
            received = passed_along(sent, "section", 1)
    totals = [jnp.zeros(item.shape, jnp.float32) for item in weights]
    back_received = jnp.zeros((row_count, piece_len, model_width), jnp.bfloat16)
    back_results = []
    for moment in range(micro + 1):
        earlier = max(moment - 1, 0)
        later = min(moment + 1, micro)
        state = jnp.where(leading, saved[earlier][0], saved[later][0])
        labels = jnp.where(leading, saved[earlier][1], saved[later][1])
        kept = layer_forward(state, labels, weights, part)[1]
        if moment < micro:
            outer = cotangent[moment].astype(jnp.float32)
        else:
            outer = jnp.zeros((row_count, piece_len, model_width), jnp.float32)
        slope_out = jnp.where(leading, back_received.astype(jnp.float32), outer)
        slope_mixed, totals = feed_backward(kept, slope_out, weights, totals)
        slope_input, totals = attend_backward(kept, slope_mixed, weights, totals)
        back_results.append(slope_input)
        if moment < micro:
            back_received = passed_along(slope_input.astype(jnp.bfloat16), "section", -1)
    reduced = (
        lax.psum_scatter(totals[0], ("dp", "seq"), scatter_dimension=1, tiled=True),
        lax.psum_scatter(lift(totals[1]), ("dp", "seq"), scatter_dimension=1, tiled=True),
        lax.psum_scatter(totals[2], ("dp", "seq"), scatter_dimension=1, tiled=True),
        lax.psum_scatter(lift(totals[3]), ("dp", "seq"), scatter_dimension=1, tiled=True),
        lax.psum_scatter(totals[4], ("dp", "seq"), scatter_dimension=1, tiled=True),
        lax.psum_scatter(lift(totals[5]), ("dp", "seq"), scatter_dimension=1, tiled=True),
        lax.psum_scatter(totals[6], ("dp", "seq"), scatter_dimension=1, tiled=True),
        lax.psum_scatter(lift(totals[7]), ("dp", "seq"), scatter_dimension=1, tiled=True),
        lax.psum_scatter(lift(totals[8]), ("dp", "seq"), scatter_dimension=1, tiled=True),
        lax.psum_scatter(lift(totals[9]), ("dp", "seq"), scatter_dimension=1, tiled=True),
        lax.psum_scatter(lift(totals[10]), ("dp", "seq"), scatter_dimension=1, tiled=True),
        lax.psum_scatter(lift(totals[11]), ("dp", "seq"), scatter_dimension=1, tiled=True),
    )
    hiddens = jnp.stack(
        [jnp.where(leading, results[index], results[index + 1]) for index in range(micro)]
    )[None]
    input_gradients = jnp.stack(
        [jnp.where(leading, back_results[index + 1], back_results[index]) for index in range(micro)]
    )[None]
    return (
        hiddens,
        input_gradients,
        reduced[0][None],
        reduced[1],
        reduced[2][None],
        reduced[3],
        reduced[4][None],
        reduced[5],
        reduced[6][None],
        reduced[7],
        reduced[8],
        reduced[9],
        reduced[10],
        reduced[11],
    )


F32 = jnp.float32
BF16 = jnp.bfloat16
ANY = pl.BlockSpec(memory_space=pl.ANY)
SMEM = pl.BlockSpec(memory_space=pltpu.SMEM)
VLIM = 60 * 1024 * 1024


def lane_iota(shape):
    return lax.broadcasted_iota(jnp.int32, shape, len(shape) - 1)


def nn(a, b):
    return lax.dot_general(a, b, (((1,), (0,)), ((), ())), preferred_element_type=F32)


def nt(a, b):
    return lax.dot_general(a, b, (((1,), (1,)), ((), ())), preferred_element_type=F32)


def tn(a, b):
    return lax.dot_general(a, b, (((0,), (0,)), ((), ())), preferred_element_type=F32)


def normalize(value):
    centered = value - jnp.mean(value, axis=-1, keepdims=True)
    scale = lax.rsqrt(jnp.mean(centered * centered, axis=-1, keepdims=True) + EPSILON)
    return centered * scale, scale


def norm_back(slope, unit, scale):
    return scale * (
        slope
        - jnp.mean(slope, axis=-1, keepdims=True)
        - unit * jnp.mean(slope * unit, axis=-1, keepdims=True)
    )


def fold(value):
    rows, columns = value.shape
    return jnp.sum(value.reshape(rows // 8, 8, columns), axis=0)


def split3(value):
    high = value.astype(BF16)
    rest = value - high.astype(F32)
    middle = rest.astype(BF16)
    low = (rest - middle.astype(F32)).astype(BF16)
    return high, middle, low


def fetch_weights(layer, sec_ref, pairs, sem):
    @pl.when(pl.program_id(0) == 0)
    def _():
        @pl.when(sec_ref[0] == layer)
        def _():
            for index, (own, other, here) in enumerate(pairs):
                pltpu.make_async_copy(own, here, sem.at[index]).start()

        @pl.when(sec_ref[0] != layer)
        def _():
            for index, (own, other, here) in enumerate(pairs):
                pltpu.make_async_copy(other, here, sem.at[index]).start()

        for index, (own, other, here) in enumerate(pairs):
            pltpu.make_async_copy(own, here, sem.at[index]).wait()


def qkv_kernel(layer, sec_ref, x_ref, gain_ref, own_ref, other_ref, bias_ref, cos_ref, sin_ref,
               lab_ref, n_ref, q_ref, k_ref, v_ref, w_ref, sem):
    fetch_weights(layer, sec_ref, [(own_ref, other_ref, w_ref)], sem)
    width = x_ref.shape[-1]
    unit, scale = normalize(x_ref[...].astype(F32))
    normed = (unit * gain_ref[...]).astype(BF16)
    n_ref[...] = normed
    joint = nn(normed, w_ref[...]) + bias_ref[...]
    cosine, sine = cos_ref[...], sin_ref[...]
    lane = lane_iota(cosine.shape)
    first = lane % HEAD_DIM < HEAD_DIM // 2
    head = lane < HEAD_DIM
    labels = lab_ref[...]
    document = lane - HEAD_DIM
    known = (document >= 0) & (document < 5)
    q_feat = jnp.where(known & (document != labels), MASKED, 0.0)
    ones = (document >= 5) & (document < 8)
    k_feat = jnp.where((known & (document == labels)) | ones, 1.0, 0.0)
    v_feat = jnp.where((document >= 0) & (document < 3), 1.0, 0.0)
    for pair in range(width // 128):
        for which, (out, feat) in enumerate(((q_ref, q_feat), (k_ref, k_feat), (v_ref, v_feat))):
            begin = which * width + pair * 128
            part = joint[:, begin:begin + 128]
            if which < 2:
                turned = jnp.where(first, pltpu.roll(part, 96, 1), pltpu.roll(part, 32, 1))
                part = part * cosine + turned * sine
            part = part.astype(BF16).astype(F32)
            if which == 0:
                part = part * HEAD_DIM ** -0.5
            out[2 * pair] = jnp.where(head, part, feat).astype(BF16)
            out[2 * pair + 1] = jnp.where(head, pltpu.roll(part, 64, 1), feat).astype(BF16)


def qkv(layer, sec, x, gain, own, other, bias, cosine, sine, labels, tb=256):
    rows, width = x.shape
    heads = width // HEAD_DIM
    const = lambda shape: pl.BlockSpec(shape, lambda i: (0,) * len(shape))
    tok = lambda n: pl.BlockSpec((tb, n), lambda i: (i, 0))
    hd = pl.BlockSpec((heads, tb, 128), lambda i: (0, i, 0))
    return pl.pallas_call(
        functools.partial(qkv_kernel, layer),
        grid=(rows // tb,),
        in_specs=[SMEM, tok(width), const((1, width)), ANY, ANY, const((1, 3 * width)), tok(128), tok(128), tok(1)],
        out_specs=[tok(width), hd, hd, hd],
        out_shape=[jax.ShapeDtypeStruct((rows, width), BF16)] + [jax.ShapeDtypeStruct((heads, rows, 128), BF16)] * 3,
        scratch_shapes=[pltpu.VMEM(own.shape, BF16), pltpu.SemaphoreType.DMA((1,))],
        compiler_params=pltpu.CompilerParams(vmem_limit_bytes=VLIM),
        cost_estimate=pl.CostEstimate(flops=2 * rows * width * 3 * width, bytes_accessed=16 * 1024 * 1024, transcendentals=0),
        name="joint_projection",
    )(sec, x, gain, own, other, bias, cosine, sine, labels)


def attend_kernel(qb, q_ref, k_ref, v_ref, o_ref, ql_ref):
    rows = q_ref.shape[1]
    lane = lane_iota((qb, 128))
    for block in range(rows // qb):
        at = pl.ds(block * qb, qb)
        done = []
        for head in range(2):
            query = q_ref[head, at, :]
            scores = nt(query, k_ref[head])
            peak = jnp.max(scores, axis=-1, keepdims=True)
            raised = jnp.exp(scores - peak).astype(BF16)
            sums = nn(raised, v_ref[head])
            total = sums[:, HEAD_DIM:HEAD_DIM + 1]
            done.append(sums / total)
            high, middle, low = split3(-(peak + jnp.log(total)))
            feat = jnp.where(lane == 69, high.astype(F32), jnp.where(lane == 70, middle.astype(F32), low.astype(F32)))
            inside = (lane >= 69) & (lane < 72)
            ql_ref[head, at, :] = jnp.where(inside, feat, query.astype(F32)).astype(BF16)
        o_ref[at, :] = jnp.where(lane < HEAD_DIM, done[0], pltpu.roll(done[1], 64, 1))


def attend(q, k, v, qb=256):
    heads, rows, _ = q.shape
    hd = pl.BlockSpec((2, rows, 128), lambda i: (i, 0, 0))
    return pl.pallas_call(
        functools.partial(attend_kernel, qb),
        grid=(heads // 2,),
        in_specs=[hd, hd, hd],
        out_specs=[pl.BlockSpec((rows, 128), lambda i: (0, i)), hd],
        out_shape=[jax.ShapeDtypeStruct((rows, heads * HEAD_DIM), F32), jax.ShapeDtypeStruct(q.shape, BF16)],
        compiler_params=pltpu.CompilerParams(vmem_limit_bytes=VLIM),
        cost_estimate=pl.CostEstimate(flops=16 * heads * rows * rows * HEAD_DIM, bytes_accessed=16 * 1024 * 1024, transcendentals=0),
        name="attention_forward",
    )(q, k, v)


def feed_kernel(layer, sec_ref, at_ref, x_ref, ig_ref, ob_ref, sg_ref, ub_ref, hg_ref, db_ref,
                wo0, wo1, wu0, wu1, wd0, wd1,
                out_ref, mixed_ref, hid_ref, gp_ref, st_ref, wo, wu, wd, sem):
    fetch_weights(layer, sec_ref, [(wo0, wo1, wo), (wu0, wu1, wu), (wd0, wd1, wd)], sem)
    unit, _ = normalize(at_ref[...])
    inner = (unit * ig_ref[...]).astype(BF16)
    mixed = x_ref[...].astype(F32) + nn(inner, wo[...]) + ob_ref[...]
    mixed_ref[...] = mixed
    unit, _ = normalize(mixed)
    normed = (unit * sg_ref[...]).astype(BF16)
    before = nn(normed, wu[...]) + ub_ref[...]
    share = 0.5 + 0.5 * lax.erf(before * 0.5 ** 0.5)
    bell = jnp.exp(before * before * -0.5) * (1.0 / math.sqrt(2.0 * math.pi))
    gp_ref[...] = (share + before * bell).astype(BF16)
    unit, scale = normalize(before * share)
    hidden = (unit * hg_ref[...]).astype(BF16)
    hid_ref[...] = hidden
    st_ref[...] = jnp.broadcast_to(scale, st_ref.shape)
    out_ref[...] = (mixed + nn(hidden, wd[...]) + db_ref[...]).astype(BF16)


def feed(layer, sec, attended, x, ig, ob, sg, ub, hg, db, wo, wu, wd, tb=256):
    rows, width = x.shape
    wide = ub.shape[-1]
    const = lambda n: pl.BlockSpec((1, n), lambda i: (0, 0))
    tok = lambda n: pl.BlockSpec((tb, n), lambda i: (i, 0))
    S = jax.ShapeDtypeStruct
    return pl.pallas_call(
        functools.partial(feed_kernel, layer),
        grid=(rows // tb,),
        in_specs=[SMEM, tok(width), tok(width), const(width), const(width), const(width), const(wide), const(wide), const(width)] + [ANY] * 6,
        out_specs=[tok(width), tok(width), tok(wide), tok(wide), tok(128)],
        out_shape=[S((rows, width), BF16), S((rows, width), F32), S((rows, wide), BF16), S((rows, wide), BF16), S((rows, 128), F32)],
        scratch_shapes=[pltpu.VMEM(wo[0].shape, BF16), pltpu.VMEM(wu[0].shape, BF16), pltpu.VMEM(wd[0].shape, BF16), pltpu.SemaphoreType.DMA((3,))],
        compiler_params=pltpu.CompilerParams(vmem_limit_bytes=VLIM),
        cost_estimate=pl.CostEstimate(flops=2 * rows * width * (2 * wide + width), bytes_accessed=40 * 1024 * 1024, transcendentals=0),
        name="feed_forward",
    )(sec, attended, x, ig, ob, sg, ub, hg, db, *wo, *wu, *wd)


def feed_back_kernel(layer, sec_ref, c_ref, hid_ref, gp_ref, st_ref, mixed_ref, at_ref,
                     ig_ref, sg_ref, hg_ref, wo0, wo1, wu0, wu1, wd0, wd1,
                     cb_ref, cm_ref, cl_ref, ch_ref, n2_ref, in_ref, wide_ref, thin_ref,
                     wo, wu, wd, wide_acc, thin_acc, sem):
    step = pl.program_id(0)

    @pl.when(step == 0)
    def _():
        wide_acc[...] = jnp.zeros_like(wide_acc)
        thin_acc[...] = jnp.zeros_like(thin_acc)

    fetch_weights(layer, sec_ref, [(wo0, wo1, wo), (wu0, wu1, wu), (wd0, wd1, wd)], sem)
    low = c_ref[...]
    outer = low.astype(F32)
    thin_acc[0] += fold(outer)
    slope = nt(low, wd[...])
    hidden = hid_ref[...].astype(F32)
    gain = hg_ref[...]
    moved = slope * hidden
    wide_acc[0] += fold(moved)
    mean_moved = jnp.mean(moved, axis=-1, keepdims=True)
    slope = slope * gain
    mean_slope = jnp.mean(slope, axis=-1, keepdims=True)
    scale = st_ref[:, 0:1]
    slope = (slope - mean_slope - hidden * (1.0 / gain) * mean_moved) * scale
    before_low = (slope * gp_ref[...].astype(F32)).astype(BF16)
    cb_ref[...] = before_low
    wide_acc[1] += fold(before_low.astype(F32))
    slope = nt(before_low, wu[...])
    unit, scale = normalize(mixed_ref[...])
    n2_ref[...] = (unit * sg_ref[...]).astype(BF16)
    thin_acc[1] += fold(slope * unit)
    mixed = outer + norm_back(slope * sg_ref[...], unit, scale)
    cm_ref[...] = mixed
    mixed_low = mixed.astype(BF16)
    cl_ref[...] = mixed_low
    thin_acc[2] += fold(mixed_low.astype(F32))
    slope = nt(mixed_low, wo[...])
    unit, scale = normalize(at_ref[...])
    in_ref[...] = (unit * ig_ref[...]).astype(BF16)
    thin_acc[3] += fold(slope * unit)
    ch_ref[...] = norm_back(slope * ig_ref[...], unit, scale).astype(BF16)

    @pl.when(step == pl.num_programs(0) - 1)
    def _():
        inverse = 1.0 / gain
        wide_ref[0:1, :] = jnp.sum(wide_acc[0], axis=0, keepdims=True) * inverse
        wide_ref[1:2, :] = jnp.sum(wide_acc[1], axis=0, keepdims=True)
        for index in range(4):
            thin_ref[index:index + 1, :] = jnp.sum(thin_acc[index], axis=0, keepdims=True)


def feed_back(layer, sec, c, hidden, gp, st, mixed, attended, ig, sg, hg, wo, wu, wd, tb=256):
    rows, width = c.shape
    wide = hg.shape[-1]
    const = lambda n, m=1: pl.BlockSpec((m, n), lambda i: (0, 0))
    tok = lambda n: pl.BlockSpec((tb, n), lambda i: (i, 0))
    S = jax.ShapeDtypeStruct
    return pl.pallas_call(
        functools.partial(feed_back_kernel, layer),
        grid=(rows // tb,),
        in_specs=[SMEM, tok(width), tok(wide), tok(wide), tok(128), tok(width), tok(width), const(width), const(width), const(wide)] + [ANY] * 6,
        out_specs=[tok(wide), tok(width), tok(width), tok(width), tok(width), tok(width), const(wide, 2), const(width, 4)],
        out_shape=[S((rows, wide), BF16), S((rows, width), F32), S((rows, width), BF16), S((rows, width), BF16), S((rows, width), BF16), S((rows, width), BF16), S((2, wide), F32), S((4, width), F32)],
        scratch_shapes=[pltpu.VMEM(wo[0].shape, BF16), pltpu.VMEM(wu[0].shape, BF16), pltpu.VMEM(wd[0].shape, BF16),
                        pltpu.VMEM((2, 8, wide), F32), pltpu.VMEM((4, 8, width), F32), pltpu.SemaphoreType.DMA((3,))],
        compiler_params=pltpu.CompilerParams(vmem_limit_bytes=VLIM),
        cost_estimate=pl.CostEstimate(flops=2 * rows * width * (2 * wide + width), bytes_accessed=50 * 1024 * 1024, transcendentals=0),
        name="feed_backward",
    )(sec, c, hidden, gp, st, mixed, attended, ig, sg, hg, *wo, *wu, *wd)


def attend_back_kernel(qb, q_ref, k_ref, v_ref, ch_ref, at_ref, cos_ref, sin_ref, cj_ref, kt, vt, qs):
    rows = q_ref.shape[1]
    lane = lane_iota((rows, 128))
    is_head = lane < HEAD_DIM
    slopes = ch_ref[...].astype(F32)
    product = slopes * at_ref[...]
    for head in range(2):
        mine = is_head if head == 0 else jnp.logical_not(is_head)
        weighted = jnp.sum(jnp.where(mine, product, 0.0), axis=-1, keepdims=True)
        high, middle, low = split3(-weighted)
        feat = jnp.where(lane == 64, high.astype(F32), jnp.where(lane == 65, middle.astype(F32), jnp.where(lane == 66, low.astype(F32), 0.0)))
        local = slopes if head == 0 else pltpu.roll(slopes, 64, 1)
        c_aug = jnp.where(is_head, local, feat).astype(BF16)
        keys, values = k_ref[head], v_ref[head]
        for block in range(rows // qb):
            at = pl.ds(block * qb, qb)
            query = q_ref[head, at, :]
            incoming = c_aug[block * qb:(block + 1) * qb, :]
            shares = jnp.exp(nt(query, keys))
            slope = (shares * nt(incoming, values)).astype(BF16)
            qs[head, at, :] = nn(slope, keys)
            key_part = tn(query, slope)[:HEAD_DIM]
            value_part = tn(incoming, shares.astype(BF16))[:HEAD_DIM]
            rng = pl.ds(head * HEAD_DIM, HEAD_DIM)
            if block == 0:
                kt[rng, :] = key_part
                vt[rng, :] = value_part
            else:
                kt[rng, :] += key_part
                vt[rng, :] += value_part
    cosine, sine = cos_ref[...], sin_ref[...]
    first = lane % HEAD_DIM < HEAD_DIM // 2
    def back(part):
        turned = jnp.where(first, pltpu.roll(part, 96, 1), pltpu.roll(part, 32, 1))
        return (part * cosine - turned * sine).astype(BF16)
    cj_ref[0] = back(jnp.where(is_head, qs[0], pltpu.roll(qs[1], 64, 1)) * HEAD_DIM ** -0.5)
    cj_ref[1] = back(kt[...].T)
    cj_ref[2] = vt[...].T.astype(BF16)


def attend_back(q, k, v, ch, attended, cosine, sine, qb=256):
    heads, rows, _ = q.shape
    width = heads * HEAD_DIM
    hd = pl.BlockSpec((2, rows, 128), lambda i: (i, 0, 0))
    col = pl.BlockSpec((rows, 128), lambda i: (0, i))
    con = pl.BlockSpec((rows, 128), lambda i: (0, 0))
    return pl.pallas_call(
        functools.partial(attend_back_kernel, qb),
        grid=(heads // 2,),
        in_specs=[hd, hd, hd, col, col, con, con],
        out_specs=pl.BlockSpec((3, rows, 128), lambda i: (0, 0, i)),
        out_shape=jax.ShapeDtypeStruct((3, rows, width), BF16),
        scratch_shapes=[pltpu.VMEM((128, rows), F32), pltpu.VMEM((128, rows), F32), pltpu.VMEM((2, rows, 128), F32)],
        compiler_params=pltpu.CompilerParams(vmem_limit_bytes=VLIM),
        cost_estimate=pl.CostEstimate(flops=40 * heads * rows * rows * HEAD_DIM, bytes_accessed=20 * 1024 * 1024, transcendentals=0),
        name="attention_backward",
    )(q, k, v, ch, attended, cosine, sine)


def qkv_back_kernel(layer, sec_ref, cj_ref, x_ref, cm_ref, gain_ref, own_ref, other_ref,
                    ci_ref, small_ref, w_ref, acc, sem):
    step = pl.program_id(0)
    fetch_weights(layer, sec_ref, [(own_ref, other_ref, w_ref)], sem)

    @pl.when(step == 0)
    def _():
        acc[...] = jnp.zeros_like(acc)

    width = x_ref.shape[-1]
    slope = nt(cj_ref[0], w_ref[:, 0:width])
    for which in range(1, 3):
        slope = slope + nt(cj_ref[which], w_ref[:, which * width:(which + 1) * width])
    unit, scale = normalize(x_ref[...].astype(F32))
    acc[0] += fold(slope * unit)
    for which in range(3):
        acc[which + 1] += fold(cj_ref[which].astype(F32))
    ci_ref[...] = (cm_ref[...] + norm_back(slope * gain_ref[...], unit, scale)).astype(BF16)

    @pl.when(step == pl.num_programs(0) - 1)
    def _():
        for index in range(4):
            small_ref[index:index + 1, :] = jnp.sum(acc[index], axis=0, keepdims=True)


def qkv_back(layer, sec, cj, x, cm, gain, own, other, tb=256):
    rows, width = x.shape
    const = lambda n, m=1: pl.BlockSpec((m, n), lambda i: (0, 0))
    tok = lambda n: pl.BlockSpec((tb, n), lambda i: (i, 0))
    S = jax.ShapeDtypeStruct
    return pl.pallas_call(
        functools.partial(qkv_back_kernel, layer),
        grid=(rows // tb,),
        in_specs=[SMEM, pl.BlockSpec((3, tb, width), lambda i: (0, i, 0)), tok(width), tok(width), const(width), ANY, ANY],
        out_specs=[tok(width), const(width, 4)],
        out_shape=[S((rows, width), BF16), S((4, width), F32)],
        scratch_shapes=[pltpu.VMEM(own.shape, BF16), pltpu.VMEM((4, 8, width), F32), pltpu.SemaphoreType.DMA((1,))],
        compiler_params=pltpu.CompilerParams(vmem_limit_bytes=VLIM),
        cost_estimate=pl.CostEstimate(flops=2 * rows * width * 3 * width, bytes_accessed=16 * 1024 * 1024, transcendentals=0),
        name="joint_backward",
    )(sec, cj, x, cm, gain, own, other)


def tables(labels, places):
    half = HEAD_DIM // 2
    lane = jnp.arange(128)
    rate = 1.0 / 10000.0 ** (jnp.arange(half, dtype=F32) * 2.0 / HEAD_DIM)
    angle = places.astype(F32)[:, None] * jnp.tile(rate, 4)[None, :]
    sign = jnp.where(lane % HEAD_DIM < half, -1.0, 1.0).astype(F32)
    return jnp.cos(angle), jnp.sin(angle) * sign


SIZES = ("joint_bias", "output_bias", "up_bias", "down_bias", "first_gain", "inner_gain", "second_gain", "hidden_gain")


def feed_grads_kernel(sec_ref, order_ref, cb_ref, hid_ref, c_ref, n2_ref, cm_ref, in_ref, small_ref,
                      keep_ref, send_ref, c_t, cm_t):
    step = pl.program_id(0)
    sec = sec_ref[0]
    parts = order_ref.shape[0] // 2
    half = n2_ref.shape[-1] // 2
    up_rows = cb_ref.shape[-1] // 2
    thin = c_ref.shape[-1] // parts
    steps = pl.num_programs(0) // 2
    outs = (keep_ref, send_ref)

    @pl.when(step == 0)
    def _():
        c_t[...] = c_ref[...].T
        cm_t[...] = cm_ref[...].T
        for side in range(2):
            which = sec if side == 0 else 1 - sec
            for part in range(parts):
                at = order_ref[side * parts + part]
                row = small_ref[pl.ds(which * parts + part, 1), 0, :]
                outs[side][at, up_rows * 2 + thin:, :] = jnp.broadcast_to(row, (16, half)).astype(BF16)

    both = tn(cb_ref[...], n2_ref[...])
    left, right = both[:, :half], both[:, half:]
    flip = jnp.full((1, 1), sec) == 0
    sides = (jnp.where(flip, left, right).astype(BF16), jnp.where(flip, right, left).astype(BF16))
    for side in range(2):
        for sub in range(2):
            at = order_ref[side * parts + step * 2 + sub]
            outs[side][at, 0:up_rows, :] = sides[side][sub * up_rows:(sub + 1) * up_rows]

    down = nn(c_t[...], hid_ref[...]).astype(BF16)
    for side in range(2):
        @pl.when(step // steps == side)
        def _():
            rows = pl.ds(pl.multiple_of(up_rows + thin * (step % steps), 16), thin)
            for part in range(parts):
                outs[side][order_ref[side * parts + part], rows, :] = down[thin * part:thin * (part + 1)]

        @pl.when(step == side * steps)
        def _():
            which = sec if side == 0 else 1 - sec
            out = nn(cm_t[...], in_ref[:, pl.ds(pl.multiple_of(which * half, 128), half)]).astype(BF16)
            for part in range(parts):
                outs[side][order_ref[side * parts + part], 2 * up_rows:2 * up_rows + thin, :] = out[thin * part:thin * (part + 1)]


def feed_grads(sec, order, cb, hidden, c, n2, cm, inner, small):
    rows, width = c.shape
    wide = cb.shape[-1]
    parts = order.shape[0] // 2
    half = width // 2
    steps = wide // half
    up_rows = wide // parts
    total = 2 * up_rows + width // parts + 16
    full = lambda n: pl.BlockSpec((rows, n), lambda i, s, o: (0, 0))
    out_spec = pl.BlockSpec((parts, total, half), lambda i, s, o: (0, 0, 0))
    out_shape = jax.ShapeDtypeStruct((parts, total, half), BF16)
    return pl.pallas_call(
        feed_grads_kernel,
        grid_spec=pltpu.PrefetchScalarGridSpec(
            num_scalar_prefetch=2,
            grid=(steps,),
            in_specs=[
                pl.BlockSpec((rows, half), lambda i, s, o: (0, i)),
                pl.BlockSpec((rows, half), lambda i, s, o: (0, jnp.where(i < steps // 2, s[0], 1 - s[0]) * (steps // 2) + i % (steps // 2))),
                full(width), full(width), full(width), full(width),
                pl.BlockSpec((2 * parts, 1, half), lambda i, s, o: (0, 0, 0)),
            ],
            out_specs=[out_spec, out_spec],
            scratch_shapes=[pltpu.VMEM((width, rows), BF16), pltpu.VMEM((width, rows), BF16)],
        ),
        out_shape=[out_shape, out_shape],
        compiler_params=pltpu.CompilerParams(vmem_limit_bytes=VLIM),
        cost_estimate=pl.CostEstimate(flops=2 * rows * width * (2 * wide + width), bytes_accessed=30 * 1024 * 1024, transcendentals=0),
        name="feed_gradients",
    )(sec, order, cb, hidden, c, n2, cm, inner, small)


def joint_grads_kernel(sec_ref, order_ref, cj_ref, n_ref, small_ref, keep_ref, send_ref, acc):
    step = pl.program_id(0)
    sec = sec_ref[0]
    parts = order_ref.shape[0] // 2
    width = n_ref.shape[-1]
    half = width // 2
    thick = acc.shape[0] // parts
    outs = (keep_ref, send_ref)
    acc[pl.ds(pl.multiple_of(step * width, 16), width), :] = tn(cj_ref[0], n_ref[...]).astype(BF16)

    @pl.when(step == pl.num_programs(0) - 1)
    def _():
        for side in range(2):
            which = sec if side == 0 else 1 - sec
            columns = pl.ds(pl.multiple_of(which * half, 128), half)
            for part in range(parts):
                at = order_ref[side * parts + part]
                outs[side][at, 0:thick, :] = acc[thick * part:thick * (part + 1), columns]
                row = small_ref[pl.ds(which * parts + part, 1), 0, :]
                outs[side][at, thick:, :] = jnp.broadcast_to(row, (16, half)).astype(BF16)


def joint_grads(sec, order, cj, normed, small):
    rows, width = normed.shape
    parts = order.shape[0] // 2
    half = width // 2
    thick = 3 * width // parts
    out_spec = pl.BlockSpec((parts, thick + 16, half), lambda i, s, o: (0, 0, 0))
    out_shape = jax.ShapeDtypeStruct((parts, thick + 16, half), BF16)
    return pl.pallas_call(
        joint_grads_kernel,
        grid_spec=pltpu.PrefetchScalarGridSpec(
            num_scalar_prefetch=2,
            grid=(3,),
            in_specs=[
                pl.BlockSpec((1, rows, width), lambda i, s, o: (i, 0, 0)),
                pl.BlockSpec((rows, width), lambda i, s, o: (0, 0)),
                pl.BlockSpec((2 * parts, 1, half), lambda i, s, o: (0, 0, 0)),
            ],
            out_specs=[out_spec, out_spec],
            scratch_shapes=[pltpu.VMEM((3 * width, width), BF16)],
        ),
        out_shape=[out_shape, out_shape],
        compiler_params=pltpu.CompilerParams(vmem_limit_bytes=VLIM),
        cost_estimate=pl.CostEstimate(flops=6 * rows * width * width, bytes_accessed=14 * 1024 * 1024, transcendentals=0),
        name="joint_gradients",
    )(sec, order, cj, normed, small)


def small_rows(items, parts, half):
    lined = jnp.concatenate([item.reshape(parts, -1) for item in items], axis=1)
    lined = lined.reshape(parts, 2, -1).transpose(1, 0, 2)
    lined = jnp.pad(lined, ((0, 0), (0, 0), (0, half - lined.shape[-1])))
    return lined.reshape(2 * parts, 1, half)


def swap_pairs(change, sizes):
    sections, dps, seqs = sizes
    pairs = []
    for section in range(sections):
        for dp in range(dps):
            for seq in range(seqs):
                a, b, c = change(section, dp, seq)
                pairs.append(((section * dps + dp) * seqs + seq, (a * dps + b) * seqs + c))
    return pairs


def reduce_chunks(kept, sent, sizes):
    every = ("section", "dp", "seq")
    moves = (
        lambda s, d, q: (s, d ^ 1, q) if s == 0 else (s, d, q ^ 1),
        lambda s, d, q: (s, d, q ^ 1) if s == 0 else (s, d ^ 1, q),
        lambda s, d, q: (s, d ^ 2, q),
        lambda s, d, q: (s, d ^ 4, q),
    )
    arrived = lax.ppermute(sent, "section", [(0, 1), (1, 0)])
    for move in moves:
        middle = kept.shape[0] // 2
        sent = (kept[middle:].astype(F32) + arrived[middle:].astype(F32)).astype(BF16)
        held = kept[:middle].astype(F32) + arrived[:middle].astype(F32)
        arrived = lax.ppermute(sent, every, swap_pairs(move, sizes))
        kept = held if middle == 1 else held.astype(BF16)
    return kept[0] + arrived[0].astype(F32)


def row_step(
    sizes,
    tokens,
    segments,
    cotangent,
    joint_weight,
    joint_bias,
    output_weight,
    output_bias,
    up_weight,
    up_bias,
    down_weight,
    down_bias,
    first_gain,
    inner_gain,
    second_gain,
    hidden_gain,
):
    micro, row_count, piece, width = tokens.shape
    rows = 2 * piece
    wide = up_weight.shape[-1]
    parts = sizes[1] * sizes[2]
    half = width // 2
    section = lax.axis_index("section")
    part = lax.axis_index("seq")
    data = lax.axis_index("dp")
    sec = section.reshape(1).astype(jnp.int32)
    mine = 2 * section + part
    swap = [(0, 1), (1, 0)]

    def pick(array, index):
        return lax.dynamic_index_in_dim(array, index, 0, keepdims=False)

    flat = tokens.reshape(micro * row_count, piece, width)
    beside = lax.ppermute(pick(flat, mine ^ 1), "seq", swap)
    state = jnp.concatenate([pick(flat, mine), beside], axis=0)
    both = [(own[0], lax.ppermute(own[0], "section", swap)) for own in (joint_weight, output_weight, up_weight, down_weight)]
    joint_pair, output_pair, up_pair, down_pair = both
    own = jnp.concatenate([joint_bias, output_bias, up_bias, down_bias, first_gain, inner_gain, second_gain, hidden_gain], axis=1)
    other = lax.ppermute(own, "section", swap)
    packs = (jnp.where(section == 0, own, other), jnp.where(section == 0, other, own))
    flat = cotangent.reshape(micro * row_count, piece, width)
    beside = lax.ppermute(pick(flat, mine ^ 1), "seq", swap)
    slope = jnp.concatenate([pick(flat, mine), beside], axis=0)

    whole = pick(segments.reshape(micro * row_count, rows), mine)
    starts = jnp.sum((whole[None, :] < whole[:, None]).astype(jnp.int32), axis=1)
    places = jnp.arange(rows, dtype=jnp.int32) - starts
    turn = lambda a: jnp.where(part == 0, a, jnp.roll(a, piece))
    cosine, sine = tables(None, turn(places))
    labels = turn(whole).reshape(rows, 1)

    mx, my, mz = data % 2, part, data // 2
    index = jnp.arange(parts, dtype=jnp.int32)
    cx, cy, cz = (index // 2) % 2 ^ mx, index % 2 ^ my, index // 4 ^ mz
    depth = cz % 2 * 2 + cz // 2
    order_x, order_y = (cx * 2 + cy) * 4 + depth, (cy * 2 + cx) * 4 + depth
    order = jnp.where(section == 0, jnp.concatenate([order_x, order_y]), jnp.concatenate([order_y, order_x]))

    lengths = (3 * width, width, wide, width, width, width, width, wide)

    def cut(pack, which):
        begin = sum(lengths[:which])
        return pack[:, begin:begin + lengths[which]]

    kept = []
    hiddens = []
    for layer in range(2):
        pack = packs[layer]
        jb, ob, ub, db, fg, ig, sg, hg = (cut(pack, which) for which in range(8))
        normed, q, k, v = qkv(layer, sec, state, fg, *joint_pair, jb, cosine, sine, labels)
        attended, query = attend(q, k, v)
        result, mixed, hidden, bend, stats = feed(layer, sec, attended, state, ig, ob, sg, ub, hg, db, output_pair, up_pair, down_pair)
        kept.append((state, normed, query, k, v, attended, mixed, hidden, bend, stats))
        hiddens.append(result)
        state = result

    done = [None, None]
    grads = [None, None]
    for layer in (1, 0):
        pack = packs[layer]
        jb, ob, ub, db, fg, ig, sg, hg = (cut(pack, which) for which in range(8))
        state, normed, query, k, v, attended, mixed, hidden, bend, stats = kept[layer]
        cb, cm, cm_low, ch, n2, inner, wide_sums, thin_sums = feed_back(
            layer, sec, slope, hidden, bend, stats, mixed, attended, ig, sg, hg, output_pair, up_pair, down_pair)
        small = small_rows((thin_sums[2], wide_sums[1], thin_sums[0], thin_sums[3], thin_sums[1], wide_sums[0]), parts, half)
        feed_part = reduce_chunks(*feed_grads(sec, order, cb, hidden, slope, n2, cm_low, inner, small), sizes)
        cj = attend_back(query, k, v, ch, attended, cosine, sine)
        back, sums = qkv_back(layer, sec, cj, state, cm, fg, *joint_pair)
        small = small_rows((sums[1:].reshape(-1), sums[0]), parts, half)
        joint_part = reduce_chunks(*joint_grads(sec, order, cj, normed, small), sizes)
        grads[layer] = jnp.concatenate([feed_part, joint_part], axis=0)
        done[layer] = back
        slope = back

    def spread(pieces):
        every = ("section", "seq")
        got = [None] * 4
        for fs in range(2):
            for fq in range(2):
                owed = [item[piece * fq:piece * (fq + 1)] for item in pieces]
                if fs == 0:
                    block = jnp.where(section == 0, owed[0], owed[1])
                else:
                    block = jnp.where(section == 0, owed[1], owed[0])
                if fs or fq:
                    pairs = [(2 * s + q, 2 * (s ^ fs) + (q ^ fq)) for s in range(2) for q in range(2)]
                    block = lax.ppermute(block, every, pairs)
                got[2 * fs + fq] = block
        stacked = jnp.stack(got)
        return jnp.stack([pick(stacked, mine ^ index) for index in range(4)]).reshape(1, micro, row_count, piece, width)

    hiddens = spread(hiddens)
    input_gradients = spread(done).astype(F32)

    ours = jnp.where(section == 0, grads[0], grads[1])
    theirs = lax.ppermute(jnp.where(section == 0, grads[1], grads[0]), "section", swap)
    left = jnp.where(section == 0, ours, theirs)
    right = jnp.where(section == 0, theirs, ours)
    up_rows, thin, thick = wide // parts, width // parts, 3 * width // parts

    def rows_of(begin, count):
        return jnp.concatenate([left[begin:begin + count], right[begin:begin + count]], axis=1)

    up_grad = rows_of(0, up_rows).T
    at = up_rows
    steps = up_rows // thin
    sides = [item[at:at + up_rows].reshape(steps, thin, half).transpose(0, 2, 1).reshape(steps * half, thin) for item in (left, right)]
    down_grad = jnp.concatenate(sides, axis=0)
    at += up_rows
    output_grad = rows_of(at, thin).T
    at += thin
    sizes_small = (thin, up_rows, thin, thin, thin, up_rows)
    used = sum(sizes_small) // 2
    line = jnp.concatenate([left[at, :used], right[at, :used]])
    at += 16
    ends = [sum(sizes_small[:i + 1]) for i in range(len(sizes_small))]
    ob, ub, db, ig, sg, hg = (line[end - size:end] for end, size in zip(ends, sizes_small))
    joint_grad = rows_of(at, thick).T
    at += thick
    used = (thick + thin) // 2
    line = jnp.concatenate([left[at, :used], right[at, :used]])
    jb, fg = line[:thick], line[thick:]
    return (
        hiddens,
        input_gradients,
        joint_grad[None],
        jb[None],
        output_grad[None],
        ob[None],
        up_grad[None],
        ub[None],
        down_grad[None],
        db[None],
        fg[None],
        ig[None],
        sg[None],
        hg[None],
    )


def choose(sizes, *arrays):
    micro, row_count, piece, width = arrays[0].shape
    if sizes == (2, 8, 2) and micro * row_count == 4:
        return row_step(sizes, *arrays)
    return shards(*arrays)


def solution(mesh):
    axes = ("section", "dp", "seq")
    return jax.shard_map(
        functools.partial(choose, tuple(mesh.shape[name] for name in axes)),
        mesh=mesh,
        in_specs=(
            P(None, "dp", "seq", None),
            P(None, "dp", None),
            P(None, "dp", "seq", None),
            P("section", None, None),
            P("section", None),
            P("section", None, None),
            P("section", None),
            P("section", None, None),
            P("section", None),
            P("section", None, None),
            P("section", None),
            P("section", None),
            P("section", None),
            P("section", None),
            P("section", None),
        ),
        out_specs=(
            P("section", None, "dp", "seq", None),
            P("section", None, "dp", "seq", None),
            P("section", None, ("dp", "seq")),
            P("section", ("dp", "seq")),
            P("section", None, ("dp", "seq")),
            P("section", ("dp", "seq")),
            P("section", None, ("dp", "seq")),
            P("section", ("dp", "seq")),
            P("section", None, ("dp", "seq")),
            P("section", ("dp", "seq")),
            P("section", ("dp", "seq")),
            P("section", ("dp", "seq")),
            P("section", ("dp", "seq")),
            P("section", ("dp", "seq")),
        ),
        check_vma=False,
    )
```

```python
import functools
import math

import jax
import jax.numpy as jnp
from jax import lax
from jax.experimental import pallas as pl
from jax.experimental.pallas import tpu as pltpu
from jax.sharding import PartitionSpec as P

HEAD_DIM = 64


EPSILON = 1e-05
MASKED = -1e30


def passed_along(value, axis, by):
    devices = lax.axis_size(axis)
    pairs = [(i, i + by) for i in range(devices) if 0 <= i + by < devices]
    return lax.ppermute(value, axis, pairs)


def layer_norm(value, gain):
    centered = value - jnp.mean(value, axis=-1, keepdims=True)
    spread = jnp.mean(centered * centered, axis=-1, keepdims=True)
    return centered * lax.rsqrt(spread + EPSILON) * gain


def feed_norm(before, gain):
    return layer_norm(jax.nn.gelu(before, approximate=False), gain)


def rotate(value, cosine, sine):
    middle = value.shape[-1] // 2
    first, second = (value[..., :middle], value[..., middle:])
    return jnp.concatenate(
        [first * cosine - second * sine, second * cosine + first * sine], axis=-1
    )


def rotate_back(incoming, cosine, sine):
    middle = incoming.shape[-1] // 2
    first, second = (incoming[..., :middle], incoming[..., middle:])
    return jnp.concatenate(
        [first * cosine + second * sine, second * cosine - first * sine], axis=-1
    )


def layer_forward(state, labels, weights, part):
    (
        joint_weight,
        joint_bias,
        output_weight,
        output_bias,
        up_weight,
        up_bias,
        down_weight,
        down_bias,
        first_gain,
        inner_gain,
        second_gain,
        hidden_gain,
    ) = weights
    row_count, piece_len, model_width = state.shape
    head_count = model_width // HEAD_DIM
    shape_heads = (row_count, piece_len, head_count, HEAD_DIM)
    offset = part * piece_len
    local_labels = lax.dynamic_slice_in_dim(labels, offset, piece_len, 1)
    starts = jnp.sum((labels[:, None, :] < local_labels[:, :, None]).astype(jnp.int32), axis=-1)
    places = offset + jnp.arange(piece_len, dtype=jnp.int32)[None, :] - starts
    inverse_rate = 1.0 / 10000.0 ** (jnp.arange(HEAD_DIM // 2, dtype=jnp.float32) * 2.0 / HEAD_DIM)
    angle = places.astype(jnp.float32)[:, :, None, None] * inverse_rate
    cosine = jnp.cos(angle)
    sine = jnp.sin(angle)
    normed = layer_norm(state, first_gain).astype(jnp.bfloat16)
    joint = jnp.dot(normed, joint_weight, preferred_element_type=jnp.float32) + joint_bias
    query = rotate(joint[..., :model_width].reshape(shape_heads), cosine, sine).astype(jnp.bfloat16)
    key = rotate(
        joint[..., model_width : 2 * model_width].reshape(shape_heads), cosine, sine
    ).astype(jnp.bfloat16)
    value = joint[..., 2 * model_width :].reshape(shape_heads).astype(jnp.bfloat16)
    keys_all, values_all = (
        lax.all_gather(key, "seq", axis=1, tiled=True),
        lax.all_gather(value, "seq", axis=1, tiled=True),
    )
    match = local_labels[:, None, :, None] == labels[:, None, None, :]
    scores = jnp.einsum(
        "rqhd,rkhd->rhqk", query, keys_all, preferred_element_type=jnp.float32
    ) * HEAD_DIM ** (-0.5)
    scores = jnp.where(match, scores, MASKED)
    peak = jnp.max(scores, axis=-1, keepdims=True)
    raised = jnp.exp(scores - peak)
    total_raised = jnp.sum(raised, axis=-1, keepdims=True)
    shares = raised / total_raised
    log_total = peak + jnp.log(total_raised)
    attended = jnp.einsum(
        "rhqk,rkhd->rqhd",
        shares.astype(jnp.bfloat16),
        values_all,
        preferred_element_type=jnp.float32,
    ).reshape(row_count, piece_len, model_width)
    inner = layer_norm(attended, inner_gain).astype(jnp.bfloat16)
    mixed = state + jnp.dot(inner, output_weight, preferred_element_type=jnp.float32) + output_bias
    normed_two = layer_norm(mixed, second_gain).astype(jnp.bfloat16)
    before = jnp.dot(normed_two, up_weight, preferred_element_type=jnp.float32) + up_bias
    hidden = feed_norm(before, hidden_gain).astype(jnp.bfloat16)
    result = mixed + jnp.dot(hidden, down_weight, preferred_element_type=jnp.float32) + down_bias
    kept = (
        state,
        normed,
        query,
        keys_all,
        values_all,
        cosine,
        sine,
        match,
        shares,
        attended,
        inner,
        mixed,
        normed_two,
        before,
        hidden,
        log_total,
        labels,
    )
    return (result, kept)


def feed_backward(kept, slope_out, weights, totals):
    (
        state,
        normed,
        query,
        keys_all,
        values_all,
        cosine,
        sine,
        match,
        shares,
        attended,
        inner,
        mixed,
        normed_two,
        before,
        hidden,
        log_total,
        labels,
    ) = kept
    (
        joint_weight,
        joint_bias,
        output_weight,
        output_bias,
        up_weight,
        up_bias,
        down_weight,
        down_bias,
        first_gain,
        inner_gain,
        second_gain,
        hidden_gain,
    ) = weights
    slope_low = slope_out.astype(jnp.bfloat16)
    totals[6] = totals[6] + jnp.einsum(
        "rcf,rcd->fd", hidden, slope_low, preferred_element_type=jnp.float32
    )
    totals[7] = totals[7] + jnp.sum(slope_low.astype(jnp.float32), axis=(0, 1))
    slope_hidden = jnp.einsum(
        "rcd,fd->rcf", slope_low, down_weight, preferred_element_type=jnp.float32
    )
    unused, puller = jax.vjp(feed_norm, before, hidden_gain)
    slope_before, slope_gain = puller(slope_hidden)
    totals[11] = totals[11] + slope_gain
    before_low = slope_before.astype(jnp.bfloat16)
    totals[4] = totals[4] + jnp.einsum(
        "rcd,rcf->df", normed_two, before_low, preferred_element_type=jnp.float32
    )
    totals[5] = totals[5] + jnp.sum(before_low.astype(jnp.float32), axis=(0, 1))
    slope_normed = jnp.einsum(
        "rcf,df->rcd", before_low, up_weight, preferred_element_type=jnp.float32
    )
    unused, puller = jax.vjp(layer_norm, mixed, second_gain)
    slope_mixed, slope_gain = puller(slope_normed)
    totals[10] = totals[10] + slope_gain
    return (slope_out + slope_mixed, totals)


def attend_backward(kept, slope_mixed, weights, totals):
    (
        state,
        normed,
        query,
        keys_all,
        values_all,
        cosine,
        sine,
        match,
        shares,
        attended,
        inner,
        mixed,
        normed_two,
        before,
        hidden,
        log_total,
        labels,
    ) = kept
    (
        joint_weight,
        joint_bias,
        output_weight,
        output_bias,
        up_weight,
        up_bias,
        down_weight,
        down_bias,
        first_gain,
        inner_gain,
        second_gain,
        hidden_gain,
    ) = weights
    row_count, piece_len, model_width = state.shape
    head_count = model_width // HEAD_DIM
    scale = HEAD_DIM ** (-0.5)
    slope_low = slope_mixed.astype(jnp.bfloat16)
    totals[2] = totals[2] + jnp.einsum(
        "rcd,rce->de", inner, slope_low, preferred_element_type=jnp.float32
    )
    totals[3] = totals[3] + jnp.sum(slope_low.astype(jnp.float32), axis=(0, 1))
    slope_inner = jnp.einsum(
        "rce,de->rcd", slope_low, output_weight, preferred_element_type=jnp.float32
    )
    unused, puller = jax.vjp(layer_norm, attended, inner_gain)
    slope_attended, slope_gain = puller(slope_inner)
    totals[9] = totals[9] + slope_gain
    slope_heads = slope_attended.astype(jnp.bfloat16).reshape(
        row_count, piece_len, head_count, HEAD_DIM
    )
    slope_shares = jnp.einsum(
        "rqhd,rkhd->rhqk", slope_heads, values_all, preferred_element_type=jnp.float32
    )
    weighted = jnp.sum(shares * slope_shares, axis=-1, keepdims=True)
    slope_scores = (shares * (slope_shares - weighted)).astype(jnp.bfloat16)
    slope_query = (
        jnp.einsum("rhqk,rkhd->rqhd", slope_scores, keys_all, preferred_element_type=jnp.float32)
        * scale
    )
    shares_low = shares.astype(jnp.bfloat16)
    key_part = (
        jnp.einsum("rhqk,rqhd->krhd", slope_scores, query, preferred_element_type=jnp.float32)
        * scale
    )
    value_part = jnp.einsum(
        "rhqk,rqhd->krhd", shares_low, slope_heads, preferred_element_type=jnp.float32
    )
    summed = lax.psum_scatter(
        jnp.concatenate([key_part, value_part], axis=-1).astype(jnp.bfloat16),
        "seq",
        scatter_dimension=0,
        tiled=True,
    ).astype(jnp.float32)
    summed = jnp.transpose(summed, (1, 0, 2, 3))
    key_raw = summed[..., :HEAD_DIM]
    slope_value = summed[..., HEAD_DIM:]
    slope_key = rotate_back(key_raw, cosine, sine)
    slope_query = rotate_back(slope_query, cosine, sine)
    flat = (row_count, piece_len, model_width)
    slope_joint = jnp.concatenate(
        [slope_query.reshape(flat), slope_key.reshape(flat), slope_value.reshape(flat)], axis=-1
    ).astype(jnp.bfloat16)
    totals[0] = totals[0] + jnp.einsum(
        "rcd,rce->de", normed, slope_joint, preferred_element_type=jnp.float32
    )
    totals[1] = totals[1] + jnp.sum(slope_joint.astype(jnp.float32), axis=(0, 1))
    slope_normed = jnp.einsum(
        "rce,de->rcd", slope_joint, joint_weight, preferred_element_type=jnp.float32
    )
    unused, puller = jax.vjp(layer_norm, state, first_gain)
    slope_state, slope_gain = puller(slope_normed)
    totals[8] = totals[8] + slope_gain
    return (slope_mixed + slope_state, totals)


def lift(vector):
    return vector.reshape(1, vector.shape[0])


def shards(
    tokens,
    segments,
    cotangent,
    joint_weight,
    joint_bias,
    output_weight,
    output_bias,
    up_weight,
    up_bias,
    down_weight,
    down_bias,
    first_gain,
    inner_gain,
    second_gain,
    hidden_gain,
):
    weights = tuple(
        (
            item[0]
            for item in (
                joint_weight,
                joint_bias,
                output_weight,
                output_bias,
                up_weight,
                up_bias,
                down_weight,
                down_bias,
                first_gain,
                inner_gain,
                second_gain,
                hidden_gain,
            )
        )
    )
    micro, row_count, piece_len, model_width = tokens.shape
    leading = lax.axis_index("section") == 0
    part = lax.axis_index("seq")
    received = jnp.zeros((row_count, piece_len, model_width), jnp.bfloat16)
    saved = []
    results = []
    for moment in range(micro + 1):
        labels = jnp.where(leading, segments[min(moment, micro - 1)], segments[max(moment - 1, 0)])
        source = jnp.where(leading, tokens[min(moment, micro - 1)], received)
        state = source.astype(jnp.float32)
        result, kept = layer_forward(state, labels, weights, part)
        sent = result.astype(jnp.bfloat16)
        results.append(sent)
        saved.append((state, labels))
        if moment < micro:
            received = passed_along(sent, "section", 1)
    totals = [jnp.zeros(item.shape, jnp.float32) for item in weights]
    back_received = jnp.zeros((row_count, piece_len, model_width), jnp.bfloat16)
    back_results = []
    for moment in range(micro + 1):
        earlier = max(moment - 1, 0)
        later = min(moment + 1, micro)
        state = jnp.where(leading, saved[earlier][0], saved[later][0])
        labels = jnp.where(leading, saved[earlier][1], saved[later][1])
        kept = layer_forward(state, labels, weights, part)[1]
        if moment < micro:
            outer = cotangent[moment].astype(jnp.float32)
        else:
            outer = jnp.zeros((row_count, piece_len, model_width), jnp.float32)
        slope_out = jnp.where(leading, back_received.astype(jnp.float32), outer)
        slope_mixed, totals = feed_backward(kept, slope_out, weights, totals)
        slope_input, totals = attend_backward(kept, slope_mixed, weights, totals)
        back_results.append(slope_input)
        if moment < micro:
            back_received = passed_along(slope_input.astype(jnp.bfloat16), "section", -1)
    reduced = (
        lax.psum_scatter(totals[0], ("dp", "seq"), scatter_dimension=1, tiled=True),
        lax.psum_scatter(lift(totals[1]), ("dp", "seq"), scatter_dimension=1, tiled=True),
        lax.psum_scatter(totals[2], ("dp", "seq"), scatter_dimension=1, tiled=True),
        lax.psum_scatter(lift(totals[3]), ("dp", "seq"), scatter_dimension=1, tiled=True),
        lax.psum_scatter(totals[4], ("dp", "seq"), scatter_dimension=1, tiled=True),
        lax.psum_scatter(lift(totals[5]), ("dp", "seq"), scatter_dimension=1, tiled=True),
        lax.psum_scatter(totals[6], ("dp", "seq"), scatter_dimension=1, tiled=True),
        lax.psum_scatter(lift(totals[7]), ("dp", "seq"), scatter_dimension=1, tiled=True),
        lax.psum_scatter(lift(totals[8]), ("dp", "seq"), scatter_dimension=1, tiled=True),
        lax.psum_scatter(lift(totals[9]), ("dp", "seq"), scatter_dimension=1, tiled=True),
        lax.psum_scatter(lift(totals[10]), ("dp", "seq"), scatter_dimension=1, tiled=True),
        lax.psum_scatter(lift(totals[11]), ("dp", "seq"), scatter_dimension=1, tiled=True),
    )
    hiddens = jnp.stack(
        [jnp.where(leading, results[index], results[index + 1]) for index in range(micro)]
    )[None]
    input_gradients = jnp.stack(
        [jnp.where(leading, back_results[index + 1], back_results[index]) for index in range(micro)]
    )[None]
    return (
        hiddens,
        input_gradients,
        reduced[0][None],
        reduced[1],
        reduced[2][None],
        reduced[3],
        reduced[4][None],
        reduced[5],
        reduced[6][None],
        reduced[7],
        reduced[8],
        reduced[9],
        reduced[10],
        reduced[11],
    )


F32 = jnp.float32
BF16 = jnp.bfloat16
ANY = pl.BlockSpec(memory_space=pl.ANY)
SMEM = pl.BlockSpec(memory_space=pltpu.SMEM)
VLIM = 60 * 1024 * 1024


def lane_iota(shape):
    return lax.broadcasted_iota(jnp.int32, shape, len(shape) - 1)


def nn(a, b):
    return lax.dot_general(a, b, (((1,), (0,)), ((), ())), preferred_element_type=F32)


def nt(a, b):
    return lax.dot_general(a, b, (((1,), (1,)), ((), ())), preferred_element_type=F32)


def tn(a, b):
    return lax.dot_general(a, b, (((0,), (0,)), ((), ())), preferred_element_type=F32)


def normalize(value):
    centered = value - jnp.mean(value, axis=-1, keepdims=True)
    scale = lax.rsqrt(jnp.mean(centered * centered, axis=-1, keepdims=True) + EPSILON)
    return centered * scale, scale


def norm_back(slope, unit, scale):
    return scale * (
        slope
        - jnp.mean(slope, axis=-1, keepdims=True)
        - unit * jnp.mean(slope * unit, axis=-1, keepdims=True)
    )


def fold(value):
    rows, columns = value.shape
    return jnp.sum(value.reshape(rows // 8, 8, columns), axis=0)


def split3(value):
    high = value.astype(BF16)
    rest = value - high.astype(F32)
    middle = rest.astype(BF16)
    low = (rest - middle.astype(F32)).astype(BF16)
    return high, middle, low


JOINT_BIAS, OUTPUT_BIAS, UP_BIAS, DOWN_BIAS, FIRST_GAIN, INNER_GAIN, SECOND_GAIN, HIDDEN_GAIN = range(8)


def vectors_of(pack_ref, width, *numbers):
    wide = 4 * width
    lengths = (3 * width, width, wide, width, width, width, width, wide)
    views = []
    for number in numbers:
        views.append(pack_ref.at[0, :, pl.ds(sum(lengths[:number]), lengths[number])])
    return views


def pack_spec(layer, pack):
    return pl.BlockSpec((1, 1, pack.shape[-1]), lambda *_: (layer, 0, 0))


def fetch_weights(layer, sec_ref, pairs, sem):
    first = pl.program_id(0) == 0

    @pl.when(first & (sec_ref[0] == layer))
    def _():
        for index, (own, other, here) in enumerate(pairs):
            pltpu.make_async_copy(own, here, sem.at[index]).start()

    @pl.when(first & (sec_ref[0] != layer))
    def _():
        for index, (own, other, here) in enumerate(pairs):
            pltpu.make_async_copy(other, here, sem.at[index]).start()

    def arrive(index):
        @pl.when(first)
        def _():
            own, other, here = pairs[index]
            pltpu.make_async_copy(own, here, sem.at[index]).wait()

    return arrive


def gelu_parts(value):
    share = 0.5 + 0.5 * lax.erf(value * 0.5 ** 0.5)
    bell = jnp.exp2(value * value * (-0.5 * math.log2(math.e)))
    return value * share, share + value * bell * (1.0 / math.sqrt(2.0 * math.pi))


def qkv_kernel(layer, blocks, sec_ref, mine_ref, x_ref, y_ref, pack_ref, own_ref, other_ref, cos_ref, sin_ref,
               lab_ref, s_ref, n_ref, q_ref, k_ref, v_ref, w_ref, sem):
    arrive = fetch_weights(layer, sec_ref, [(own_ref, other_ref, w_ref)], sem)
    width = x_ref.shape[-1]
    gain_ref, bias_ref = vectors_of(pack_ref, width, FIRST_GAIN, JOINT_BIAS)
    state = jnp.where(jnp.full((1, 1), pl.program_id(0)) < blocks, x_ref[0], y_ref[...])
    s_ref[...] = state
    unit, scale = normalize(state.astype(F32))
    normed = (unit * gain_ref[...]).astype(BF16)
    n_ref[...] = normed
    cosine, sine = cos_ref[...], sin_ref[...]
    lane = lane_iota(cosine.shape)
    first = lane % HEAD_DIM < HEAD_DIM // 2
    head = lane < HEAD_DIM
    labels = lab_ref[...]
    document = lane - HEAD_DIM
    known = (document >= 0) & (document < 5)
    q_feat = jnp.where(known & (document != labels), MASKED, 0.0)
    ones = (document >= 5) & (document < 8)
    k_feat = jnp.where((known & (document == labels)) | ones, 1.0, 0.0)
    v_feat = jnp.where((document >= 0) & (document < 3), 1.0, 0.0)
    kinds = ((q_ref, q_feat), (k_ref, k_feat), (v_ref, v_feat))
    step = 256
    chunks = 3 * width // step

    def product(chunk):
        at = pl.ds(chunk * step, step)
        return nn(normed, w_ref[:, at]) + bias_ref[:, at]

    arrive(0)
    later = product(0)
    for chunk in range(chunks):
        joint = later
        if chunk + 1 < chunks:
            later = product(chunk + 1)
        for sub in range(step // 128):
            pair = chunk * step // 128 + sub
            which = pair * 128 // width
            out, feat = kinds[which]
            pair = pair - which * width // 128
            part = joint[:, sub * 128:(sub + 1) * 128]
            if which < 2:
                turned = jnp.where(first, pltpu.roll(part, 96, 1), pltpu.roll(part, 32, 1))
                part = part * cosine + turned * sine
            if which == 0:
                part = part * HEAD_DIM ** -0.5
            out[2 * pair] = jnp.where(head, part, feat).astype(BF16)
            out[2 * pair + 1] = jnp.where(head, pltpu.roll(part, 64, 1), feat).astype(BF16)


def qkv(layer, sec, x, pack, own, other, cosine, sine, labels, mine, tb=256):
    if isinstance(x, tuple):
        x, y = x
        blocks = x.shape[1] // tb
        rows, width = 2 * x.shape[1], x.shape[2]
    else:
        rows, width = x.shape
        blocks = rows // tb
        x, y = x[None], x
        mine = jnp.int32(0)
    heads = width // HEAD_DIM
    const = lambda shape: pl.BlockSpec(shape, lambda i, s, m: (0,) * len(shape))
    tok = lambda n: pl.BlockSpec((tb, n), lambda i, s, m: (i, 0))
    hd = pl.BlockSpec((heads, tb, 128), lambda i, s, m: (0, i, 0))
    return pl.pallas_call(
        functools.partial(qkv_kernel, layer, blocks),
        grid_spec=pltpu.PrefetchScalarGridSpec(
            num_scalar_prefetch=2,
            grid=(rows // tb,),
            in_specs=[pl.BlockSpec((1, tb, width), lambda i, s, m: (m[0], jnp.minimum(i, blocks - 1), 0)),
                      pl.BlockSpec((tb, width), lambda i, s, m: (jnp.maximum(i - blocks, 0), 0)),
                      pack_spec(layer, pack), ANY, ANY, tok(128), tok(128), tok(128)],
            out_specs=[tok(width), tok(width), hd, hd, hd],
            scratch_shapes=[pltpu.VMEM(own.shape, BF16), pltpu.SemaphoreType.DMA((1,))],
        ),
        out_shape=[jax.ShapeDtypeStruct((rows, width), BF16)] * 2 + [jax.ShapeDtypeStruct((heads, rows, 128), BF16)] * 3,
        compiler_params=pltpu.CompilerParams(vmem_limit_bytes=VLIM),
        cost_estimate=pl.CostEstimate(flops=2 * rows * width * 3 * width, bytes_accessed=16 * 1024 * 1024, transcendentals=0),
        name="joint_projection",
    )(sec, mine.reshape(1).astype(jnp.int32), x, y, pack, own, other, cosine, sine, labels)


def attend_kernel(qb, q_ref, k_ref, v_ref, o_ref, ql_ref):
    rows = q_ref.shape[1]
    lane = lane_iota((qb, 128))
    inside = (lane >= 69) & (lane < 72)
    work = [(head, block) for block in range(rows // qb) for head in range(2)]
    ready = {}

    def score(index):
        if index < len(work):
            head, block = work[index]
            ready[index] = nt(q_ref[head, pl.ds(block * qb, qb), :], k_ref[head])

    score(0)
    score(1)
    done = []
    for index, (head, block) in enumerate(work):
        score(index + 2)
        scores = ready.pop(index)
        at = pl.ds(block * qb, qb)
        peak = jnp.max(scores, axis=-1, keepdims=True)
        raised = jnp.exp(scores - peak).astype(BF16)
        sums = nn(raised, v_ref[head])
        total = sums[:, HEAD_DIM:HEAD_DIM + 1]
        done.append(sums * (1.0 / total))
        high, middle, low = split3(-(peak + jnp.log(total)))
        feat = jnp.where(lane == 69, high.astype(F32), jnp.where(lane == 70, middle.astype(F32), low.astype(F32)))
        ql_ref[head, at, :] = jnp.where(inside, feat, q_ref[head, at, :].astype(F32)).astype(BF16)
        if head == 1:
            o_ref[at, :] = jnp.where(lane < HEAD_DIM, done[0], pltpu.roll(done[1], 64, 1))
            done = []


def attend(q, k, v, qb=256):
    heads, rows, _ = q.shape
    hd = pl.BlockSpec((2, rows, 128), lambda i: (i, 0, 0))
    return pl.pallas_call(
        functools.partial(attend_kernel, qb),
        grid=(heads // 2,),
        in_specs=[hd, hd, hd],
        out_specs=[pl.BlockSpec((rows, 128), lambda i: (0, i)), hd],
        out_shape=[jax.ShapeDtypeStruct((rows, heads * HEAD_DIM), F32), jax.ShapeDtypeStruct(q.shape, BF16)],
        compiler_params=pltpu.CompilerParams(vmem_limit_bytes=VLIM),
        cost_estimate=pl.CostEstimate(flops=16 * heads * rows * rows * HEAD_DIM, bytes_accessed=16 * 1024 * 1024, transcendentals=0),
        name="attention_forward",
    )(q, k, v)


def feed_kernel(layer, sec_ref, at_ref, x_ref, pack_ref,
                wo0, wo1, wu0, wu1, wd0, wd1,
                out_ref, mixed_ref, hid_ref, gp_ref, st_ref, wo, wu, wd, bent, sem):
    arrive = fetch_weights(layer, sec_ref, [(wo0, wo1, wo), (wu0, wu1, wu), (wd0, wd1, wd)], sem)
    ig_ref, ob_ref, sg_ref, ub_ref, hg_ref, db_ref = vectors_of(
        pack_ref, x_ref.shape[-1], INNER_GAIN, OUTPUT_BIAS, SECOND_GAIN, UP_BIAS, HIDDEN_GAIN, DOWN_BIAS)
    wide = hg_ref.shape[-1]
    unit, _ = normalize(at_ref[...])
    inner = (unit * ig_ref[...]).astype(BF16)
    arrive(0)
    mixed = x_ref[...].astype(F32) + nn(inner, wo[...]) + ob_ref[...]
    mixed_ref[...] = mixed
    unit, _ = normalize(mixed)
    normed = (unit * sg_ref[...]).astype(BF16)
    step = 512
    chunks = wide // step

    def rise(chunk):
        at = pl.ds(chunk * step, step)
        return nn(normed, wu[:, at]) + ub_ref[:, at]

    arrive(1)
    later = rise(0)
    total = 0.0
    for chunk in range(chunks):
        before = later
        if chunk + 1 < chunks:
            later = rise(chunk + 1)
        at = pl.ds(chunk * step, step)
        value, bend = gelu_parts(before)
        gp_ref[:, at] = bend.astype(BF16)
        bent[:, at] = value
        total = total + jnp.sum(value, axis=-1, keepdims=True)
    mean = total * (1.0 / wide)
    spread = 0.0
    for chunk in range(chunks):
        centered = bent[:, pl.ds(chunk * step, step)] - mean
        spread = spread + jnp.sum(centered * centered, axis=-1, keepdims=True)
    scale = lax.rsqrt(spread * (1.0 / wide) + EPSILON)
    st_ref[...] = jnp.broadcast_to(scale, st_ref.shape)
    arrive(2)
    result = mixed + db_ref[...]
    for chunk in range(chunks):
        at = pl.ds(chunk * step, step)
        hidden = ((bent[:, at] - mean) * scale * hg_ref[:, at]).astype(BF16)
        hid_ref[:, at] = hidden
    result = result + nn(hid_ref[...], wd[...])
    out_ref[...] = result.astype(BF16)


def feed(layer, sec, attended, x, pack, wo, wu, wd, tb=512):
    rows, width = x.shape
    wide = wd[0].shape[0]
    tok = lambda n: pl.BlockSpec((tb, n), lambda i: (i, 0))
    S = jax.ShapeDtypeStruct
    return pl.pallas_call(
        functools.partial(feed_kernel, layer),
        grid=(rows // tb,),
        in_specs=[SMEM, tok(width), tok(width), pack_spec(layer, pack)] + [ANY] * 6,
        out_specs=[tok(width), tok(width), tok(wide), tok(wide), tok(128)],
        out_shape=[S((rows, width), BF16), S((rows, width), F32), S((rows, wide), BF16), S((rows, wide), BF16), S((rows, 128), F32)],
        scratch_shapes=[pltpu.VMEM(wo[0].shape, BF16), pltpu.VMEM(wu[0].shape, BF16), pltpu.VMEM(wd[0].shape, BF16), pltpu.VMEM((tb, wide), F32), pltpu.SemaphoreType.DMA((3,))],
        compiler_params=pltpu.CompilerParams(vmem_limit_bytes=VLIM),
        cost_estimate=pl.CostEstimate(flops=2 * rows * width * (2 * wide + width), bytes_accessed=40 * 1024 * 1024, transcendentals=0),
        name="feed_forward",
    )(sec, attended, x, pack, *wo, *wu, *wd)


def feed_back_kernel(layer, sec_ref, c_ref, hid_ref, gp_ref, st_ref, mixed_ref, at_ref,
                     pack_ref, wo0, wo1, wu0, wu1, wd0, wd1,
                     cb_ref, cm_ref, cl_ref, ch_ref, n2_ref, in_ref, wide_ref, thin_ref,
                     wo, wu, wd, sloped, wide_acc, thin_acc, sem):
    now = pl.program_id(0)
    ig_ref, sg_ref, hg_ref = vectors_of(pack_ref, c_ref.shape[-1], INNER_GAIN, SECOND_GAIN, HIDDEN_GAIN)

    @pl.when(now == 0)
    def _():
        wide_acc[...] = jnp.zeros_like(wide_acc)
        thin_acc[...] = jnp.zeros_like(thin_acc)

    arrive = fetch_weights(layer, sec_ref, [(wo0, wo1, wo), (wu0, wu1, wu), (wd0, wd1, wd)], sem)
    low = c_ref[...]
    outer = low.astype(F32)
    thin_acc[0] += fold(outer)
    wide = hg_ref.shape[-1]
    step = 512
    chunks = wide // step

    def fall(chunk):
        return nt(low, wd[pl.ds(chunk * step, step), :])

    arrive(2)
    later = fall(0)
    sum_moved = 0.0
    sum_slope = 0.0
    for chunk in range(chunks):
        slope = later
        if chunk + 1 < chunks:
            later = fall(chunk + 1)
        at = pl.ds(chunk * step, step)
        moved = slope * hid_ref[:, at].astype(F32)
        wide_acc[0, :, at] += fold(moved)
        sum_moved = sum_moved + jnp.sum(moved, axis=-1, keepdims=True)
        slope = slope * hg_ref[:, at]
        sum_slope = sum_slope + jnp.sum(slope, axis=-1, keepdims=True)
        sloped[:, at] = slope
    scale = st_ref[:, 0:1]
    mean_moved = sum_moved * (1.0 / wide)
    mean_slope = sum_slope * (1.0 / wide)
    arrive(1)
    slope_two = 0.0
    for chunk in range(chunks):
        at = pl.ds(chunk * step, step)
        unit = hid_ref[:, at].astype(F32) * (1.0 / hg_ref[:, at])
        slope = (sloped[:, at] - mean_slope - unit * mean_moved) * scale
        before_low = (slope * gp_ref[:, at].astype(F32)).astype(BF16)
        cb_ref[:, at] = before_low
        wide_acc[1, :, at] += fold(before_low.astype(F32))
        slope_two = slope_two + nt(before_low, wu[:, at])
    unit, scale = normalize(mixed_ref[...])
    n2_ref[...] = (unit * sg_ref[...]).astype(BF16)
    thin_acc[1] += fold(slope_two * unit)
    mixed = outer + norm_back(slope_two * sg_ref[...], unit, scale)
    cm_ref[...] = mixed
    mixed_low = mixed.astype(BF16)
    cl_ref[...] = mixed_low
    thin_acc[2] += fold(mixed_low.astype(F32))
    arrive(0)
    slope = nt(mixed_low, wo[...])
    unit, scale = normalize(at_ref[...])
    in_ref[...] = (unit * ig_ref[...]).astype(BF16)
    thin_acc[3] += fold(slope * unit)
    ch_ref[...] = norm_back(slope * ig_ref[...], unit, scale).astype(BF16)

    @pl.when(now == pl.num_programs(0) - 1)
    def _():
        inverse = 1.0 / hg_ref[...]
        wide_ref[0:1, :] = jnp.sum(wide_acc[0], axis=0, keepdims=True) * inverse
        wide_ref[1:2, :] = jnp.sum(wide_acc[1], axis=0, keepdims=True)
        for index in range(4):
            thin_ref[index:index + 1, :] = jnp.sum(thin_acc[index], axis=0, keepdims=True)


def feed_back(layer, sec, c, hidden, gp, st, mixed, attended, pack, wo, wu, wd, tb=256):
    rows, width = c.shape
    wide = wd[0].shape[0]
    const = lambda n, m=1: pl.BlockSpec((m, n), lambda i: (0, 0))
    tok = lambda n: pl.BlockSpec((tb, n), lambda i: (i, 0))
    S = jax.ShapeDtypeStruct
    return pl.pallas_call(
        functools.partial(feed_back_kernel, layer),
        grid=(rows // tb,),
        in_specs=[SMEM, tok(width), tok(wide), tok(wide), tok(128), tok(width), tok(width), pack_spec(layer, pack)] + [ANY] * 6,
        out_specs=[tok(wide), tok(width), tok(width), tok(width), tok(width), tok(width), const(wide, 2), const(width, 4)],
        out_shape=[S((rows, wide), BF16), S((rows, width), F32), S((rows, width), BF16), S((rows, width), BF16), S((rows, width), BF16), S((rows, width), BF16), S((2, wide), F32), S((4, width), F32)],
        scratch_shapes=[pltpu.VMEM(wo[0].shape, BF16), pltpu.VMEM(wu[0].shape, BF16), pltpu.VMEM(wd[0].shape, BF16),
                        pltpu.VMEM((tb, wide), F32), pltpu.VMEM((2, 8, wide), F32), pltpu.VMEM((4, 8, width), F32), pltpu.SemaphoreType.DMA((3,))],
        compiler_params=pltpu.CompilerParams(vmem_limit_bytes=VLIM),
        cost_estimate=pl.CostEstimate(flops=2 * rows * width * (2 * wide + width), bytes_accessed=50 * 1024 * 1024, transcendentals=0),
        name="feed_backward",
    )(sec, c, hidden, gp, st, mixed, attended, pack, *wo, *wu, *wd)


def attend_back_kernel(qb, q_ref, k_ref, v_ref, ch_ref, at_ref, cos_ref, sin_ref, cj_ref, kt, vt, qs, shares_ref, slope_ref):
    rows = q_ref.shape[1]
    lane = lane_iota((rows, 128))
    is_head = lane < HEAD_DIM
    slopes = ch_ref[...].astype(F32)
    product = slopes * at_ref[...]
    incoming = []
    for head in range(2):
        mine = is_head if head == 0 else jnp.logical_not(is_head)
        weighted = jnp.sum(jnp.where(mine, product, 0.0), axis=-1, keepdims=True)
        high, middle, low = split3(-weighted)
        feat = jnp.where(lane == 64, high.astype(F32), jnp.where(lane == 65, middle.astype(F32), jnp.where(lane == 66, low.astype(F32), 0.0)))
        local = slopes if head == 0 else pltpu.roll(slopes, 64, 1)
        incoming.append(jnp.where(is_head, local, feat).astype(BF16))
    blocks = rows // qb
    work = [(head, block) for head in range(2) for block in range(blocks)]
    ready = {}

    def score(index):
        if index < len(work):
            head, block = work[index]
            at = block * qb
            ready[index] = (
                nt(q_ref[head, pl.ds(at, qb), :], k_ref[head]),
                nt(incoming[head][at:at + qb], v_ref[head]),
            )

    score(0)
    for index, (head, block) in enumerate(work):
        score(index + 1)
        scores, turned = ready.pop(index)
        shares = jnp.exp(scores)
        slope = (shares * turned).astype(BF16)
        at = pl.ds(block * qb, qb)
        slope_ref[head, at, :] = slope
        shares_ref[head, at, :] = shares.astype(BF16)
        qs[head, at, :] = nn(slope, k_ref[head])
        if block == blocks - 1:
            rng = pl.ds(head * HEAD_DIM, HEAD_DIM)
            kt[rng, :] = nn(q_ref[head].T[:HEAD_DIM], slope_ref[head])
            vt[rng, :] = nn(incoming[head].T[:HEAD_DIM], shares_ref[head])
    cosine, sine = cos_ref[...], sin_ref[...]
    first = lane % HEAD_DIM < HEAD_DIM // 2

    def back(part):
        turned = jnp.where(first, pltpu.roll(part, 96, 1), pltpu.roll(part, 32, 1))
        return (part * cosine - turned * sine).astype(BF16)

    cj_ref[0] = back(jnp.where(is_head, qs[0], pltpu.roll(qs[1], 64, 1)) * HEAD_DIM ** -0.5)
    cj_ref[1] = back(kt[...].T)
    cj_ref[2] = vt[...].T.astype(BF16)


def attend_back(q, k, v, ch, attended, cosine, sine, begin=0, count=None, into=None, qb=256):
    heads, rows, _ = q.shape
    width = heads * HEAD_DIM
    count = heads // 2 - begin if count is None else count
    hd = pl.BlockSpec((2, rows, 128), lambda i: (i + begin, 0, 0))
    col = pl.BlockSpec((rows, 128), lambda i: (0, i + begin))
    con = pl.BlockSpec((rows, 128), lambda i: (0, 0))
    body = functools.partial(attend_back_kernel, qb)
    extra = () if into is None else (into,)

    def kernel(*refs):
        body(*refs[:7], *refs[7 + len(extra):])

    return pl.pallas_call(
        kernel,
        grid=(count,),
        in_specs=[hd, hd, hd, col, col, con, con] + [ANY] * len(extra),
        out_specs=pl.BlockSpec((3, rows, 128), lambda i: (0, 0, i + begin)),
        out_shape=jax.ShapeDtypeStruct((3, rows, width), BF16),
        input_output_aliases={7: 0} if extra else {},
        scratch_shapes=[pltpu.VMEM((128, rows), F32), pltpu.VMEM((128, rows), F32), pltpu.VMEM((2, rows, 128), F32),
                        pltpu.VMEM((2, rows, rows), BF16), pltpu.VMEM((2, rows, rows), BF16)],
        compiler_params=pltpu.CompilerParams(vmem_limit_bytes=VLIM),
        cost_estimate=pl.CostEstimate(flops=80 * count * rows * rows * HEAD_DIM, bytes_accessed=3 * count * 1024 * 1024, transcendentals=0),
        name="attention_backward",
    )(q, k, v, ch, attended, cosine, sine, *extra)


def qkv_back_kernel(layer, sec_ref, cj_ref, x_ref, cm_ref, pack_ref, own_ref, other_ref,
                    ci_ref, small_ref, w_ref, acc, sem):
    step = pl.program_id(0)
    arrive = fetch_weights(layer, sec_ref, [(own_ref, other_ref, w_ref)], sem)

    @pl.when(step == 0)
    def _():
        acc[...] = jnp.zeros_like(acc)

    width = x_ref.shape[-1]
    (gain_ref,) = vectors_of(pack_ref, width, FIRST_GAIN)
    arrive(0)
    slope = nt(cj_ref[0], w_ref[:, 0:width])
    for which in range(1, 3):
        slope = slope + nt(cj_ref[which], w_ref[:, which * width:(which + 1) * width])
    unit, scale = normalize(x_ref[...].astype(F32))
    acc[0] += fold(slope * unit)
    for which in range(3):
        acc[which + 1] += fold(cj_ref[which].astype(F32))
    ci_ref[...] = (cm_ref[...] + norm_back(slope * gain_ref[...], unit, scale)).astype(BF16)

    @pl.when(step == pl.num_programs(0) - 1)
    def _():
        for index in range(4):
            small_ref[index:index + 1, :] = jnp.sum(acc[index], axis=0, keepdims=True)


def qkv_back(layer, sec, cj, x, cm, pack, own, other, tb=256):
    rows, width = x.shape
    const = lambda n, m=1: pl.BlockSpec((m, n), lambda i: (0, 0))
    tok = lambda n: pl.BlockSpec((tb, n), lambda i: (i, 0))
    S = jax.ShapeDtypeStruct
    return pl.pallas_call(
        functools.partial(qkv_back_kernel, layer),
        grid=(rows // tb,),
        in_specs=[SMEM, pl.BlockSpec((3, tb, width), lambda i: (0, i, 0)), tok(width), tok(width), pack_spec(layer, pack), ANY, ANY],
        out_specs=[tok(width), const(width, 4)],
        out_shape=[S((rows, width), BF16), S((4, width), F32)],
        scratch_shapes=[pltpu.VMEM(own.shape, BF16), pltpu.VMEM((4, 8, width), F32), pltpu.SemaphoreType.DMA((1,))],
        compiler_params=pltpu.CompilerParams(vmem_limit_bytes=VLIM),
        cost_estimate=pl.CostEstimate(flops=2 * rows * width * 3 * width, bytes_accessed=16 * 1024 * 1024, transcendentals=0),
        name="joint_backward",
    )(sec, cj, x, cm, pack, own, other)


def feed_grads_kernel(sec_ref, order_ref, cb_ref, hid_ref, c_ref, n2_ref, cm_ref, in_ref, wide_ref, thin_ref,
                      keep_ref, send_ref, c_t, cm_t):
    step = pl.program_id(0)
    sec = sec_ref[0]
    parts = order_ref.shape[0] // 2
    half = n2_ref.shape[-1] // 2
    up_rows = cb_ref.shape[-1] // 2
    thin = c_ref.shape[-1] // parts
    steps = pl.num_programs(0) // 2
    outs = (keep_ref, send_ref)
    sides = [pl.ds(pl.multiple_of(which * half, 128), half) for which in (sec, 1 - sec)]

    @pl.when(step == 0)
    def _():
        c_t[...] = c_ref[...].T
        cm_t[...] = cm_ref[...].T
        for window in range(parts // 2):
            at = pl.ds(window * half, half)
            far = pl.ds(window // (parts // 4) * half, half)
            rows = jnp.concatenate([wide_ref[:, at], thin_ref[:, far], jnp.zeros((10, half), F32)], axis=0).astype(BF16)
            for side in range(2):
                for sub in range(2):
                    outs[side][order_ref[side * parts + window * 2 + sub], up_rows * 2 + thin:, :] = rows

    for side in range(2):
        up = tn(cb_ref[...], n2_ref[:, sides[side]]).astype(BF16)
        for sub in range(2):
            at = order_ref[side * parts + step * 2 + sub]
            outs[side][at, 0:up_rows, :] = up[sub * up_rows:(sub + 1) * up_rows]

    down = nn(c_t[...], hid_ref[...]).astype(BF16)
    rows = pl.ds(pl.multiple_of(up_rows + thin * (step % steps), 16), thin)
    for side in range(2):
        @pl.when(step // steps == side)
        def _():
            for part in range(parts):
                outs[side][order_ref[side * parts + part], rows, :] = down[thin * part:thin * (part + 1)]

        @pl.when(step == side * steps)
        def _():
            out = nn(cm_t[...], in_ref[:, sides[side]]).astype(BF16)
            for part in range(parts):
                outs[side][order_ref[side * parts + part], 2 * up_rows:2 * up_rows + thin, :] = out[thin * part:thin * (part + 1)]


def feed_grads(sec, order, cb, hidden, c, n2, cm, inner, wide_sums, thin_sums):
    rows, width = c.shape
    wide = cb.shape[-1]
    parts = order.shape[0] // 2
    half = width // 2
    steps = wide // half
    up_rows = wide // parts
    total = 2 * up_rows + width // parts + 16
    full = lambda n, m=rows: pl.BlockSpec((m, n), lambda i, s, o: (0, 0))
    out_spec = pl.BlockSpec((parts, total, half), lambda i, s, o: (0, 0, 0))
    out_shape = jax.ShapeDtypeStruct((parts, total, half), BF16)
    return pl.pallas_call(
        feed_grads_kernel,
        grid_spec=pltpu.PrefetchScalarGridSpec(
            num_scalar_prefetch=2,
            grid=(steps,),
            in_specs=[
                pl.BlockSpec((rows, half), lambda i, s, o: (0, i)),
                pl.BlockSpec((rows, half), lambda i, s, o: (0, jnp.where(i < steps // 2, s[0], 1 - s[0]) * (steps // 2) + i % (steps // 2))),
                full(width), full(width), full(width), full(width), full(wide, 2), full(width, 4),
            ],
            out_specs=[out_spec, out_spec],
            scratch_shapes=[pltpu.VMEM((width, rows), BF16), pltpu.VMEM((width, rows), BF16)],
        ),
        out_shape=[out_shape, out_shape],
        compiler_params=pltpu.CompilerParams(vmem_limit_bytes=VLIM),
        cost_estimate=pl.CostEstimate(flops=2 * rows * width * (2 * wide + width), bytes_accessed=30 * 1024 * 1024, transcendentals=0),
        name="feed_gradients",
    )(sec, order, cb, hidden, c, n2, cm, inner, wide_sums, thin_sums)


def joint_grads_kernel(sec_ref, order_ref, cj_ref, n_ref, sums_ref, keep_ref, send_ref):
    step = pl.program_id(0)
    sec = sec_ref[0]
    parts = order_ref.shape[0] // 2
    width = n_ref.shape[-1]
    half = width // 2
    thick = 3 * width // parts
    outs = (keep_ref, send_ref)
    for side, which in enumerate((sec, 1 - sec)):
        sums = tn(cj_ref[0], n_ref[:, pl.ds(pl.multiple_of(which * half, 128), half)]).astype(BF16)
        for block in range(3):
            @pl.when(step == block)
            def _():
                for part in range(parts):
                    low, high = max(thick * part, width * block), min(thick * (part + 1), width * (block + 1))
                    if low < high:
                        at = order_ref[side * parts + part]
                        outs[side][at, low - thick * part:high - thick * part, :] = sums[low - width * block:high - width * block]

    @pl.when(step == 0)
    def _():
        for part in range(parts):
            window = thick * part // half
            rows = [sums_ref[1 + w // 2:2 + w // 2, w % 2 * half:w % 2 * half + half] for w in (window, min(window + 1, 5))]
            far = part // (parts // 2) * half
            rows = jnp.concatenate(rows + [sums_ref[0:1, far:far + half], jnp.zeros((13, half), F32)], axis=0).astype(BF16)
            for side in range(2):
                outs[side][order_ref[side * parts + part], thick:, :] = rows


def joint_grads(sec, order, cj, normed, sums):
    rows, width = normed.shape
    parts = order.shape[0] // 2
    half = width // 2
    thick = 3 * width // parts
    out_spec = pl.BlockSpec((parts, thick + 16, half), lambda i, s, o: (0, 0, 0))
    out_shape = jax.ShapeDtypeStruct((parts, thick + 16, half), BF16)
    return pl.pallas_call(
        joint_grads_kernel,
        grid_spec=pltpu.PrefetchScalarGridSpec(
            num_scalar_prefetch=2,
            grid=(3,),
            in_specs=[
                pl.BlockSpec((1, rows, width), lambda i, s, o: (i, 0, 0)),
                pl.BlockSpec((rows, width), lambda i, s, o: (0, 0)),
                pl.BlockSpec((4, width), lambda i, s, o: (0, 0)),
            ],
            out_specs=[out_spec, out_spec],
        ),
        out_shape=[out_shape, out_shape],
        compiler_params=pltpu.CompilerParams(vmem_limit_bytes=VLIM),
        cost_estimate=pl.CostEstimate(flops=6 * rows * width * width, bytes_accessed=14 * 1024 * 1024, transcendentals=0),
        name="joint_gradients",
    )(sec, order, cj, normed, sums)


def prepare_kernel(lengths, mine_ref, part_ref, seg_ref, rate_ref, *refs):
    vectors, (cos_ref, sin_ref, lab_ref, pack_ref) = refs[:len(lengths)], refs[len(lengths):]
    begin = 0
    for vector, length in zip(vectors, lengths):
        pack_ref[:, begin:begin + length] = vector[...]
        begin += length
    rows = seg_ref.shape[-1]
    piece = rows // 2
    second = jnp.full((1, 1), part_ref[0]) == 1
    row = seg_ref[0].astype(F32)
    turned = jnp.where(second, jnp.concatenate([row[:, piece:], row[:, :piece]], axis=1), row)
    labels = jnp.broadcast_to(turned, (128, rows)).T
    starts = jnp.zeros_like(labels)
    for document in range(1, 5):
        count = jnp.sum(jnp.where(row < document, 1.0, 0.0), axis=1, keepdims=True)
        starts = jnp.where(labels == document, count, starts)
    time = lax.broadcasted_iota(jnp.int32, labels.shape, 0).astype(F32)
    shift = jnp.where(second, jnp.where(time < piece, piece * 1.0, -piece * 1.0), 0.0)
    angle = (time + shift - starts) * rate_ref[...]
    lane = lane_iota(labels.shape)
    cos_ref[...] = jnp.cos(angle)
    sin_ref[...] = jnp.sin(angle) * jnp.where(lane % HEAD_DIM < HEAD_DIM // 2, -1.0, 1.0)
    lab_ref[...] = labels.astype(jnp.int32)


def prepare(mine, part, segments, vectors):
    rows = segments.shape[-1]
    lengths = tuple(vector.shape[-1] for vector in vectors)
    half = HEAD_DIM // 2
    rate = jnp.tile(1.0 / 10000.0 ** (jnp.arange(half, dtype=F32) * 2.0 / HEAD_DIM), 4)[None]
    whole = lambda m, n: pl.BlockSpec((m, n), lambda i, a, b: (0, 0))
    return pl.pallas_call(
        functools.partial(prepare_kernel, lengths),
        grid_spec=pltpu.PrefetchScalarGridSpec(
            num_scalar_prefetch=2,
            grid=(1,),
            in_specs=[pl.BlockSpec((1, 1, rows), lambda i, a, b: (a[0], 0, 0)), whole(1, 128)] + [whole(1, length) for length in lengths],
            out_specs=[whole(rows, 128), whole(rows, 128), whole(rows, 128), whole(1, sum(lengths))],
        ),
        out_shape=[jax.ShapeDtypeStruct((rows, 128), F32)] * 2 + [jax.ShapeDtypeStruct((rows, 128), jnp.int32), jax.ShapeDtypeStruct((1, sum(lengths)), F32)],
        compiler_params=pltpu.CompilerParams(vmem_limit_bytes=VLIM),
        name="row_tables",
    )(mine.reshape(1).astype(jnp.int32), part.reshape(1).astype(jnp.int32), segments, rate, *vectors)


def swap_pairs(change, sizes):
    sections, dps, seqs = sizes
    pairs = []
    for section in range(sections):
        for dp in range(dps):
            for seq in range(seqs):
                a, b, c = change(section, dp, seq)
                pairs.append(((section * dps + dp) * seqs + seq, (a * dps + b) * seqs + c))
    return pairs


FEED, JOINT = range(2)


class Reduction:
    def __init__(self, kept, sent, sizes):
        self.sizes = sizes
        self.kept, self.sent = kept, sent
        self.stage = 0
        self.result = None

    def send(self):
        if self.stage == 0:
            self.arrived = lax.ppermute(self.sent, "section", [(0, 1), (1, 0)])
        else:
            moves = (
                lambda s, d, q: (s, d ^ 1, q) if s == 0 else (s, d, q ^ 1),
                lambda s, d, q: (s, d, q ^ 1) if s == 0 else (s, d ^ 1, q),
                lambda s, d, q: (s, d ^ 2, q),
                lambda s, d, q: (s, d ^ 4, q),
            )
            self.arrived = lax.ppermute(self.sent, ("section", "dp", "seq"), swap_pairs(moves[self.stage - 1], self.sizes))
        self.stage += 1

    def add(self):
        kept, arrived = self.kept, self.arrived
        middle = kept.shape[0] // 2
        if middle == 0:
            self.result = kept[0].astype(F32) + arrived[0].astype(F32)
            return
        self.sent = (kept[middle:].astype(F32) + arrived[middle:].astype(F32)).astype(BF16)
        self.kept = (kept[:middle].astype(F32) + arrived[:middle].astype(F32)).astype(BF16)

    def finish(self):
        if self.result is not None:
            return self.result
        while self.stage < 5:
            self.add()
            self.send()
        self.add()
        return self.result


def advance(value, *moving):
    for item in moving:
        if item.stage:
            item.add()
    if all(item.stage == 5 for item in moving):
        results = [item.result for item in moving]
        value, results = lax.optimization_barrier((value, results))
        for item, result in zip(moving, results):
            item.result = result
        return value
    parts = [array for item in moving for array in (item.kept, item.sent)]
    value, parts = lax.optimization_barrier((value, parts))
    for index, item in enumerate(moving):
        item.kept, item.sent = parts[2 * index:2 * index + 2]
        item.send()
    return value


def row_step(
    sizes,
    tokens,
    segments,
    cotangent,
    joint_weight,
    joint_bias,
    output_weight,
    output_bias,
    up_weight,
    up_bias,
    down_weight,
    down_bias,
    first_gain,
    inner_gain,
    second_gain,
    hidden_gain,
):
    micro, row_count, piece, width = tokens.shape
    rows = 2 * piece
    wide = up_weight.shape[-1]
    parts = sizes[1] * sizes[2]
    half = width // 2
    section = lax.axis_index("section")
    part = lax.axis_index("seq")
    data = lax.axis_index("dp")
    sec = section.reshape(1).astype(jnp.int32)
    mine = 2 * section + part
    swap = [(0, 1), (1, 0)]

    def pick(array, index):
        return lax.dynamic_index_in_dim(array, index, 0, keepdims=False)

    flat_tokens = tokens.reshape(micro * row_count, piece, width)
    beside = lax.ppermute(pick(flat_tokens, mine ^ 1), "seq", swap)
    both = [(own[0], lax.ppermute(own[0], "section", swap)) for own in (joint_weight, output_weight, up_weight, down_weight)]
    joint_pair, output_pair, up_pair, down_pair = both
    cosine, sine, labels, own = prepare(mine, part, segments.reshape(micro * row_count, 1, rows), (
        joint_bias, output_bias, up_bias, down_bias, first_gain, inner_gain, second_gain, hidden_gain))
    other = lax.ppermute(own, "section", swap)
    pack = jnp.where(section == 0, jnp.stack([own, other]), jnp.stack([other, own]))

    mx, my, mz = data % 2, part, data // 2
    index = jnp.arange(parts, dtype=jnp.int32)
    cx, cy, cz = (index // 2) % 2 ^ mx, index % 2 ^ my, index // 4 ^ mz
    depth = cz % 2 * 2 + cz // 2
    order_x, order_y = (cx * 2 + cy) * 4 + depth, (cy * 2 + cx) * 4 + depth
    order = jnp.where(section == 0, jnp.concatenate([order_x, order_y]), jnp.concatenate([order_y, order_x]))

    kept = []
    hiddens = []
    for layer in range(2):
        if layer == 0:
            state, normed, q, k, v = qkv(layer, sec, (flat_tokens, beside), pack, *joint_pair, cosine, sine, labels, mine)
            state, cotangent = lax.optimization_barrier((state, cotangent))
            flat = cotangent.reshape(micro * row_count, piece, width)
            slope = jnp.concatenate([pick(flat, mine), lax.ppermute(pick(flat, mine ^ 1), "seq", swap)], axis=0)
        else:
            _, normed, q, k, v = qkv(layer, sec, state, pack, *joint_pair, cosine, sine, labels, mine)
        attended, query = attend(q, k, v)
        result, mixed, hidden, bend, stats = feed(layer, sec, attended, state, pack, output_pair, up_pair, down_pair)
        kept.append((state, normed, query, k, v, attended, mixed, hidden, bend, stats))
        hiddens.append(result)
        state = result

    def halves(item):
        return item[:piece], item[piece:]

    every = ("section", "seq")
    blocks = []
    for fs, fq in ((0, 1), (1, 0), (1, 1)):
        first, second = (halves(item)[fq] for item in hiddens)
        owed = jnp.where(section == fs, first, second)
        blocks.append((owed, [(2 * s + q, 2 * (s ^ fs) + (q ^ fq)) for s in range(2) for q in range(2)]))
    slope, owed = lax.optimization_barrier((slope, [block for block, pairs in blocks]))
    gathered = [lax.ppermute(block, every, pairs) for block, (_, pairs) in zip(owed, blocks)]
    own = jnp.where(section == 0, halves(hiddens[0])[0], halves(hiddens[1])[0])

    def place(blocks):
        stacked = jnp.stack(blocks)
        return jnp.stack([pick(stacked, mine ^ index) for index in range(4)]).reshape(1, micro, row_count, piece, width)

    def deliver(layer, back):
        own, other = halves(back)
        moves = (
            (other, [(2 * layer + q, 2 * layer + (q ^ 1)) for q in range(2)]),
            (own, [(2 * (1 - layer) + q, 2 * layer + q) for q in range(2)]),
            (other, [(2 * (1 - layer) + q, 2 * layer + (q ^ 1)) for q in range(2)]),
        )
        return [own] + [lax.ppermute(block, every, pairs) for block, pairs in moves]

    flights = {}
    delivered = [None, None]

    for layer in (1, 0):
        state, normed, query, k, v, attended, mixed, hidden, bend, stats = kept[layer]
        cb, cm, cm_low, ch, n2, inner, wide_sums, thin_sums = feed_back(
            layer, sec, slope, hidden, bend, stats, mixed, attended, pack, output_pair, up_pair, down_pair)
        if layer == 0:
            cb = advance(cb, flights[FEED, 1], flights[JOINT, 1])
        flights[FEED, layer] = Reduction(*feed_grads(sec, order, cb, hidden, slope, n2, cm_low, inner, wide_sums, thin_sums), sizes)
        if layer == 1:
            ch = advance(ch, flights[FEED, 1])
            cj = attend_back(query, k, v, ch, attended, cosine, sine)
            cj, gathered = lax.optimization_barrier((cj, gathered))
            cj = advance(cj, flights[FEED, 1])
        else:
            ch, delivered[1] = lax.optimization_barrier((ch, delivered[1]))
            ch = advance(ch, flights[FEED, 0], flights[FEED, 1], flights[JOINT, 1])
            count = query.shape[0] // 4
            cj = attend_back(query, k, v, ch, attended, cosine, sine, 0, count)
            cj = advance(cj, flights[FEED, 0], flights[FEED, 1], flights[JOINT, 1])
            cj = attend_back(query, k, v, ch, attended, cosine, sine, count, None, cj)
            cj = advance(cj, flights[FEED, 1])
            cj = advance(cj, flights[JOINT, 1], flights[FEED, 0])
        back, sums = qkv_back(layer, sec, cj, state, cm, pack, *joint_pair)
        delivered[layer] = deliver(layer, back)
        if layer == 0:
            cj = advance(cj, flights[JOINT, 1])
            cj = advance(cj, flights[FEED, 0])
        flights[JOINT, layer] = Reduction(*joint_grads(sec, order, cj, normed, sums), sizes)
        if layer == 1:
            back = advance(back, flights[JOINT, 1])
        slope = back
    last, before = flights[JOINT, 0], flights[FEED, 0]
    last.send()
    last.add()
    before.kept, _ = lax.optimization_barrier((before.kept, last.sent))
    last.send()
    hiddens = place([own] + gathered)
    input_gradients = place([jnp.where(section == 0, a, b) for a, b in zip(*delivered)]).astype(F32)

    def settle(name):
        grads = [flights[name, layer].finish() for layer in range(2)]
        ours = jnp.where(section == 0, grads[0], grads[1])
        theirs = lax.ppermute(jnp.where(section == 0, grads[1], grads[0]), "section", swap)
        return jnp.where(section == 0, ours, theirs), jnp.where(section == 0, theirs, ours)

    left, right = settle(FEED)
    up_rows, thin, thick = wide // parts, width // parts, 3 * width // parts

    def rows_of(begin, count):
        return jnp.concatenate([left[begin:begin + count], right[begin:begin + count]], axis=1)

    up_grad = rows_of(0, up_rows).T
    at = up_rows
    steps = up_rows // thin
    sides = [item[at:at + up_rows].reshape(steps, thin, half).transpose(0, 2, 1).reshape(steps * half, thin) for item in (left, right)]
    down_grad = jnp.concatenate(sides, axis=0)
    at += up_rows
    output_grad = rows_of(at, thin).T
    at += thin
    index = 2 * data + part

    def piece_of(row, count):
        return lax.dynamic_slice_in_dim(row, index * count % half, count)

    hg, ub = (piece_of(left[at + number], up_rows) for number in range(2))
    db, sg, ob, ig = (piece_of(left[at + 2 + number], thin) for number in range(4))
    left, right = settle(JOINT)
    joint_grad = rows_of(0, thick).T
    at = thick
    jb = lax.dynamic_slice_in_dim(jnp.concatenate([left[at], left[at + 1]]), index * thick % half, thick)
    fg = piece_of(left[at + 2], thin)
    return (
        hiddens,
        input_gradients,
        joint_grad[None],
        jb[None],
        output_grad[None],
        ob[None],
        up_grad[None],
        ub[None],
        down_grad[None],
        db[None],
        fg[None],
        ig[None],
        sg[None],
        hg[None],
    )


def choose(sizes, *arrays):
    micro, row_count, piece, width = arrays[0].shape
    if sizes == (2, 8, 2) and micro * row_count == 4:
        return row_step(sizes, *arrays)
    return shards(*arrays)


def solution(mesh):
    axes = ("section", "dp", "seq")
    return jax.shard_map(
        functools.partial(choose, tuple(mesh.shape[name] for name in axes)),
        mesh=mesh,
        in_specs=(
            P(None, "dp", "seq", None),
            P(None, "dp", None),
            P(None, "dp", "seq", None),
            P("section", None, None),
            P("section", None),
            P("section", None, None),
            P("section", None),
            P("section", None, None),
            P("section", None),
            P("section", None, None),
            P("section", None),
            P("section", None),
            P("section", None),
            P("section", None),
            P("section", None),
        ),
        out_specs=(
            P("section", None, "dp", "seq", None),
            P("section", None, "dp", "seq", None),
            P("section", None, ("dp", "seq")),
            P("section", ("dp", "seq")),
            P("section", None, ("dp", "seq")),
            P("section", ("dp", "seq")),
            P("section", None, ("dp", "seq")),
            P("section", ("dp", "seq")),
            P("section", None, ("dp", "seq")),
            P("section", ("dp", "seq")),
            P("section", ("dp", "seq")),
            P("section", ("dp", "seq")),
            P("section", ("dp", "seq")),
            P("section", ("dp", "seq")),
        ),
        check_vma=False,
    )
```

```python
import functools
import math

import jax
import jax.numpy as jnp
from jax import lax
from jax.experimental import pallas as pl
from jax.experimental.pallas import tpu as pltpu
from jax.sharding import PartitionSpec as P

HEAD_DIM = 64


EPSILON = 1e-05
MASKED = -1e30


def passed_along(value, axis, by):
    devices = lax.axis_size(axis)
    pairs = [(i, i + by) for i in range(devices) if 0 <= i + by < devices]
    return lax.ppermute(value, axis, pairs)


def layer_norm(value, gain):
    centered = value - jnp.mean(value, axis=-1, keepdims=True)
    spread = jnp.mean(centered * centered, axis=-1, keepdims=True)
    return centered * lax.rsqrt(spread + EPSILON) * gain


def feed_norm(before, gain):
    return layer_norm(jax.nn.gelu(before, approximate=False), gain)


def rotate(value, cosine, sine):
    middle = value.shape[-1] // 2
    first, second = (value[..., :middle], value[..., middle:])
    return jnp.concatenate(
        [first * cosine - second * sine, second * cosine + first * sine], axis=-1
    )


def rotate_back(incoming, cosine, sine):
    middle = incoming.shape[-1] // 2
    first, second = (incoming[..., :middle], incoming[..., middle:])
    return jnp.concatenate(
        [first * cosine + second * sine, second * cosine - first * sine], axis=-1
    )


def layer_forward(state, labels, weights, part):
    (
        joint_weight,
        joint_bias,
        output_weight,
        output_bias,
        up_weight,
        up_bias,
        down_weight,
        down_bias,
        first_gain,
        inner_gain,
        second_gain,
        hidden_gain,
    ) = weights
    row_count, piece_len, model_width = state.shape
    head_count = model_width // HEAD_DIM
    shape_heads = (row_count, piece_len, head_count, HEAD_DIM)
    offset = part * piece_len
    local_labels = lax.dynamic_slice_in_dim(labels, offset, piece_len, 1)
    starts = jnp.sum((labels[:, None, :] < local_labels[:, :, None]).astype(jnp.int32), axis=-1)
    places = offset + jnp.arange(piece_len, dtype=jnp.int32)[None, :] - starts
    inverse_rate = 1.0 / 10000.0 ** (jnp.arange(HEAD_DIM // 2, dtype=jnp.float32) * 2.0 / HEAD_DIM)
    angle = places.astype(jnp.float32)[:, :, None, None] * inverse_rate
    cosine = jnp.cos(angle)
    sine = jnp.sin(angle)
    normed = layer_norm(state, first_gain).astype(jnp.bfloat16)
    joint = jnp.dot(normed, joint_weight, preferred_element_type=jnp.float32) + joint_bias
    query = rotate(joint[..., :model_width].reshape(shape_heads), cosine, sine).astype(jnp.bfloat16)
    key = rotate(
        joint[..., model_width : 2 * model_width].reshape(shape_heads), cosine, sine
    ).astype(jnp.bfloat16)
    value = joint[..., 2 * model_width :].reshape(shape_heads).astype(jnp.bfloat16)
    keys_all, values_all = (
        lax.all_gather(key, "seq", axis=1, tiled=True),
        lax.all_gather(value, "seq", axis=1, tiled=True),
    )
    match = local_labels[:, None, :, None] == labels[:, None, None, :]
    scores = jnp.einsum(
        "rqhd,rkhd->rhqk", query, keys_all, preferred_element_type=jnp.float32
    ) * HEAD_DIM ** (-0.5)
    scores = jnp.where(match, scores, MASKED)
    peak = jnp.max(scores, axis=-1, keepdims=True)
    raised = jnp.exp(scores - peak)
    total_raised = jnp.sum(raised, axis=-1, keepdims=True)
    shares = raised / total_raised
    log_total = peak + jnp.log(total_raised)
    attended = jnp.einsum(
        "rhqk,rkhd->rqhd",
        shares.astype(jnp.bfloat16),
        values_all,
        preferred_element_type=jnp.float32,
    ).reshape(row_count, piece_len, model_width)
    inner = layer_norm(attended, inner_gain).astype(jnp.bfloat16)
    mixed = state + jnp.dot(inner, output_weight, preferred_element_type=jnp.float32) + output_bias
    normed_two = layer_norm(mixed, second_gain).astype(jnp.bfloat16)
    before = jnp.dot(normed_two, up_weight, preferred_element_type=jnp.float32) + up_bias
    hidden = feed_norm(before, hidden_gain).astype(jnp.bfloat16)
    result = mixed + jnp.dot(hidden, down_weight, preferred_element_type=jnp.float32) + down_bias
    kept = (
        state,
        normed,
        query,
        keys_all,
        values_all,
        cosine,
        sine,
        match,
        shares,
        attended,
        inner,
        mixed,
        normed_two,
        before,
        hidden,
        log_total,
        labels,
    )
    return (result, kept)


def feed_backward(kept, slope_out, weights, totals):
    (
        state,
        normed,
        query,
        keys_all,
        values_all,
        cosine,
        sine,
        match,
        shares,
        attended,
        inner,
        mixed,
        normed_two,
        before,
        hidden,
        log_total,
        labels,
    ) = kept
    (
        joint_weight,
        joint_bias,
        output_weight,
        output_bias,
        up_weight,
        up_bias,
        down_weight,
        down_bias,
        first_gain,
        inner_gain,
        second_gain,
        hidden_gain,
    ) = weights
    slope_low = slope_out.astype(jnp.bfloat16)
    totals[6] = totals[6] + jnp.einsum(
        "rcf,rcd->fd", hidden, slope_low, preferred_element_type=jnp.float32
    )
    totals[7] = totals[7] + jnp.sum(slope_low.astype(jnp.float32), axis=(0, 1))
    slope_hidden = jnp.einsum(
        "rcd,fd->rcf", slope_low, down_weight, preferred_element_type=jnp.float32
    )
    unused, puller = jax.vjp(feed_norm, before, hidden_gain)
    slope_before, slope_gain = puller(slope_hidden)
    totals[11] = totals[11] + slope_gain
    before_low = slope_before.astype(jnp.bfloat16)
    totals[4] = totals[4] + jnp.einsum(
        "rcd,rcf->df", normed_two, before_low, preferred_element_type=jnp.float32
    )
    totals[5] = totals[5] + jnp.sum(before_low.astype(jnp.float32), axis=(0, 1))
    slope_normed = jnp.einsum(
        "rcf,df->rcd", before_low, up_weight, preferred_element_type=jnp.float32
    )
    unused, puller = jax.vjp(layer_norm, mixed, second_gain)
    slope_mixed, slope_gain = puller(slope_normed)
    totals[10] = totals[10] + slope_gain
    return (slope_out + slope_mixed, totals)


def attend_backward(kept, slope_mixed, weights, totals):
    (
        state,
        normed,
        query,
        keys_all,
        values_all,
        cosine,
        sine,
        match,
        shares,
        attended,
        inner,
        mixed,
        normed_two,
        before,
        hidden,
        log_total,
        labels,
    ) = kept
    (
        joint_weight,
        joint_bias,
        output_weight,
        output_bias,
        up_weight,
        up_bias,
        down_weight,
        down_bias,
        first_gain,
        inner_gain,
        second_gain,
        hidden_gain,
    ) = weights
    row_count, piece_len, model_width = state.shape
    head_count = model_width // HEAD_DIM
    scale = HEAD_DIM ** (-0.5)
    slope_low = slope_mixed.astype(jnp.bfloat16)
    totals[2] = totals[2] + jnp.einsum(
        "rcd,rce->de", inner, slope_low, preferred_element_type=jnp.float32
    )
    totals[3] = totals[3] + jnp.sum(slope_low.astype(jnp.float32), axis=(0, 1))
    slope_inner = jnp.einsum(
        "rce,de->rcd", slope_low, output_weight, preferred_element_type=jnp.float32
    )
    unused, puller = jax.vjp(layer_norm, attended, inner_gain)
    slope_attended, slope_gain = puller(slope_inner)
    totals[9] = totals[9] + slope_gain
    slope_heads = slope_attended.astype(jnp.bfloat16).reshape(
        row_count, piece_len, head_count, HEAD_DIM
    )
    slope_shares = jnp.einsum(
        "rqhd,rkhd->rhqk", slope_heads, values_all, preferred_element_type=jnp.float32
    )
    weighted = jnp.sum(shares * slope_shares, axis=-1, keepdims=True)
    slope_scores = (shares * (slope_shares - weighted)).astype(jnp.bfloat16)
    slope_query = (
        jnp.einsum("rhqk,rkhd->rqhd", slope_scores, keys_all, preferred_element_type=jnp.float32)
        * scale
    )
    shares_low = shares.astype(jnp.bfloat16)
    key_part = (
        jnp.einsum("rhqk,rqhd->krhd", slope_scores, query, preferred_element_type=jnp.float32)
        * scale
    )
    value_part = jnp.einsum(
        "rhqk,rqhd->krhd", shares_low, slope_heads, preferred_element_type=jnp.float32
    )
    summed = lax.psum_scatter(
        jnp.concatenate([key_part, value_part], axis=-1).astype(jnp.bfloat16),
        "seq",
        scatter_dimension=0,
        tiled=True,
    ).astype(jnp.float32)
    summed = jnp.transpose(summed, (1, 0, 2, 3))
    key_raw = summed[..., :HEAD_DIM]
    slope_value = summed[..., HEAD_DIM:]
    slope_key = rotate_back(key_raw, cosine, sine)
    slope_query = rotate_back(slope_query, cosine, sine)
    flat = (row_count, piece_len, model_width)
    slope_joint = jnp.concatenate(
        [slope_query.reshape(flat), slope_key.reshape(flat), slope_value.reshape(flat)], axis=-1
    ).astype(jnp.bfloat16)
    totals[0] = totals[0] + jnp.einsum(
        "rcd,rce->de", normed, slope_joint, preferred_element_type=jnp.float32
    )
    totals[1] = totals[1] + jnp.sum(slope_joint.astype(jnp.float32), axis=(0, 1))
    slope_normed = jnp.einsum(
        "rce,de->rcd", slope_joint, joint_weight, preferred_element_type=jnp.float32
    )
    unused, puller = jax.vjp(layer_norm, state, first_gain)
    slope_state, slope_gain = puller(slope_normed)
    totals[8] = totals[8] + slope_gain
    return (slope_mixed + slope_state, totals)


def lift(vector):
    return vector.reshape(1, vector.shape[0])


def shards(
    tokens,
    segments,
    cotangent,
    joint_weight,
    joint_bias,
    output_weight,
    output_bias,
    up_weight,
    up_bias,
    down_weight,
    down_bias,
    first_gain,
    inner_gain,
    second_gain,
    hidden_gain,
):
    weights = tuple(
        (
            item[0]
            for item in (
                joint_weight,
                joint_bias,
                output_weight,
                output_bias,
                up_weight,
                up_bias,
                down_weight,
                down_bias,
                first_gain,
                inner_gain,
                second_gain,
                hidden_gain,
            )
        )
    )
    micro, row_count, piece_len, model_width = tokens.shape
    leading = lax.axis_index("section") == 0
    part = lax.axis_index("seq")
    received = jnp.zeros((row_count, piece_len, model_width), jnp.bfloat16)
    saved = []
    results = []
    for moment in range(micro + 1):
        labels = jnp.where(leading, segments[min(moment, micro - 1)], segments[max(moment - 1, 0)])
        source = jnp.where(leading, tokens[min(moment, micro - 1)], received)
        state = source.astype(jnp.float32)
        result, kept = layer_forward(state, labels, weights, part)
        sent = result.astype(jnp.bfloat16)
        results.append(sent)
        saved.append((state, labels))
        if moment < micro:
            received = passed_along(sent, "section", 1)
    totals = [jnp.zeros(item.shape, jnp.float32) for item in weights]
    back_received = jnp.zeros((row_count, piece_len, model_width), jnp.bfloat16)
    back_results = []
    for moment in range(micro + 1):
        earlier = max(moment - 1, 0)
        later = min(moment + 1, micro)
        state = jnp.where(leading, saved[earlier][0], saved[later][0])
        labels = jnp.where(leading, saved[earlier][1], saved[later][1])
        kept = layer_forward(state, labels, weights, part)[1]
        if moment < micro:
            outer = cotangent[moment].astype(jnp.float32)
        else:
            outer = jnp.zeros((row_count, piece_len, model_width), jnp.float32)
        slope_out = jnp.where(leading, back_received.astype(jnp.float32), outer)
        slope_mixed, totals = feed_backward(kept, slope_out, weights, totals)
        slope_input, totals = attend_backward(kept, slope_mixed, weights, totals)
        back_results.append(slope_input)
        if moment < micro:
            back_received = passed_along(slope_input.astype(jnp.bfloat16), "section", -1)
    reduced = (
        lax.psum_scatter(totals[0], ("dp", "seq"), scatter_dimension=1, tiled=True),
        lax.psum_scatter(lift(totals[1]), ("dp", "seq"), scatter_dimension=1, tiled=True),
        lax.psum_scatter(totals[2], ("dp", "seq"), scatter_dimension=1, tiled=True),
        lax.psum_scatter(lift(totals[3]), ("dp", "seq"), scatter_dimension=1, tiled=True),
        lax.psum_scatter(totals[4], ("dp", "seq"), scatter_dimension=1, tiled=True),
        lax.psum_scatter(lift(totals[5]), ("dp", "seq"), scatter_dimension=1, tiled=True),
        lax.psum_scatter(totals[6], ("dp", "seq"), scatter_dimension=1, tiled=True),
        lax.psum_scatter(lift(totals[7]), ("dp", "seq"), scatter_dimension=1, tiled=True),
        lax.psum_scatter(lift(totals[8]), ("dp", "seq"), scatter_dimension=1, tiled=True),
        lax.psum_scatter(lift(totals[9]), ("dp", "seq"), scatter_dimension=1, tiled=True),
        lax.psum_scatter(lift(totals[10]), ("dp", "seq"), scatter_dimension=1, tiled=True),
        lax.psum_scatter(lift(totals[11]), ("dp", "seq"), scatter_dimension=1, tiled=True),
    )
    hiddens = jnp.stack(
        [jnp.where(leading, results[index], results[index + 1]) for index in range(micro)]
    )[None]
    input_gradients = jnp.stack(
        [jnp.where(leading, back_results[index + 1], back_results[index]) for index in range(micro)]
    )[None]
    return (
        hiddens,
        input_gradients,
        reduced[0][None],
        reduced[1],
        reduced[2][None],
        reduced[3],
        reduced[4][None],
        reduced[5],
        reduced[6][None],
        reduced[7],
        reduced[8],
        reduced[9],
        reduced[10],
        reduced[11],
    )


F32 = jnp.float32
BF16 = jnp.bfloat16
ANY = pl.BlockSpec(memory_space=pl.ANY)
SMEM = pl.BlockSpec(memory_space=pltpu.SMEM)
VLIM = 60 * 1024 * 1024


def lane_iota(shape):
    return lax.broadcasted_iota(jnp.int32, shape, len(shape) - 1)


def nn(a, b):
    return lax.dot_general(a, b, (((1,), (0,)), ((), ())), preferred_element_type=F32)


def nt(a, b):
    return lax.dot_general(a, b, (((1,), (1,)), ((), ())), preferred_element_type=F32)


def tn(a, b):
    return lax.dot_general(a, b, (((0,), (0,)), ((), ())), preferred_element_type=F32)


def normalize(value):
    centered = value - jnp.mean(value, axis=-1, keepdims=True)
    scale = lax.rsqrt(jnp.mean(centered * centered, axis=-1, keepdims=True) + EPSILON)
    return centered * scale, scale


def norm_back(slope, unit, scale):
    return scale * (
        slope
        - jnp.mean(slope, axis=-1, keepdims=True)
        - unit * jnp.mean(slope * unit, axis=-1, keepdims=True)
    )


def fold(value):
    rows, columns = value.shape
    return jnp.sum(value.reshape(rows // 8, 8, columns), axis=0)


def split3(value):
    high = value.astype(BF16)
    rest = value - high.astype(F32)
    middle = rest.astype(BF16)
    low = (rest - middle.astype(F32)).astype(BF16)
    return high, middle, low


JOINT_BIAS, OUTPUT_BIAS, UP_BIAS, DOWN_BIAS, FIRST_GAIN, INNER_GAIN, SECOND_GAIN, HIDDEN_GAIN = range(8)


def vectors_of(pack_ref, width, *numbers):
    wide = 4 * width
    lengths = (3 * width, width, wide, width, width, width, width, wide)
    views = []
    for number in numbers:
        views.append(pack_ref.at[0, :, pl.ds(sum(lengths[:number]), lengths[number])])
    return views


def pack_spec(layer, pack):
    return pl.BlockSpec((1, 1, pack.shape[-1]), lambda *_: (layer, 0, 0))


def fetch_weights(layer, sec_ref, pairs, sem):
    first = pl.program_id(0) == 0

    @pl.when(first & (sec_ref[0] == layer))
    def _():
        for index, (own, other, here) in enumerate(pairs):
            pltpu.make_async_copy(own, here, sem.at[index]).start()

    @pl.when(first & (sec_ref[0] != layer))
    def _():
        for index, (own, other, here) in enumerate(pairs):
            pltpu.make_async_copy(other, here, sem.at[index]).start()

    def arrive(index):
        @pl.when(first)
        def _():
            own, other, here = pairs[index]
            pltpu.make_async_copy(own, here, sem.at[index]).wait()

    return arrive


def gelu_parts(value):
    share = 0.5 + 0.5 * lax.erf(value * 0.5 ** 0.5)
    bell = jnp.exp2(value * value * (-0.5 * math.log2(math.e)))
    return value * share, share + value * bell * (1.0 / math.sqrt(2.0 * math.pi))


def qkv_kernel(layer, blocks, sec_ref, mine_ref, x_ref, y_ref, pack_ref, own_ref, other_ref, cos_ref, sin_ref,
               lab_ref, s_ref, n_ref, q_ref, k_ref, v_ref, w_ref, sem):
    arrive = fetch_weights(layer, sec_ref, [(own_ref, other_ref, w_ref)], sem)
    width = x_ref.shape[-1]
    gain_ref, bias_ref = vectors_of(pack_ref, width, FIRST_GAIN, JOINT_BIAS)
    state = jnp.where(jnp.full((1, 1), pl.program_id(0)) < blocks, x_ref[0], y_ref[...])
    s_ref[...] = state
    unit, scale = normalize(state.astype(F32))
    normed = (unit * gain_ref[...]).astype(BF16)
    n_ref[...] = normed
    cosine, sine = cos_ref[...], sin_ref[...]
    lane = lane_iota(cosine.shape)
    first = lane % HEAD_DIM < HEAD_DIM // 2
    head = lane < HEAD_DIM
    labels = lab_ref[...]
    document = lane - HEAD_DIM
    known = (document >= 0) & (document < 5)
    q_feat = jnp.where(known & (document != labels), MASKED, 0.0)
    ones = (document >= 5) & (document < 8)
    k_feat = jnp.where((known & (document == labels)) | ones, 1.0, 0.0)
    v_feat = jnp.where((document >= 0) & (document < 3), 1.0, 0.0)
    kinds = ((q_ref, q_feat), (k_ref, k_feat), (v_ref, v_feat))
    step = 256
    chunks = 3 * width // step

    def product(chunk):
        at = pl.ds(chunk * step, step)
        return nn(normed, w_ref[:, at]) + bias_ref[:, at]

    arrive(0)
    later = product(0)
    for chunk in range(chunks):
        joint = later
        if chunk + 1 < chunks:
            later = product(chunk + 1)
        for sub in range(step // 128):
            pair = chunk * step // 128 + sub
            which = pair * 128 // width
            out, feat = kinds[which]
            pair = pair - which * width // 128
            part = joint[:, sub * 128:(sub + 1) * 128]
            if which < 2:
                turned = jnp.where(first, pltpu.roll(part, 96, 1), pltpu.roll(part, 32, 1))
                part = part * cosine + turned * sine
            if which == 0:
                part = part * HEAD_DIM ** -0.5
            out[2 * pair] = jnp.where(head, part, feat).astype(BF16)
            out[2 * pair + 1] = jnp.where(head, pltpu.roll(part, 64, 1), feat).astype(BF16)


def qkv(layer, sec, x, pack, own, other, cosine, sine, labels, mine, tb=256):
    if isinstance(x, tuple):
        x, y = x
        blocks = x.shape[1] // tb
        rows, width = 2 * x.shape[1], x.shape[2]
    else:
        rows, width = x.shape
        blocks = rows // tb
        x, y = x[None], x
        mine = jnp.int32(0)
    heads = width // HEAD_DIM
    const = lambda shape: pl.BlockSpec(shape, lambda i, s, m: (0,) * len(shape))
    tok = lambda n: pl.BlockSpec((tb, n), lambda i, s, m: (i, 0))
    hd = pl.BlockSpec((heads, tb, 128), lambda i, s, m: (0, i, 0))
    return pl.pallas_call(
        functools.partial(qkv_kernel, layer, blocks),
        grid_spec=pltpu.PrefetchScalarGridSpec(
            num_scalar_prefetch=2,
            grid=(rows // tb,),
            in_specs=[pl.BlockSpec((1, tb, width), lambda i, s, m: (m[0], jnp.minimum(i, blocks - 1), 0)),
                      pl.BlockSpec((tb, width), lambda i, s, m: (jnp.maximum(i - blocks, 0), 0)),
                      pack_spec(layer, pack), ANY, ANY, tok(128), tok(128), tok(128)],
            out_specs=[tok(width), tok(width), hd, hd, hd],
            scratch_shapes=[pltpu.VMEM(own.shape, BF16), pltpu.SemaphoreType.DMA((1,))],
        ),
        out_shape=[jax.ShapeDtypeStruct((rows, width), BF16)] * 2 + [jax.ShapeDtypeStruct((heads, rows, 128), BF16)] * 3,
        compiler_params=pltpu.CompilerParams(vmem_limit_bytes=VLIM),
        cost_estimate=pl.CostEstimate(flops=2 * rows * width * 3 * width, bytes_accessed=16 * 1024 * 1024, transcendentals=0),
        name="joint_projection",
    )(sec, mine.reshape(1).astype(jnp.int32), x, y, pack, own, other, cosine, sine, labels)


def attend_kernel(qb, q_ref, k_ref, v_ref, o_ref, ql_ref):
    rows = q_ref.shape[1]
    lane = lane_iota((qb, 128))
    inside = (lane >= 69) & (lane < 72)
    work = [(head, block) for block in range(rows // qb) for head in range(2)]
    ready = {}

    def score(index):
        if index < len(work):
            head, block = work[index]
            ready[index] = nt(q_ref[head, pl.ds(block * qb, qb), :], k_ref[head])

    score(0)
    score(1)
    done = []
    for index, (head, block) in enumerate(work):
        score(index + 2)
        scores = ready.pop(index)
        at = pl.ds(block * qb, qb)
        peak = jnp.max(scores, axis=-1, keepdims=True)
        raised = jnp.exp(scores - peak).astype(BF16)
        sums = nn(raised, v_ref[head])
        total = sums[:, HEAD_DIM:HEAD_DIM + 1]
        done.append(sums * (1.0 / total))
        high, middle, low = split3(-(peak + jnp.log(total)))
        feat = jnp.where(lane == 69, high.astype(F32), jnp.where(lane == 70, middle.astype(F32), low.astype(F32)))
        ql_ref[head, at, :] = jnp.where(inside, feat, q_ref[head, at, :].astype(F32)).astype(BF16)
        if head == 1:
            o_ref[at, :] = jnp.where(lane < HEAD_DIM, done[0], pltpu.roll(done[1], 64, 1))
            done = []


def attend(q, k, v, qb=256):
    heads, rows, _ = q.shape
    hd = pl.BlockSpec((2, rows, 128), lambda i: (i, 0, 0))
    return pl.pallas_call(
        functools.partial(attend_kernel, qb),
        grid=(heads // 2,),
        in_specs=[hd, hd, hd],
        out_specs=[pl.BlockSpec((rows, 128), lambda i: (0, i)), hd],
        out_shape=[jax.ShapeDtypeStruct((rows, heads * HEAD_DIM), F32), jax.ShapeDtypeStruct(q.shape, BF16)],
        compiler_params=pltpu.CompilerParams(vmem_limit_bytes=VLIM),
        cost_estimate=pl.CostEstimate(flops=16 * heads * rows * rows * HEAD_DIM, bytes_accessed=16 * 1024 * 1024, transcendentals=0),
        name="attention_forward",
    )(q, k, v)


def feed_kernel(layer, sec_ref, at_ref, x_ref, pack_ref,
                wo0, wo1, wu0, wu1, wd0, wd1,
                out_ref, mixed_ref, hid_ref, gp_ref, st_ref, wo, wu, wd, bent, sem):
    arrive = fetch_weights(layer, sec_ref, [(wo0, wo1, wo), (wu0, wu1, wu), (wd0, wd1, wd)], sem)
    ig_ref, ob_ref, sg_ref, ub_ref, hg_ref, db_ref = vectors_of(
        pack_ref, x_ref.shape[-1], INNER_GAIN, OUTPUT_BIAS, SECOND_GAIN, UP_BIAS, HIDDEN_GAIN, DOWN_BIAS)
    wide = hg_ref.shape[-1]
    unit, _ = normalize(at_ref[...])
    inner = (unit * ig_ref[...]).astype(BF16)
    arrive(0)
    mixed = x_ref[...].astype(F32) + nn(inner, wo[...]) + ob_ref[...]
    mixed_ref[...] = mixed
    unit, _ = normalize(mixed)
    normed = (unit * sg_ref[...]).astype(BF16)
    step = 512
    chunks = wide // step

    def rise(chunk):
        at = pl.ds(chunk * step, step)
        return nn(normed, wu[:, at]) + ub_ref[:, at]

    arrive(1)
    later = rise(0)
    total = 0.0
    for chunk in range(chunks):
        before = later
        if chunk + 1 < chunks:
            later = rise(chunk + 1)
        at = pl.ds(chunk * step, step)
        value, bend = gelu_parts(before)
        gp_ref[:, at] = bend.astype(BF16)
        bent[:, at] = value
        total = total + jnp.sum(value, axis=-1, keepdims=True)
    mean = total * (1.0 / wide)
    spread = 0.0
    for chunk in range(chunks):
        centered = bent[:, pl.ds(chunk * step, step)] - mean
        spread = spread + jnp.sum(centered * centered, axis=-1, keepdims=True)
    scale = lax.rsqrt(spread * (1.0 / wide) + EPSILON)
    st_ref[...] = jnp.broadcast_to(scale, st_ref.shape)
    arrive(2)
    result = mixed + db_ref[...]
    for chunk in range(chunks):
        at = pl.ds(chunk * step, step)
        hidden = ((bent[:, at] - mean) * scale * hg_ref[:, at]).astype(BF16)
        hid_ref[:, at] = hidden
    result = result + nn(hid_ref[...], wd[...])
    out_ref[...] = result.astype(BF16)


def feed(layer, sec, attended, x, pack, wo, wu, wd, tb=512):
    rows, width = x.shape
    wide = wd[0].shape[0]
    tok = lambda n: pl.BlockSpec((tb, n), lambda i: (i, 0))
    S = jax.ShapeDtypeStruct
    return pl.pallas_call(
        functools.partial(feed_kernel, layer),
        grid=(rows // tb,),
        in_specs=[SMEM, tok(width), tok(width), pack_spec(layer, pack)] + [ANY] * 6,
        out_specs=[tok(width), tok(width), tok(wide), tok(wide), tok(128)],
        out_shape=[S((rows, width), BF16), S((rows, width), F32), S((rows, wide), BF16), S((rows, wide), BF16), S((rows, 128), F32)],
        scratch_shapes=[pltpu.VMEM(wo[0].shape, BF16), pltpu.VMEM(wu[0].shape, BF16), pltpu.VMEM(wd[0].shape, BF16), pltpu.VMEM((tb, wide), F32), pltpu.SemaphoreType.DMA((3,))],
        compiler_params=pltpu.CompilerParams(vmem_limit_bytes=VLIM),
        cost_estimate=pl.CostEstimate(flops=2 * rows * width * (2 * wide + width), bytes_accessed=40 * 1024 * 1024, transcendentals=0),
        name="feed_forward",
    )(sec, attended, x, pack, *wo, *wu, *wd)


def feed_back_kernel(layer, sec_ref, c_ref, hid_ref, gp_ref, st_ref, mixed_ref, at_ref,
                     pack_ref, wo0, wo1, wu0, wu1, wd0, wd1,
                     cb_ref, cm_ref, cl_ref, ch_ref, n2_ref, in_ref, wide_ref, thin_ref,
                     wo, wu, wd, sloped, wide_acc, thin_acc, sem):
    now = pl.program_id(0)
    ig_ref, sg_ref, hg_ref = vectors_of(pack_ref, c_ref.shape[-1], INNER_GAIN, SECOND_GAIN, HIDDEN_GAIN)

    @pl.when(now == 0)
    def _():
        wide_acc[...] = jnp.zeros_like(wide_acc)
        thin_acc[...] = jnp.zeros_like(thin_acc)

    arrive = fetch_weights(layer, sec_ref, [(wo0, wo1, wo), (wu0, wu1, wu), (wd0, wd1, wd)], sem)
    low = c_ref[...]
    outer = low.astype(F32)
    thin_acc[0] += fold(outer)
    wide = hg_ref.shape[-1]
    step = 512
    chunks = wide // step

    def fall(chunk):
        return nt(low, wd[pl.ds(chunk * step, step), :])

    arrive(2)
    later = fall(0)
    sum_moved = 0.0
    sum_slope = 0.0
    for chunk in range(chunks):
        slope = later
        if chunk + 1 < chunks:
            later = fall(chunk + 1)
        at = pl.ds(chunk * step, step)
        moved = slope * hid_ref[:, at].astype(F32)
        wide_acc[0, :, at] += fold(moved)
        sum_moved = sum_moved + jnp.sum(moved, axis=-1, keepdims=True)
        slope = slope * hg_ref[:, at]
        sum_slope = sum_slope + jnp.sum(slope, axis=-1, keepdims=True)
        sloped[:, at] = slope
    scale = st_ref[:, 0:1]
    mean_moved = sum_moved * (1.0 / wide)
    mean_slope = sum_slope * (1.0 / wide)
    arrive(1)
    slope_two = 0.0
    for chunk in range(chunks):
        at = pl.ds(chunk * step, step)
        unit = hid_ref[:, at].astype(F32) * (1.0 / hg_ref[:, at])
        slope = (sloped[:, at] - mean_slope - unit * mean_moved) * scale
        before_low = (slope * gp_ref[:, at].astype(F32)).astype(BF16)
        cb_ref[:, at] = before_low
        wide_acc[1, :, at] += fold(before_low.astype(F32))
        slope_two = slope_two + nt(before_low, wu[:, at])
    unit, scale = normalize(mixed_ref[...])
    n2_ref[...] = (unit * sg_ref[...]).astype(BF16)
    thin_acc[1] += fold(slope_two * unit)
    mixed = outer + norm_back(slope_two * sg_ref[...], unit, scale)
    cm_ref[...] = mixed
    mixed_low = mixed.astype(BF16)
    cl_ref[...] = mixed_low
    thin_acc[2] += fold(mixed_low.astype(F32))
    arrive(0)
    slope = nt(mixed_low, wo[...])
    unit, scale = normalize(at_ref[...])
    in_ref[...] = (unit * ig_ref[...]).astype(BF16)
    thin_acc[3] += fold(slope * unit)
    ch_ref[...] = norm_back(slope * ig_ref[...], unit, scale).astype(BF16)

    @pl.when(now == pl.num_programs(0) - 1)
    def _():
        inverse = 1.0 / hg_ref[...]
        wide_ref[0:1, :] = jnp.sum(wide_acc[0], axis=0, keepdims=True) * inverse
        wide_ref[1:2, :] = jnp.sum(wide_acc[1], axis=0, keepdims=True)
        for index in range(4):
            thin_ref[index:index + 1, :] = jnp.sum(thin_acc[index], axis=0, keepdims=True)


def feed_back(layer, sec, c, hidden, gp, st, mixed, attended, pack, wo, wu, wd, tb=256):
    rows, width = c.shape
    wide = wd[0].shape[0]
    const = lambda n, m=1: pl.BlockSpec((m, n), lambda i: (0, 0))
    tok = lambda n: pl.BlockSpec((tb, n), lambda i: (i, 0))
    S = jax.ShapeDtypeStruct
    return pl.pallas_call(
        functools.partial(feed_back_kernel, layer),
        grid=(rows // tb,),
        in_specs=[SMEM, tok(width), tok(wide), tok(wide), tok(128), tok(width), tok(width), pack_spec(layer, pack)] + [ANY] * 6,
        out_specs=[tok(wide), tok(width), tok(width), tok(width), tok(width), tok(width), const(wide, 2), const(width, 4)],
        out_shape=[S((rows, wide), BF16), S((rows, width), F32), S((rows, width), BF16), S((rows, width), BF16), S((rows, width), BF16), S((rows, width), BF16), S((2, wide), F32), S((4, width), F32)],
        scratch_shapes=[pltpu.VMEM(wo[0].shape, BF16), pltpu.VMEM(wu[0].shape, BF16), pltpu.VMEM(wd[0].shape, BF16),
                        pltpu.VMEM((tb, wide), F32), pltpu.VMEM((2, 8, wide), F32), pltpu.VMEM((4, 8, width), F32), pltpu.SemaphoreType.DMA((3,))],
        compiler_params=pltpu.CompilerParams(vmem_limit_bytes=VLIM),
        cost_estimate=pl.CostEstimate(flops=2 * rows * width * (2 * wide + width), bytes_accessed=50 * 1024 * 1024, transcendentals=0),
        name="feed_backward",
    )(sec, c, hidden, gp, st, mixed, attended, pack, *wo, *wu, *wd)


def attend_back_kernel(qb, q_ref, k_ref, v_ref, ch_ref, at_ref, cos_ref, sin_ref, cj_ref, kt, vt, qs, shares_ref, slope_ref):
    rows = q_ref.shape[1]
    lane = lane_iota((rows, 128))
    is_head = lane < HEAD_DIM
    slopes = ch_ref[...].astype(F32)
    product = slopes * at_ref[...]
    incoming = []
    for head in range(2):
        mine = is_head if head == 0 else jnp.logical_not(is_head)
        weighted = jnp.sum(jnp.where(mine, product, 0.0), axis=-1, keepdims=True)
        high, middle, low = split3(-weighted)
        feat = jnp.where(lane == 64, high.astype(F32), jnp.where(lane == 65, middle.astype(F32), jnp.where(lane == 66, low.astype(F32), 0.0)))
        local = slopes if head == 0 else pltpu.roll(slopes, 64, 1)
        incoming.append(jnp.where(is_head, local, feat).astype(BF16))
    blocks = rows // qb
    work = [(head, block) for head in range(2) for block in range(blocks)]
    ready = {}

    def score(index):
        if index < len(work):
            head, block = work[index]
            at = block * qb
            ready[index] = (
                nt(q_ref[head, pl.ds(at, qb), :], k_ref[head]),
                nt(incoming[head][at:at + qb], v_ref[head]),
            )

    score(0)
    for index, (head, block) in enumerate(work):
        score(index + 1)
        scores, turned = ready.pop(index)
        shares = jnp.exp(scores)
        slope = (shares * turned).astype(BF16)
        at = pl.ds(block * qb, qb)
        slope_ref[head, at, :] = slope
        shares_ref[head, at, :] = shares.astype(BF16)
        qs[head, at, :] = nn(slope, k_ref[head])
        if block == blocks - 1:
            rng = pl.ds(head * HEAD_DIM, HEAD_DIM)
            kt[rng, :] = nn(q_ref[head].T[:HEAD_DIM], slope_ref[head])
            vt[rng, :] = nn(incoming[head].T[:HEAD_DIM], shares_ref[head])
    cosine, sine = cos_ref[...], sin_ref[...]
    first = lane % HEAD_DIM < HEAD_DIM // 2

    def back(part):
        turned = jnp.where(first, pltpu.roll(part, 96, 1), pltpu.roll(part, 32, 1))
        return (part * cosine - turned * sine).astype(BF16)

    cj_ref[0] = back(jnp.where(is_head, qs[0], pltpu.roll(qs[1], 64, 1)) * HEAD_DIM ** -0.5)
    cj_ref[1] = back(kt[...].T)
    cj_ref[2] = vt[...].T.astype(BF16)


def attend_back(q, k, v, ch, attended, cosine, sine, begin=0, count=None, into=None, qb=256):
    heads, rows, _ = q.shape
    width = heads * HEAD_DIM
    count = heads // 2 - begin if count is None else count
    hd = pl.BlockSpec((2, rows, 128), lambda i: (i + begin, 0, 0))
    col = pl.BlockSpec((rows, 128), lambda i: (0, i + begin))
    con = pl.BlockSpec((rows, 128), lambda i: (0, 0))
    body = functools.partial(attend_back_kernel, qb)
    extra = () if into is None else (into,)

    def kernel(*refs):
        body(*refs[:7], *refs[7 + len(extra):])

    return pl.pallas_call(
        kernel,
        grid=(count,),
        in_specs=[hd, hd, hd, col, col, con, con] + [ANY] * len(extra),
        out_specs=pl.BlockSpec((3, rows, 128), lambda i: (0, 0, i + begin)),
        out_shape=jax.ShapeDtypeStruct((3, rows, width), BF16),
        input_output_aliases={7: 0} if extra else {},
        scratch_shapes=[pltpu.VMEM((128, rows), F32), pltpu.VMEM((128, rows), F32), pltpu.VMEM((2, rows, 128), F32),
                        pltpu.VMEM((2, rows, rows), BF16), pltpu.VMEM((2, rows, rows), BF16)],
        compiler_params=pltpu.CompilerParams(vmem_limit_bytes=VLIM),
        cost_estimate=pl.CostEstimate(flops=80 * count * rows * rows * HEAD_DIM, bytes_accessed=3 * count * 1024 * 1024, transcendentals=0),
        name="attention_backward",
    )(q, k, v, ch, attended, cosine, sine, *extra)


def qkv_back_kernel(layer, sec_ref, cj_ref, x_ref, cm_ref, pack_ref, own_ref, other_ref,
                    ci_ref, small_ref, w_ref, acc, sem):
    step = pl.program_id(0)
    arrive = fetch_weights(layer, sec_ref, [(own_ref, other_ref, w_ref)], sem)

    @pl.when(step == 0)
    def _():
        acc[...] = jnp.zeros_like(acc)

    width = x_ref.shape[-1]
    (gain_ref,) = vectors_of(pack_ref, width, FIRST_GAIN)
    arrive(0)
    slope = nt(cj_ref[0], w_ref[:, 0:width])
    for which in range(1, 3):
        slope = slope + nt(cj_ref[which], w_ref[:, which * width:(which + 1) * width])
    unit, scale = normalize(x_ref[...].astype(F32))
    acc[0] += fold(slope * unit)
    for which in range(3):
        acc[which + 1] += fold(cj_ref[which].astype(F32))
    ci_ref[...] = (cm_ref[...] + norm_back(slope * gain_ref[...], unit, scale)).astype(BF16)

    @pl.when(step == pl.num_programs(0) - 1)
    def _():
        for index in range(4):
            small_ref[index:index + 1, :] = jnp.sum(acc[index], axis=0, keepdims=True)


def qkv_back(layer, sec, cj, x, cm, pack, own, other, tb=256):
    rows, width = x.shape
    const = lambda n, m=1: pl.BlockSpec((m, n), lambda i: (0, 0))
    tok = lambda n: pl.BlockSpec((tb, n), lambda i: (i, 0))
    S = jax.ShapeDtypeStruct
    return pl.pallas_call(
        functools.partial(qkv_back_kernel, layer),
        grid=(rows // tb,),
        in_specs=[SMEM, pl.BlockSpec((3, tb, width), lambda i: (0, i, 0)), tok(width), tok(width), pack_spec(layer, pack), ANY, ANY],
        out_specs=[tok(width), const(width, 4)],
        out_shape=[S((rows, width), BF16), S((4, width), F32)],
        scratch_shapes=[pltpu.VMEM(own.shape, BF16), pltpu.VMEM((4, 8, width), F32), pltpu.SemaphoreType.DMA((1,))],
        compiler_params=pltpu.CompilerParams(vmem_limit_bytes=VLIM),
        cost_estimate=pl.CostEstimate(flops=2 * rows * width * 3 * width, bytes_accessed=16 * 1024 * 1024, transcendentals=0),
        name="joint_backward",
    )(sec, cj, x, cm, pack, own, other)


def feed_grads_kernel(sec_ref, order_ref, cb_ref, hid_ref, c_ref, n2_ref, cm_ref, in_ref, wide_ref, thin_ref,
                      keep_ref, send_ref, c_t, cm_t):
    step = pl.program_id(0)
    sec = sec_ref[0]
    parts = order_ref.shape[0] // 2
    half = n2_ref.shape[-1] // 2
    up_rows = cb_ref.shape[-1] // 2
    thin = c_ref.shape[-1] // parts
    steps = pl.num_programs(0) // 2
    outs = (keep_ref, send_ref)
    sides = [pl.ds(pl.multiple_of(which * half, 128), half) for which in (sec, 1 - sec)]

    @pl.when(step == 0)
    def _():
        c_t[...] = c_ref[...].T
        cm_t[...] = cm_ref[...].T
        for window in range(parts // 2):
            at = pl.ds(window * half, half)
            far = pl.ds(window // (parts // 4) * half, half)
            rows = jnp.concatenate([wide_ref[:, at], thin_ref[:, far], jnp.zeros((10, half), F32)], axis=0).astype(BF16)
            for side in range(2):
                for sub in range(2):
                    outs[side][order_ref[side * parts + window * 2 + sub], up_rows * 2 + thin:, :] = rows

    for side in range(2):
        up = tn(cb_ref[...], n2_ref[:, sides[side]]).astype(BF16)
        for sub in range(2):
            at = order_ref[side * parts + step * 2 + sub]
            outs[side][at, 0:up_rows, :] = up[sub * up_rows:(sub + 1) * up_rows]

    down = nn(c_t[...], hid_ref[...]).astype(BF16)
    rows = pl.ds(pl.multiple_of(up_rows + thin * (step % steps), 16), thin)
    for side in range(2):
        @pl.when(step // steps == side)
        def _():
            for part in range(parts):
                outs[side][order_ref[side * parts + part], rows, :] = down[thin * part:thin * (part + 1)]

        @pl.when(step == side * steps)
        def _():
            out = nn(cm_t[...], in_ref[:, sides[side]]).astype(BF16)
            for part in range(parts):
                outs[side][order_ref[side * parts + part], 2 * up_rows:2 * up_rows + thin, :] = out[thin * part:thin * (part + 1)]


def feed_grads(sec, order, cb, hidden, c, n2, cm, inner, wide_sums, thin_sums):
    rows, width = c.shape
    wide = cb.shape[-1]
    parts = order.shape[0] // 2
    half = width // 2
    steps = wide // half
    up_rows = wide // parts
    total = 2 * up_rows + width // parts + 16
    full = lambda n, m=rows: pl.BlockSpec((m, n), lambda i, s, o: (0, 0))
    out_spec = pl.BlockSpec((parts, total, half), lambda i, s, o: (0, 0, 0))
    out_shape = jax.ShapeDtypeStruct((parts, total, half), BF16)
    return pl.pallas_call(
        feed_grads_kernel,
        grid_spec=pltpu.PrefetchScalarGridSpec(
            num_scalar_prefetch=2,
            grid=(steps,),
            in_specs=[
                pl.BlockSpec((rows, half), lambda i, s, o: (0, i)),
                pl.BlockSpec((rows, half), lambda i, s, o: (0, jnp.where(i < steps // 2, s[0], 1 - s[0]) * (steps // 2) + i % (steps // 2))),
                full(width), full(width), full(width), full(width), full(wide, 2), full(width, 4),
            ],
            out_specs=[out_spec, out_spec],
            scratch_shapes=[pltpu.VMEM((width, rows), BF16), pltpu.VMEM((width, rows), BF16)],
        ),
        out_shape=[out_shape, out_shape],
        compiler_params=pltpu.CompilerParams(vmem_limit_bytes=VLIM),
        cost_estimate=pl.CostEstimate(flops=2 * rows * width * (2 * wide + width), bytes_accessed=30 * 1024 * 1024, transcendentals=0),
        name="feed_gradients",
    )(sec, order, cb, hidden, c, n2, cm, inner, wide_sums, thin_sums)


def joint_grads_kernel(sec_ref, order_ref, cj_ref, n_ref, sums_ref, keep_ref, send_ref):
    step = pl.program_id(0)
    sec = sec_ref[0]
    parts = order_ref.shape[0] // 2
    width = n_ref.shape[-1]
    half = width // 2
    thick = 3 * width // parts
    outs = (keep_ref, send_ref)
    for side, which in enumerate((sec, 1 - sec)):
        sums = tn(cj_ref[0], n_ref[:, pl.ds(pl.multiple_of(which * half, 128), half)]).astype(BF16)
        for block in range(3):
            @pl.when(step == block)
            def _():
                for part in range(parts):
                    low, high = max(thick * part, width * block), min(thick * (part + 1), width * (block + 1))
                    if low < high:
                        at = order_ref[side * parts + part]
                        outs[side][at, low - thick * part:high - thick * part, :] = sums[low - width * block:high - width * block]

    @pl.when(step == 0)
    def _():
        for part in range(parts):
            window = thick * part // half
            rows = [sums_ref[1 + w // 2:2 + w // 2, w % 2 * half:w % 2 * half + half] for w in (window, min(window + 1, 5))]
            far = part // (parts // 2) * half
            rows = jnp.concatenate(rows + [sums_ref[0:1, far:far + half], jnp.zeros((13, half), F32)], axis=0).astype(BF16)
            for side in range(2):
                outs[side][order_ref[side * parts + part], thick:, :] = rows


def joint_grads(sec, order, cj, normed, sums):
    rows, width = normed.shape
    parts = order.shape[0] // 2
    half = width // 2
    thick = 3 * width // parts
    out_spec = pl.BlockSpec((parts, thick + 16, half), lambda i, s, o: (0, 0, 0))
    out_shape = jax.ShapeDtypeStruct((parts, thick + 16, half), BF16)
    return pl.pallas_call(
        joint_grads_kernel,
        grid_spec=pltpu.PrefetchScalarGridSpec(
            num_scalar_prefetch=2,
            grid=(3,),
            in_specs=[
                pl.BlockSpec((1, rows, width), lambda i, s, o: (i, 0, 0)),
                pl.BlockSpec((rows, width), lambda i, s, o: (0, 0)),
                pl.BlockSpec((4, width), lambda i, s, o: (0, 0)),
            ],
            out_specs=[out_spec, out_spec],
        ),
        out_shape=[out_shape, out_shape],
        compiler_params=pltpu.CompilerParams(vmem_limit_bytes=VLIM),
        cost_estimate=pl.CostEstimate(flops=6 * rows * width * width, bytes_accessed=14 * 1024 * 1024, transcendentals=0),
        name="joint_gradients",
    )(sec, order, cj, normed, sums)


def prepare_kernel(lengths, mine_ref, part_ref, seg_ref, rate_ref, *refs):
    vectors, (cos_ref, sin_ref, lab_ref, pack_ref) = refs[:len(lengths)], refs[len(lengths):]
    begin = 0
    for vector, length in zip(vectors, lengths):
        pack_ref[:, begin:begin + length] = vector[...]
        begin += length
    rows = seg_ref.shape[-1]
    piece = rows // 2
    second = jnp.full((1, 1), part_ref[0]) == 1
    row = seg_ref[0].astype(F32)
    turned = jnp.where(second, jnp.concatenate([row[:, piece:], row[:, :piece]], axis=1), row)
    labels = jnp.broadcast_to(turned, (128, rows)).T
    starts = jnp.zeros_like(labels)
    for document in range(1, 5):
        count = jnp.sum(jnp.where(row < document, 1.0, 0.0), axis=1, keepdims=True)
        starts = jnp.where(labels == document, count, starts)
    time = lax.broadcasted_iota(jnp.int32, labels.shape, 0).astype(F32)
    shift = jnp.where(second, jnp.where(time < piece, piece * 1.0, -piece * 1.0), 0.0)
    angle = (time + shift - starts) * rate_ref[...]
    lane = lane_iota(labels.shape)
    cos_ref[...] = jnp.cos(angle)
    sin_ref[...] = jnp.sin(angle) * jnp.where(lane % HEAD_DIM < HEAD_DIM // 2, -1.0, 1.0)
    lab_ref[...] = labels.astype(jnp.int32)


def prepare(mine, part, segments, vectors):
    rows = segments.shape[-1]
    lengths = tuple(vector.shape[-1] for vector in vectors)
    half = HEAD_DIM // 2
    rate = jnp.tile(1.0 / 10000.0 ** (jnp.arange(half, dtype=F32) * 2.0 / HEAD_DIM), 4)[None]
    whole = lambda m, n: pl.BlockSpec((m, n), lambda i, a, b: (0, 0))
    return pl.pallas_call(
        functools.partial(prepare_kernel, lengths),
        grid_spec=pltpu.PrefetchScalarGridSpec(
            num_scalar_prefetch=2,
            grid=(1,),
            in_specs=[pl.BlockSpec((1, 1, rows), lambda i, a, b: (a[0], 0, 0)), whole(1, 128)] + [whole(1, length) for length in lengths],
            out_specs=[whole(rows, 128), whole(rows, 128), whole(rows, 128), whole(1, sum(lengths))],
        ),
        out_shape=[jax.ShapeDtypeStruct((rows, 128), F32)] * 2 + [jax.ShapeDtypeStruct((rows, 128), jnp.int32), jax.ShapeDtypeStruct((1, sum(lengths)), F32)],
        compiler_params=pltpu.CompilerParams(vmem_limit_bytes=VLIM),
        name="row_tables",
    )(mine.reshape(1).astype(jnp.int32), part.reshape(1).astype(jnp.int32), segments, rate, *vectors)


def swap_pairs(change, sizes):
    sections, dps, seqs = sizes
    pairs = []
    for section in range(sections):
        for dp in range(dps):
            for seq in range(seqs):
                a, b, c = change(section, dp, seq)
                pairs.append(((section * dps + dp) * seqs + seq, (a * dps + b) * seqs + c))
    return pairs


FEED, JOINT = range(2)


class Reduction:
    def __init__(self, kept, sent, sizes):
        self.sizes = sizes
        self.kept, self.sent = kept, sent
        self.stage = 0
        self.result = None

    def send(self):
        if self.stage == 0:
            self.arrived = lax.ppermute(self.sent, "section", [(0, 1), (1, 0)])
        else:
            moves = (
                lambda s, d, q: (s, d ^ 1, q) if s == 0 else (s, d, q ^ 1),
                lambda s, d, q: (s, d, q ^ 1) if s == 0 else (s, d ^ 1, q),
                lambda s, d, q: (s, d ^ 2, q),
                lambda s, d, q: (s, d ^ 4, q),
            )
            self.arrived = lax.ppermute(self.sent, ("section", "dp", "seq"), swap_pairs(moves[self.stage - 1], self.sizes))
        self.stage += 1

    def add(self):
        kept, arrived = self.kept, self.arrived
        middle = kept.shape[0] // 2
        if middle == 0:
            self.result = kept[0].astype(F32) + arrived[0].astype(F32)
            return
        self.sent = (kept[middle:].astype(F32) + arrived[middle:].astype(F32)).astype(BF16)
        self.kept = (kept[:middle].astype(F32) + arrived[:middle].astype(F32)).astype(BF16)

    def finish(self):
        if self.result is not None:
            return self.result
        while self.stage < 5:
            self.add()
            self.send()
        self.add()
        return self.result


def advance(value, *moving):
    for item in moving:
        if item.stage:
            item.add()
    if all(item.stage == 5 for item in moving):
        results = [item.result for item in moving]
        value, results = lax.optimization_barrier((value, results))
        for item, result in zip(moving, results):
            item.result = result
        return value
    parts = [array for item in moving for array in (item.kept, item.sent)]
    value, parts = lax.optimization_barrier((value, parts))
    for index, item in enumerate(moving):
        item.kept, item.sent = parts[2 * index:2 * index + 2]
        item.send()
    return value


def last_kernel(cj_ref, n_ref, x_ref, cm_ref, pack_ref, own_ref, other_ref, feed_keep, feed_send, done_ref,
                out_ref, mine_ref, got_ref,
                w_ref, back, cj_t, acc, j_keep, j_send, r0, r1, r2, r3, r4, k1, k2, k3, k4, s1, s2, s3, s4,
                f1, f2, f3, fk2, fk3, fs2, fs3, swap_out, landed, send_sem, recv_sem, local_sem):
    s, d, q = (lax.axis_index(name) for name in ("section", "dp", "seq"))
    x = (s, d + 1 - 2 * (d % 2), q)
    y = (s, d, 1 - q)
    first = (s, (1 - s) * x[1] + s * d, (1 - s) * q + s * y[2])
    second = (s, s * x[1] + (1 - s) * d, s * q + (1 - s) * y[2])
    near = (s, d + 2 - 4 * (d // 2 % 2), q)
    far = (s, d + 4 - 8 * (d // 4), q)
    core = (1 - s, d, q)
    parts, thick, half = j_keep.shape
    thick -= 16
    width = n_ref.shape[-1]
    piece = got_ref.shape[1]

    @pl.when(s == 0)
    def _():
        pltpu.make_async_copy(own_ref, w_ref, local_sem).start()

    @pl.when(s == 1)
    def _():
        pltpu.make_async_copy(other_ref, w_ref, local_sem).start()

    barrier = pltpu.get_barrier_semaphore()
    across = (1 - s, d, 1 - q)
    for other in (core, x, y, near, far, across):
        pl.semaphore_signal(barrier, inc=1, device_id=other, device_id_type=pl.DeviceIdType.MESH)
    pl.semaphore_wait(barrier, 6)

    def ready(number, source, target, other):
        return pltpu.make_async_remote_copy(
            src_ref=source, dst_ref=target, send_sem=send_sem.at[number], recv_sem=recv_sem.at[number],
            device_id=other, device_id_type=pl.DeviceIdType.MESH)

    def send(number, source, target, other):
        copy = ready(number, source, target, other)
        copy.start()
        return copy

    def total(one, two):
        return one.astype(F32) + two.astype(F32)

    feed_rows = feed_keep.shape[1]
    feed_blocks = [pl.ds(number * (feed_rows // 2), feed_rows // 2) for number in range(2)]
    feed_flights = [send(number, feed_send.at[:, at], f1.at[:, at], second) for number, at in enumerate(feed_blocks)]
    (gain_ref,) = vectors_of(pack_ref, width, FIRST_GAIN)
    acc[...] = jnp.zeros_like(acc)
    tb = piece // 2
    rows = x_ref.shape[0]
    order = [2, 3, 0, 1]

    def slope_of(block):
        at = pl.ds(block * tb, tb)
        slope = nt(cj_ref[0, at], w_ref[:, 0:width])
        for which in range(1, 3):
            slope = slope + nt(cj_ref[which, at], w_ref[:, which * width:(which + 1) * width])
        return slope

    pltpu.make_async_copy(own_ref, w_ref, local_sem).wait()
    to_y = ready(16, back.at[pl.ds(piece, piece)], got_ref.at[0], (0, d, 1 - q))
    to_core = ready(17, back.at[pl.ds(0, piece)], got_ref.at[1], (0, d, q))
    to_across = ready(18, back.at[pl.ds(piece, piece)], got_ref.at[2], (0, d, 1 - q))
    later = slope_of(order[0])
    for number, block in enumerate(order):
        slope = later
        if number + 1 < len(order):
            later = slope_of(order[number + 1])
        at = pl.ds(block * tb, tb)
        unit, scale = normalize(x_ref[at, :].astype(F32))
        acc[0] += fold(slope * unit)
        for which in range(3):
            acc[which + 1] += fold(cj_ref[which, at].astype(F32))
        back[at, :] = (cm_ref[at, :] + norm_back(slope * gain_ref[...], unit, scale)).astype(BF16)
        if number == 1:
            @pl.when(s == 0)
            def _():
                to_y.start()
    mine_ref[...] = back[0:piece, :]

    sums = [jnp.sum(acc[number], axis=0, keepdims=True) for number in range(4)]
    for which in range(3):
        cj_t[which] = cj_ref[which].T

    def position(part, owner):
        bx, by = (part // 2 % 2 + d % 2) % 2, (part % 2 + q) % 2
        bz, cz = (part // 4 + d // 2) % 2, (part // 8 + d // 4) % 2
        depth = bz * 2 + cz
        return (1 - owner) * ((bx * 2 + by) * 4 + depth) + owner * ((by * 2 + bx) * 4 + depth)

    def gradients(target, owner):
        for block in range(3):
            found = nn(cj_t[block], n_ref[:, pl.ds(pl.multiple_of(owner * half, 128), half)]).astype(BF16)
            for part in range(parts):
                low, high = max(thick * part, width * block), min(thick * (part + 1), width * (block + 1))
                if low < high:
                    target[position(part, owner), low - thick * part:high - thick * part, :] = found[low - width * block:high - width * block]
        for part in range(parts):
            window = thick * part // half
            lines = [sums[1 + w // 2][:, w % 2 * half:w % 2 * half + half] for w in (window, min(window + 1, 5))]
            away = part // (parts // 2) * half
            lines = jnp.concatenate(lines + [sums[0][:, away:away + half], jnp.zeros((13, half), F32)], axis=0)
            target[position(part, owner), thick:, :] = lines.astype(BF16)

    gradients(j_send, 1 - s)
    blocks = [pl.ds(number * (thick + 16) // 2, (thick + 16) // 2) for number in range(2)]
    flights = [send(2 + number, j_send.at[:, at], r0.at[:, at], core) for number, at in enumerate(blocks)]
    for number, at in enumerate(feed_blocks):
        feed_flights[number].wait()
        fs2[:, at] = total(feed_keep[2:, at], f1[2:, at]).astype(BF16)
        feed_flights[number] = send(4 + number, fs2.at[:, at], f2.at[:, at], near)
        fk2[:, at] = total(feed_keep[:2, at], f1[:2, at]).astype(BF16)
    gradients(j_keep, s)
    kept, arrived = j_keep, r0
    for stage, (sent, held, target, other) in enumerate(
        ((s1, k1, r1, first), (s2, k2, r2, second), (s3, k3, r3, near), (s4, k4, r4, far))):
        middle = kept.shape[0] // 2
        for number, at in enumerate(blocks):
            flights[number].wait()
            sent[:, at] = total(kept[middle:, at], arrived[middle:, at]).astype(BF16)
            flights[number] = send(8 + 2 * stage + number, sent.at[:, at], target.at[:, at], other)
            held[:, at] = total(kept[:middle, at], arrived[:middle, at]).astype(BF16)
        kept, arrived = held, target
        if stage == 0:
            for number, at in enumerate(feed_blocks):
                feed_flights[number].wait()
                fs3[:, at] = total(fk2[1:, at], f2[1:, at]).astype(BF16)
                feed_flights[number] = send(6 + number, fs3.at[:, at], f3.at[:, at], far)
                fk3[:, at] = total(fk2[:1, at], f2[:1, at])
        if stage == 1:
            @pl.when(s == 1)
            def _():
                to_core.start()
                to_across.start()
    own = jnp.full((1, 1), s) == 0

    def settle(at, mine):
        done = done_ref[at, :]
        swap_out[at, :] = jnp.where(own, done, mine)
        out_ref[pl.ds(s, 1), at, :] = jnp.where(own, mine, done)[None]

    for number, at in enumerate(feed_blocks):
        feed_flights[number].wait()
        settle(at, fk3[0, at] + f3[0, at].astype(F32))
    for number, at in enumerate(blocks):
        flights[number].wait()
        settle(pl.ds(feed_rows + number * (thick + 16) // 2, (thick + 16) // 2), total(kept[0, at], arrived[0, at]))
    send(19, swap_out, landed, core).wait()
    out_ref[pl.ds(1 - s, 1)] = landed[...][None]

    @pl.when(s == 0)
    def _():
        to_y.wait_send()
        for copy in (to_y, to_core, to_across):
            copy.wait_recv()

    @pl.when(s == 1)
    def _():
        to_core.wait_send()
        to_across.wait_send()


def last_step(cj, normed, state, cm, pack, own, other, feed_keep, feed_send, done, parts):
    rows, width = state.shape
    half, piece = width // 2, rows // 2
    thick = 3 * width // parts + 16
    feed_rows = feed_keep.shape[1]
    vm = pl.BlockSpec(memory_space=pltpu.VMEM)
    level = lambda n, m=thick, t=BF16: pltpu.VMEM((n, m, half), t)
    steps = [parts >> number for number in range(1, 5)]
    S = jax.ShapeDtypeStruct
    return pl.pallas_call(
        last_kernel,
        in_specs=[vm] * 5 + [ANY] * 2 + [vm] * 3,
        out_specs=[vm] * 3,
        out_shape=[S((2, feed_rows + thick, half), F32), S((piece, width), BF16), S((3, piece, width), BF16)],
        scratch_shapes=[pltpu.VMEM(own.shape, BF16), pltpu.VMEM((rows, width), BF16), pltpu.VMEM((3, width, rows), BF16),
                        pltpu.VMEM((4, 8, width), F32)]
        + [level(parts)] * 3 + [level(n) for n in steps] * 3
        + [level(4, feed_rows), level(2, feed_rows), level(1, feed_rows), level(2, feed_rows), level(1, feed_rows, F32),
           level(2, feed_rows), level(1, feed_rows)]
        + [pltpu.VMEM((feed_rows + thick, half), F32)] * 2
        + [pltpu.SemaphoreType.DMA((20,)), pltpu.SemaphoreType.DMA((20,)), pltpu.SemaphoreType.DMA],
        compiler_params=pltpu.CompilerParams(collective_id=0, has_side_effects=True, vmem_limit_bytes=VLIM),
        cost_estimate=pl.CostEstimate(flops=0, bytes_accessed=100 * 1024 * 1024, transcendentals=0),
        name="last_step",
    )(cj, normed, state, cm, pack, own, other, feed_keep, feed_send, done)


def assemble_kernel(parts, index_ref, both_ref, joint_ref, jb_ref, out_ref, ob_ref, up_ref, ub_ref, down_ref, db_ref,
                    fg_ref, ig_ref, sg_ref, hg_ref):
    half = both_ref.shape[-1]
    index = index_ref[0]
    up_rows, thin, thick = up_ref.shape[0], out_ref.shape[0], joint_ref.shape[0]
    steps = up_rows // thin
    for side in range(2):
        at = pl.ds(side * half, half)
        up_ref[:, at] = both_ref[side, 0:up_rows, :]
        for step in range(steps):
            begin = up_rows + step * thin
            down_ref[:, pl.ds((side * steps + step) * half, half)] = both_ref[side, begin:begin + thin, :]
        begin = 2 * up_rows
        out_ref[:, at] = both_ref[side, begin:begin + thin, :]
        begin = 2 * up_rows + thin + 16
        joint_ref[:, at] = both_ref[side, begin:begin + thick, :]

    def cut(row, count, target):
        begin = index * count % half
        best = row[:, 0:count]
        for number in range(1, half // count):
            best = jnp.where(jnp.full((1, 1), begin) == number * count, row[:, number * count:(number + 1) * count], best)
        target[...] = best

    at = 2 * up_rows + thin
    for number, (target, count) in enumerate(((hg_ref, up_rows), (ub_ref, up_rows), (db_ref, thin), (sg_ref, thin), (ob_ref, thin), (ig_ref, thin))):
        cut(both_ref[0, at + number:at + number + 1, :], count, target)
    at += 16 + thick
    cut(both_ref[0, at + 2:at + 3, :], thin, fg_ref)
    line = jnp.concatenate([both_ref[0, at:at + 1, :], both_ref[0, at + 1:at + 2, :]], axis=1)
    best = line[:, 0:thick]
    for part in range(1, parts):
        begin = part * thick % half
        best = jnp.where(jnp.full((1, 1), index) == part, line[:, begin:begin + thick], best)
    jb_ref[...] = best


def assemble(index, both, parts, width):
    wide = 4 * width
    S = lambda *shape: jax.ShapeDtypeStruct(shape, F32)
    vm = pl.BlockSpec(memory_space=pltpu.VMEM)
    thin, up_rows, thick = width // parts, wide // parts, 3 * width // parts
    results = pl.pallas_call(
        functools.partial(assemble_kernel, parts),
        in_specs=[SMEM, vm],
        out_specs=[vm] * 12,
        out_shape=[S(thick, width), S(1, thick), S(thin, width), S(1, thin), S(up_rows, width), S(1, up_rows),
                   S(thin, wide), S(1, thin), S(1, thin), S(1, thin), S(1, thin), S(1, up_rows)],
        compiler_params=pltpu.CompilerParams(vmem_limit_bytes=VLIM),
        name="gradient_outputs",
    )(index.reshape(1).astype(jnp.int32), both)
    return tuple(item.T[None] if number in (0, 2, 4, 6) else item for number, item in enumerate(results))


def row_step(
    sizes,
    tokens,
    segments,
    cotangent,
    joint_weight,
    joint_bias,
    output_weight,
    output_bias,
    up_weight,
    up_bias,
    down_weight,
    down_bias,
    first_gain,
    inner_gain,
    second_gain,
    hidden_gain,
):
    micro, row_count, piece, width = tokens.shape
    rows = 2 * piece
    wide = up_weight.shape[-1]
    parts = sizes[1] * sizes[2]
    half = width // 2
    section = lax.axis_index("section")
    part = lax.axis_index("seq")
    data = lax.axis_index("dp")
    sec = section.reshape(1).astype(jnp.int32)
    mine = 2 * section + part
    swap = [(0, 1), (1, 0)]

    def pick(array, index):
        return lax.dynamic_index_in_dim(array, index, 0, keepdims=False)

    flat_tokens = tokens.reshape(micro * row_count, piece, width)
    beside = lax.ppermute(pick(flat_tokens, mine ^ 1), "seq", swap)
    both = [(own[0], lax.ppermute(own[0], "section", swap)) for own in (joint_weight, output_weight, up_weight, down_weight)]
    joint_pair, output_pair, up_pair, down_pair = both
    cosine, sine, labels, own = prepare(mine, part, segments.reshape(micro * row_count, 1, rows), (
        joint_bias, output_bias, up_bias, down_bias, first_gain, inner_gain, second_gain, hidden_gain))
    other = lax.ppermute(own, "section", swap)
    pack = jnp.where(section == 0, jnp.stack([own, other]), jnp.stack([other, own]))

    mx, my, mz = data % 2, part, data // 2
    index = jnp.arange(parts, dtype=jnp.int32)
    cx, cy, cz = (index // 2) % 2 ^ mx, index % 2 ^ my, index // 4 ^ mz
    depth = cz % 2 * 2 + cz // 2
    order_x, order_y = (cx * 2 + cy) * 4 + depth, (cy * 2 + cx) * 4 + depth
    order = jnp.where(section == 0, jnp.concatenate([order_x, order_y]), jnp.concatenate([order_y, order_x]))

    kept = []
    hiddens = []
    for layer in range(2):
        if layer == 0:
            state, normed, q, k, v = qkv(layer, sec, (flat_tokens, beside), pack, *joint_pair, cosine, sine, labels, mine)
            state, cotangent = lax.optimization_barrier((state, cotangent))
            flat = cotangent.reshape(micro * row_count, piece, width)
            slope = jnp.concatenate([pick(flat, mine), lax.ppermute(pick(flat, mine ^ 1), "seq", swap)], axis=0)
        else:
            _, normed, q, k, v = qkv(layer, sec, state, pack, *joint_pair, cosine, sine, labels, mine)
        attended, query = attend(q, k, v)
        result, mixed, hidden, bend, stats = feed(layer, sec, attended, state, pack, output_pair, up_pair, down_pair)
        kept.append((state, normed, query, k, v, attended, mixed, hidden, bend, stats))
        hiddens.append(result)
        state = result

    def halves(item):
        return item[:piece], item[piece:]

    every = ("section", "seq")
    blocks = []
    for fs, fq in ((0, 1), (1, 0), (1, 1)):
        first, second = (halves(item)[fq] for item in hiddens)
        owed = jnp.where(section == fs, first, second)
        blocks.append((owed, [(2 * s + q, 2 * (s ^ fs) + (q ^ fq)) for s in range(2) for q in range(2)]))
    slope, owed = lax.optimization_barrier((slope, [block for block, pairs in blocks]))
    gathered = [lax.ppermute(block, every, pairs) for block, (_, pairs) in zip(owed, blocks)]
    own = jnp.where(section == 0, halves(hiddens[0])[0], halves(hiddens[1])[0])

    def place(blocks):
        stacked = jnp.stack(blocks)
        return jnp.stack([pick(stacked, mine ^ index) for index in range(4)]).reshape(1, micro, row_count, piece, width)

    def deliver(layer, back):
        own, other = halves(back)
        moves = (
            (other, [(2 * layer + q, 2 * layer + (q ^ 1)) for q in range(2)]),
            (own, [(2 * (1 - layer) + q, 2 * layer + q) for q in range(2)]),
            (other, [(2 * (1 - layer) + q, 2 * layer + (q ^ 1)) for q in range(2)]),
        )
        return [own] + [lax.ppermute(block, every, pairs) for block, pairs in moves]

    flights = {}
    delivered = [None, None]

    for layer in (1, 0):
        state, normed, query, k, v, attended, mixed, hidden, bend, stats = kept[layer]
        cb, cm, cm_low, ch, n2, inner, wide_sums, thin_sums = feed_back(
            layer, sec, slope, hidden, bend, stats, mixed, attended, pack, output_pair, up_pair, down_pair)
        if layer == 0:
            cb = advance(cb, flights[FEED, 1], flights[JOINT, 1])
        flights[FEED, layer] = Reduction(*feed_grads(sec, order, cb, hidden, slope, n2, cm_low, inner, wide_sums, thin_sums), sizes)
        if layer == 1:
            ch = advance(ch, flights[FEED, 1])
            cj = attend_back(query, k, v, ch, attended, cosine, sine)
            cj, gathered = lax.optimization_barrier((cj, gathered))
            cj = advance(cj, flights[FEED, 1])
        else:
            ch, delivered[1] = lax.optimization_barrier((ch, delivered[1]))
            ch = advance(ch, flights[FEED, 0], flights[FEED, 1], flights[JOINT, 1])
            count = query.shape[0] // 4
            cj = attend_back(query, k, v, ch, attended, cosine, sine, 0, count)
            cj = advance(cj, flights[FEED, 0], flights[FEED, 1], flights[JOINT, 1])
            cj = attend_back(query, k, v, ch, attended, cosine, sine, count, None, cj)
            cj = advance(cj, flights[FEED, 1])
            flights[JOINT, 1].add()
            flights[JOINT, 1].send()
            flights[FEED, 0].add()
        if layer == 0:
            break
        back, sums = qkv_back(layer, sec, cj, state, cm, pack, *joint_pair)
        delivered[layer] = deliver(layer, back)
        flights[JOINT, layer] = Reduction(*joint_grads(sec, order, cj, normed, sums), sizes)
        if layer == 1:
            back = advance(back, flights[JOINT, 1])
        slope = back
    before = flights[FEED, 0]
    done = jnp.concatenate([flights[FEED, 1].finish(), flights[JOINT, 1].finish()], axis=0)
    both, ours, got = last_step(cj, normed, state, cm, pack, *joint_pair, before.kept, before.sent, done, parts)
    hiddens = place([own] + gathered)
    input_gradients = place([jnp.where(section == 0, a, b) for a, b in zip((ours, got[0], got[1], got[2]), delivered[1])]).astype(F32)

    return (hiddens, input_gradients) + tuple(assemble(2 * data + part, both, parts, width))


def choose(sizes, *arrays):
    micro, row_count, piece, width = arrays[0].shape
    if sizes == (2, 8, 2) and micro * row_count == 4:
        return row_step(sizes, *arrays)
    return shards(*arrays)


def solution(mesh):
    axes = ("section", "dp", "seq")
    return jax.shard_map(
        functools.partial(choose, tuple(mesh.shape[name] for name in axes)),
        mesh=mesh,
        in_specs=(
            P(None, "dp", "seq", None),
            P(None, "dp", None),
            P(None, "dp", "seq", None),
            P("section", None, None),
            P("section", None),
            P("section", None, None),
            P("section", None),
            P("section", None, None),
            P("section", None),
            P("section", None, None),
            P("section", None),
            P("section", None),
            P("section", None),
            P("section", None),
            P("section", None),
        ),
        out_specs=(
            P("section", None, "dp", "seq", None),
            P("section", None, "dp", "seq", None),
            P("section", None, ("dp", "seq")),
            P("section", ("dp", "seq")),
            P("section", None, ("dp", "seq")),
            P("section", ("dp", "seq")),
            P("section", None, ("dp", "seq")),
            P("section", ("dp", "seq")),
            P("section", None, ("dp", "seq")),
            P("section", ("dp", "seq")),
            P("section", ("dp", "seq")),
            P("section", ("dp", "seq")),
            P("section", ("dp", "seq")),
            P("section", ("dp", "seq")),
        ),
        check_vma=False,
    )
```

```python
import functools
import math

import jax
import jax.numpy as jnp
from jax import lax
from jax.experimental import pallas as pl
from jax.experimental.pallas import tpu as pltpu
from jax.sharding import PartitionSpec as P

HEAD_DIM = 64


EPSILON = 1e-05
MASKED = -1e30


def passed_along(value, axis, by):
    devices = lax.axis_size(axis)
    pairs = [(i, i + by) for i in range(devices) if 0 <= i + by < devices]
    return lax.ppermute(value, axis, pairs)


def layer_norm(value, gain):
    centered = value - jnp.mean(value, axis=-1, keepdims=True)
    spread = jnp.mean(centered * centered, axis=-1, keepdims=True)
    return centered * lax.rsqrt(spread + EPSILON) * gain


def feed_norm(before, gain):
    return layer_norm(jax.nn.gelu(before, approximate=False), gain)


def rotate(value, cosine, sine):
    middle = value.shape[-1] // 2
    first, second = (value[..., :middle], value[..., middle:])
    return jnp.concatenate(
        [first * cosine - second * sine, second * cosine + first * sine], axis=-1
    )


def rotate_back(incoming, cosine, sine):
    middle = incoming.shape[-1] // 2
    first, second = (incoming[..., :middle], incoming[..., middle:])
    return jnp.concatenate(
        [first * cosine + second * sine, second * cosine - first * sine], axis=-1
    )


def layer_forward(state, labels, weights, part):
    (
        joint_weight,
        joint_bias,
        output_weight,
        output_bias,
        up_weight,
        up_bias,
        down_weight,
        down_bias,
        first_gain,
        inner_gain,
        second_gain,
        hidden_gain,
    ) = weights
    row_count, piece_len, model_width = state.shape
    head_count = model_width // HEAD_DIM
    shape_heads = (row_count, piece_len, head_count, HEAD_DIM)
    offset = part * piece_len
    local_labels = lax.dynamic_slice_in_dim(labels, offset, piece_len, 1)
    starts = jnp.sum((labels[:, None, :] < local_labels[:, :, None]).astype(jnp.int32), axis=-1)
    places = offset + jnp.arange(piece_len, dtype=jnp.int32)[None, :] - starts
    inverse_rate = 1.0 / 10000.0 ** (jnp.arange(HEAD_DIM // 2, dtype=jnp.float32) * 2.0 / HEAD_DIM)
    angle = places.astype(jnp.float32)[:, :, None, None] * inverse_rate
    cosine = jnp.cos(angle)
    sine = jnp.sin(angle)
    normed = layer_norm(state, first_gain).astype(jnp.bfloat16)
    joint = jnp.dot(normed, joint_weight, preferred_element_type=jnp.float32) + joint_bias
    query = rotate(joint[..., :model_width].reshape(shape_heads), cosine, sine).astype(jnp.bfloat16)
    key = rotate(
        joint[..., model_width : 2 * model_width].reshape(shape_heads), cosine, sine
    ).astype(jnp.bfloat16)
    value = joint[..., 2 * model_width :].reshape(shape_heads).astype(jnp.bfloat16)
    keys_all, values_all = (
        lax.all_gather(key, "seq", axis=1, tiled=True),
        lax.all_gather(value, "seq", axis=1, tiled=True),
    )
    match = local_labels[:, None, :, None] == labels[:, None, None, :]
    scores = jnp.einsum(
        "rqhd,rkhd->rhqk", query, keys_all, preferred_element_type=jnp.float32
    ) * HEAD_DIM ** (-0.5)
    scores = jnp.where(match, scores, MASKED)
    peak = jnp.max(scores, axis=-1, keepdims=True)
    raised = jnp.exp(scores - peak)
    total_raised = jnp.sum(raised, axis=-1, keepdims=True)
    shares = raised / total_raised
    log_total = peak + jnp.log(total_raised)
    attended = jnp.einsum(
        "rhqk,rkhd->rqhd",
        shares.astype(jnp.bfloat16),
        values_all,
        preferred_element_type=jnp.float32,
    ).reshape(row_count, piece_len, model_width)
    inner = layer_norm(attended, inner_gain).astype(jnp.bfloat16)
    mixed = state + jnp.dot(inner, output_weight, preferred_element_type=jnp.float32) + output_bias
    normed_two = layer_norm(mixed, second_gain).astype(jnp.bfloat16)
    before = jnp.dot(normed_two, up_weight, preferred_element_type=jnp.float32) + up_bias
    hidden = feed_norm(before, hidden_gain).astype(jnp.bfloat16)
    result = mixed + jnp.dot(hidden, down_weight, preferred_element_type=jnp.float32) + down_bias
    kept = (
        state,
        normed,
        query,
        keys_all,
        values_all,
        cosine,
        sine,
        match,
        shares,
        attended,
        inner,
        mixed,
        normed_two,
        before,
        hidden,
        log_total,
        labels,
    )
    return (result, kept)


def feed_backward(kept, slope_out, weights, totals):
    (
        state,
        normed,
        query,
        keys_all,
        values_all,
        cosine,
        sine,
        match,
        shares,
        attended,
        inner,
        mixed,
        normed_two,
        before,
        hidden,
        log_total,
        labels,
    ) = kept
    (
        joint_weight,
        joint_bias,
        output_weight,
        output_bias,
        up_weight,
        up_bias,
        down_weight,
        down_bias,
        first_gain,
        inner_gain,
        second_gain,
        hidden_gain,
    ) = weights
    slope_low = slope_out.astype(jnp.bfloat16)
    totals[6] = totals[6] + jnp.einsum(
        "rcf,rcd->fd", hidden, slope_low, preferred_element_type=jnp.float32
    )
    totals[7] = totals[7] + jnp.sum(slope_low.astype(jnp.float32), axis=(0, 1))
    slope_hidden = jnp.einsum(
        "rcd,fd->rcf", slope_low, down_weight, preferred_element_type=jnp.float32
    )
    unused, puller = jax.vjp(feed_norm, before, hidden_gain)
    slope_before, slope_gain = puller(slope_hidden)
    totals[11] = totals[11] + slope_gain
    before_low = slope_before.astype(jnp.bfloat16)
    totals[4] = totals[4] + jnp.einsum(
        "rcd,rcf->df", normed_two, before_low, preferred_element_type=jnp.float32
    )
    totals[5] = totals[5] + jnp.sum(before_low.astype(jnp.float32), axis=(0, 1))
    slope_normed = jnp.einsum(
        "rcf,df->rcd", before_low, up_weight, preferred_element_type=jnp.float32
    )
    unused, puller = jax.vjp(layer_norm, mixed, second_gain)
    slope_mixed, slope_gain = puller(slope_normed)
    totals[10] = totals[10] + slope_gain
    return (slope_out + slope_mixed, totals)


def attend_backward(kept, slope_mixed, weights, totals):
    (
        state,
        normed,
        query,
        keys_all,
        values_all,
        cosine,
        sine,
        match,
        shares,
        attended,
        inner,
        mixed,
        normed_two,
        before,
        hidden,
        log_total,
        labels,
    ) = kept
    (
        joint_weight,
        joint_bias,
        output_weight,
        output_bias,
        up_weight,
        up_bias,
        down_weight,
        down_bias,
        first_gain,
        inner_gain,
        second_gain,
        hidden_gain,
    ) = weights
    row_count, piece_len, model_width = state.shape
    head_count = model_width // HEAD_DIM
    scale = HEAD_DIM ** (-0.5)
    slope_low = slope_mixed.astype(jnp.bfloat16)
    totals[2] = totals[2] + jnp.einsum(
        "rcd,rce->de", inner, slope_low, preferred_element_type=jnp.float32
    )
    totals[3] = totals[3] + jnp.sum(slope_low.astype(jnp.float32), axis=(0, 1))
    slope_inner = jnp.einsum(
        "rce,de->rcd", slope_low, output_weight, preferred_element_type=jnp.float32
    )
    unused, puller = jax.vjp(layer_norm, attended, inner_gain)
    slope_attended, slope_gain = puller(slope_inner)
    totals[9] = totals[9] + slope_gain
    slope_heads = slope_attended.astype(jnp.bfloat16).reshape(
        row_count, piece_len, head_count, HEAD_DIM
    )
    slope_shares = jnp.einsum(
        "rqhd,rkhd->rhqk", slope_heads, values_all, preferred_element_type=jnp.float32
    )
    weighted = jnp.sum(shares * slope_shares, axis=-1, keepdims=True)
    slope_scores = (shares * (slope_shares - weighted)).astype(jnp.bfloat16)
    slope_query = (
        jnp.einsum("rhqk,rkhd->rqhd", slope_scores, keys_all, preferred_element_type=jnp.float32)
        * scale
    )
    shares_low = shares.astype(jnp.bfloat16)
    key_part = (
        jnp.einsum("rhqk,rqhd->krhd", slope_scores, query, preferred_element_type=jnp.float32)
        * scale
    )
    value_part = jnp.einsum(
        "rhqk,rqhd->krhd", shares_low, slope_heads, preferred_element_type=jnp.float32
    )
    summed = lax.psum_scatter(
        jnp.concatenate([key_part, value_part], axis=-1).astype(jnp.bfloat16),
        "seq",
        scatter_dimension=0,
        tiled=True,
    ).astype(jnp.float32)
    summed = jnp.transpose(summed, (1, 0, 2, 3))
    key_raw = summed[..., :HEAD_DIM]
    slope_value = summed[..., HEAD_DIM:]
    slope_key = rotate_back(key_raw, cosine, sine)
    slope_query = rotate_back(slope_query, cosine, sine)
    flat = (row_count, piece_len, model_width)
    slope_joint = jnp.concatenate(
        [slope_query.reshape(flat), slope_key.reshape(flat), slope_value.reshape(flat)], axis=-1
    ).astype(jnp.bfloat16)
    totals[0] = totals[0] + jnp.einsum(
        "rcd,rce->de", normed, slope_joint, preferred_element_type=jnp.float32
    )
    totals[1] = totals[1] + jnp.sum(slope_joint.astype(jnp.float32), axis=(0, 1))
    slope_normed = jnp.einsum(
        "rce,de->rcd", slope_joint, joint_weight, preferred_element_type=jnp.float32
    )
    unused, puller = jax.vjp(layer_norm, state, first_gain)
    slope_state, slope_gain = puller(slope_normed)
    totals[8] = totals[8] + slope_gain
    return (slope_mixed + slope_state, totals)


def lift(vector):
    return vector.reshape(1, vector.shape[0])


def shards(
    tokens,
    segments,
    cotangent,
    joint_weight,
    joint_bias,
    output_weight,
    output_bias,
    up_weight,
    up_bias,
    down_weight,
    down_bias,
    first_gain,
    inner_gain,
    second_gain,
    hidden_gain,
):
    weights = tuple(
        (
            item[0]
            for item in (
                joint_weight,
                joint_bias,
                output_weight,
                output_bias,
                up_weight,
                up_bias,
                down_weight,
                down_bias,
                first_gain,
                inner_gain,
                second_gain,
                hidden_gain,
            )
        )
    )
    micro, row_count, piece_len, model_width = tokens.shape
    leading = lax.axis_index("section") == 0
    part = lax.axis_index("seq")
    received = jnp.zeros((row_count, piece_len, model_width), jnp.bfloat16)
    saved = []
    results = []
    for moment in range(micro + 1):
        labels = jnp.where(leading, segments[min(moment, micro - 1)], segments[max(moment - 1, 0)])
        source = jnp.where(leading, tokens[min(moment, micro - 1)], received)
        state = source.astype(jnp.float32)
        result, kept = layer_forward(state, labels, weights, part)
        sent = result.astype(jnp.bfloat16)
        results.append(sent)
        saved.append((state, labels))
        if moment < micro:
            received = passed_along(sent, "section", 1)
    totals = [jnp.zeros(item.shape, jnp.float32) for item in weights]
    back_received = jnp.zeros((row_count, piece_len, model_width), jnp.bfloat16)
    back_results = []
    for moment in range(micro + 1):
        earlier = max(moment - 1, 0)
        later = min(moment + 1, micro)
        state = jnp.where(leading, saved[earlier][0], saved[later][0])
        labels = jnp.where(leading, saved[earlier][1], saved[later][1])
        kept = layer_forward(state, labels, weights, part)[1]
        if moment < micro:
            outer = cotangent[moment].astype(jnp.float32)
        else:
            outer = jnp.zeros((row_count, piece_len, model_width), jnp.float32)
        slope_out = jnp.where(leading, back_received.astype(jnp.float32), outer)
        slope_mixed, totals = feed_backward(kept, slope_out, weights, totals)
        slope_input, totals = attend_backward(kept, slope_mixed, weights, totals)
        back_results.append(slope_input)
        if moment < micro:
            back_received = passed_along(slope_input.astype(jnp.bfloat16), "section", -1)
    reduced = (
        lax.psum_scatter(totals[0], ("dp", "seq"), scatter_dimension=1, tiled=True),
        lax.psum_scatter(lift(totals[1]), ("dp", "seq"), scatter_dimension=1, tiled=True),
        lax.psum_scatter(totals[2], ("dp", "seq"), scatter_dimension=1, tiled=True),
        lax.psum_scatter(lift(totals[3]), ("dp", "seq"), scatter_dimension=1, tiled=True),
        lax.psum_scatter(totals[4], ("dp", "seq"), scatter_dimension=1, tiled=True),
        lax.psum_scatter(lift(totals[5]), ("dp", "seq"), scatter_dimension=1, tiled=True),
        lax.psum_scatter(totals[6], ("dp", "seq"), scatter_dimension=1, tiled=True),
        lax.psum_scatter(lift(totals[7]), ("dp", "seq"), scatter_dimension=1, tiled=True),
        lax.psum_scatter(lift(totals[8]), ("dp", "seq"), scatter_dimension=1, tiled=True),
        lax.psum_scatter(lift(totals[9]), ("dp", "seq"), scatter_dimension=1, tiled=True),
        lax.psum_scatter(lift(totals[10]), ("dp", "seq"), scatter_dimension=1, tiled=True),
        lax.psum_scatter(lift(totals[11]), ("dp", "seq"), scatter_dimension=1, tiled=True),
    )
    hiddens = jnp.stack(
        [jnp.where(leading, results[index], results[index + 1]) for index in range(micro)]
    )[None]
    input_gradients = jnp.stack(
        [jnp.where(leading, back_results[index + 1], back_results[index]) for index in range(micro)]
    )[None]
    return (
        hiddens,
        input_gradients,
        reduced[0][None],
        reduced[1],
        reduced[2][None],
        reduced[3],
        reduced[4][None],
        reduced[5],
        reduced[6][None],
        reduced[7],
        reduced[8],
        reduced[9],
        reduced[10],
        reduced[11],
    )


F32 = jnp.float32
BF16 = jnp.bfloat16
ANY = pl.BlockSpec(memory_space=pl.ANY)
SMEM = pl.BlockSpec(memory_space=pltpu.SMEM)
VLIM = 60 * 1024 * 1024


def lane_iota(shape):
    return lax.broadcasted_iota(jnp.int32, shape, len(shape) - 1)


def nn(a, b):
    return lax.dot_general(a, b, (((1,), (0,)), ((), ())), preferred_element_type=F32)


def nt(a, b):
    return lax.dot_general(a, b, (((1,), (1,)), ((), ())), preferred_element_type=F32)


def tn(a, b):
    return lax.dot_general(a, b, (((0,), (0,)), ((), ())), preferred_element_type=F32)


def normalize(value):
    centered = value - jnp.mean(value, axis=-1, keepdims=True)
    scale = lax.rsqrt(jnp.mean(centered * centered, axis=-1, keepdims=True) + EPSILON)
    return centered * scale, scale


def norm_back(slope, unit, scale):
    return scale * (
        slope
        - jnp.mean(slope, axis=-1, keepdims=True)
        - unit * jnp.mean(slope * unit, axis=-1, keepdims=True)
    )


def fold(value):
    rows, columns = value.shape
    return jnp.sum(value.reshape(rows // 8, 8, columns), axis=0)


def split3(value):
    high = value.astype(BF16)
    rest = value - high.astype(F32)
    middle = rest.astype(BF16)
    low = (rest - middle.astype(F32)).astype(BF16)
    return high, middle, low


JOINT_BIAS, OUTPUT_BIAS, UP_BIAS, DOWN_BIAS, FIRST_GAIN, INNER_GAIN, SECOND_GAIN, HIDDEN_GAIN = range(8)


def vectors_of(pack_ref, width, *numbers):
    wide = 4 * width
    lengths = (3 * width, width, wide, width, width, width, width, wide)
    views = []
    for number in numbers:
        views.append(pack_ref.at[0, :, pl.ds(sum(lengths[:number]), lengths[number])])
    return views


def pack_spec(layer, pack):
    return pl.BlockSpec((1, 1, pack.shape[-1]), lambda *_: (layer, 0, 0))


def fetch_weights(layer, sec_ref, pairs, sem):
    first = pl.program_id(0) == 0

    @pl.when(first & (sec_ref[0] == layer))
    def _():
        for index, (own, other, here) in enumerate(pairs):
            pltpu.make_async_copy(own, here, sem.at[index]).start()

    @pl.when(first & (sec_ref[0] != layer))
    def _():
        for index, (own, other, here) in enumerate(pairs):
            pltpu.make_async_copy(other, here, sem.at[index]).start()

    def arrive(index):
        @pl.when(first)
        def _():
            own, other, here = pairs[index]
            pltpu.make_async_copy(own, here, sem.at[index]).wait()

    return arrive


def gelu_parts(value):
    share = 0.5 + 0.5 * lax.erf(value * 0.5 ** 0.5)
    bell = jnp.exp2(value * value * (-0.5 * math.log2(math.e)))
    return value * share, share + value * bell * (1.0 / math.sqrt(2.0 * math.pi))


def qkv_kernel(layer, blocks, sec_ref, mine_ref, x_ref, y_ref, pack_ref, own_ref, other_ref, cos_ref, sin_ref,
               lab_ref, s_ref, n_ref, q_ref, k_ref, v_ref, w_ref, sem):
    arrive = fetch_weights(layer, sec_ref, [(own_ref, other_ref, w_ref)], sem)
    width = x_ref.shape[-1]
    gain_ref, bias_ref = vectors_of(pack_ref, width, FIRST_GAIN, JOINT_BIAS)
    state = jnp.where(jnp.full((1, 1), pl.program_id(0)) < blocks, x_ref[0], y_ref[...])
    s_ref[...] = state
    unit, scale = normalize(state.astype(F32))
    normed = (unit * gain_ref[...]).astype(BF16)
    n_ref[...] = normed
    cosine, sine = cos_ref[...], sin_ref[...]
    lane = lane_iota(cosine.shape)
    first = lane % HEAD_DIM < HEAD_DIM // 2
    head = lane < HEAD_DIM
    labels = lab_ref[...]
    document = lane - HEAD_DIM
    known = (document >= 0) & (document < 5)
    q_feat = jnp.where(known & (document != labels), MASKED, 0.0)
    ones = (document >= 5) & (document < 8)
    k_feat = jnp.where((known & (document == labels)) | ones, 1.0, 0.0)
    v_feat = jnp.where((document >= 0) & (document < 3), 1.0, 0.0)
    kinds = ((q_ref, q_feat), (k_ref, k_feat), (v_ref, v_feat))
    step = 256
    chunks = 3 * width // step

    def product(chunk):
        at = pl.ds(chunk * step, step)
        return nn(normed, w_ref[:, at]) + bias_ref[:, at]

    arrive(0)
    later = product(0)
    for chunk in range(chunks):
        joint = later
        if chunk + 1 < chunks:
            later = product(chunk + 1)
        for sub in range(step // 128):
            pair = chunk * step // 128 + sub
            which = pair * 128 // width
            out, feat = kinds[which]
            pair = pair - which * width // 128
            part = joint[:, sub * 128:(sub + 1) * 128]
            if which < 2:
                turned = jnp.where(first, pltpu.roll(part, 96, 1), pltpu.roll(part, 32, 1))
                part = part * cosine + turned * sine
            if which == 0:
                part = part * HEAD_DIM ** -0.5
            out[2 * pair] = jnp.where(head, part, feat).astype(BF16)
            out[2 * pair + 1] = jnp.where(head, pltpu.roll(part, 64, 1), feat).astype(BF16)


def qkv(layer, sec, x, pack, own, other, cosine, sine, labels, mine, tb=256):
    if isinstance(x, tuple):
        x, y = x
        blocks = x.shape[1] // tb
        rows, width = 2 * x.shape[1], x.shape[2]
    else:
        rows, width = x.shape
        blocks = rows // tb
        x, y = x[None], x
        mine = jnp.int32(0)
    heads = width // HEAD_DIM
    const = lambda shape: pl.BlockSpec(shape, lambda i, s, m: (0,) * len(shape))
    tok = lambda n: pl.BlockSpec((tb, n), lambda i, s, m: (i, 0))
    hd = pl.BlockSpec((heads, tb, 128), lambda i, s, m: (0, i, 0))
    return pl.pallas_call(
        functools.partial(qkv_kernel, layer, blocks),
        grid_spec=pltpu.PrefetchScalarGridSpec(
            num_scalar_prefetch=2,
            grid=(rows // tb,),
            in_specs=[pl.BlockSpec((1, tb, width), lambda i, s, m: (m[0], jnp.minimum(i, blocks - 1), 0)),
                      pl.BlockSpec((tb, width), lambda i, s, m: (jnp.maximum(i - blocks, 0), 0)),
                      pack_spec(layer, pack), ANY, ANY, tok(128), tok(128), tok(128)],
            out_specs=[tok(width), tok(width), hd, hd, hd],
            scratch_shapes=[pltpu.VMEM(own.shape, BF16), pltpu.SemaphoreType.DMA((1,))],
        ),
        out_shape=[jax.ShapeDtypeStruct((rows, width), BF16)] * 2 + [jax.ShapeDtypeStruct((heads, rows, 128), BF16)] * 3,
        compiler_params=pltpu.CompilerParams(vmem_limit_bytes=VLIM),
        cost_estimate=pl.CostEstimate(flops=1 * 2 * rows * width * 3 * width, bytes_accessed=16 * 1024 * 1024, transcendentals=0),
        name="joint_projection",
    )(sec, mine.reshape(1).astype(jnp.int32), x, y, pack, own, other, cosine, sine, labels)


def attend_kernel(qb, q_ref, k_ref, v_ref, o_ref, ql_ref):
    rows = q_ref.shape[1]
    lane = lane_iota((qb, 128))
    inside = (lane >= 69) & (lane < 72)
    work = [(head, block) for block in range(rows // qb) for head in range(2)]
    ready = {}

    def score(index):
        if index < len(work):
            head, block = work[index]
            ready[index] = nt(q_ref[head, pl.ds(block * qb, qb), :], k_ref[head])

    score(0)
    score(1)
    done = []
    for index, (head, block) in enumerate(work):
        score(index + 2)
        scores = ready.pop(index)
        at = pl.ds(block * qb, qb)
        peak = jnp.max(scores, axis=-1, keepdims=True)
        raised = jnp.exp(scores - peak).astype(BF16)
        sums = nn(raised, v_ref[head])
        total = sums[:, HEAD_DIM:HEAD_DIM + 1]
        done.append(sums * (1.0 / total))
        high, middle, low = split3(-(peak + jnp.log(total)))
        feat = jnp.where(lane == 69, high.astype(F32), jnp.where(lane == 70, middle.astype(F32), low.astype(F32)))
        ql_ref[head, at, :] = jnp.where(inside, feat, q_ref[head, at, :].astype(F32)).astype(BF16)
        if head == 1:
            o_ref[at, :] = jnp.where(lane < HEAD_DIM, done[0], pltpu.roll(done[1], 64, 1))
            done = []


def attend(q, k, v, qb=256):
    heads, rows, _ = q.shape
    hd = pl.BlockSpec((2, rows, 128), lambda i: (i, 0, 0))
    return pl.pallas_call(
        functools.partial(attend_kernel, qb),
        grid=(heads // 2,),
        in_specs=[hd, hd, hd],
        out_specs=[pl.BlockSpec((rows, 128), lambda i: (0, i)), hd],
        out_shape=[jax.ShapeDtypeStruct((rows, heads * HEAD_DIM), F32), jax.ShapeDtypeStruct(q.shape, BF16)],
        compiler_params=pltpu.CompilerParams(vmem_limit_bytes=VLIM),
        cost_estimate=pl.CostEstimate(flops=1 * 16 * heads * rows * rows * HEAD_DIM, bytes_accessed=16 * 1024 * 1024, transcendentals=0),
        name="attention_forward",
    )(q, k, v)


def feed_kernel(layer, sec_ref, at_ref, x_ref, pack_ref,
                wo0, wo1, wu0, wu1, wd0, wd1,
                out_ref, mixed_ref, hid_ref, gp_ref, st_ref, wo, wu, wd, bent, sem):
    arrive = fetch_weights(layer, sec_ref, [(wo0, wo1, wo), (wu0, wu1, wu), (wd0, wd1, wd)], sem)
    ig_ref, ob_ref, sg_ref, ub_ref, hg_ref, db_ref = vectors_of(
        pack_ref, x_ref.shape[-1], INNER_GAIN, OUTPUT_BIAS, SECOND_GAIN, UP_BIAS, HIDDEN_GAIN, DOWN_BIAS)
    wide = hg_ref.shape[-1]
    unit, _ = normalize(at_ref[...])
    inner = (unit * ig_ref[...]).astype(BF16)
    arrive(0)
    mixed = x_ref[...].astype(F32) + nn(inner, wo[...]) + ob_ref[...]
    mixed_ref[...] = mixed
    unit, _ = normalize(mixed)
    normed = (unit * sg_ref[...]).astype(BF16)
    step = 512
    chunks = wide // step

    def rise(chunk):
        at = pl.ds(chunk * step, step)
        return nn(normed, wu[:, at]) + ub_ref[:, at]

    arrive(1)
    later = rise(0)
    total = 0.0
    for chunk in range(chunks):
        before = later
        if chunk + 1 < chunks:
            later = rise(chunk + 1)
        at = pl.ds(chunk * step, step)
        value, bend = gelu_parts(before)
        gp_ref[:, at] = bend.astype(BF16)
        bent[:, at] = value
        total = total + jnp.sum(value, axis=-1, keepdims=True)
    mean = total * (1.0 / wide)
    spread = 0.0
    for chunk in range(chunks):
        centered = bent[:, pl.ds(chunk * step, step)] - mean
        spread = spread + jnp.sum(centered * centered, axis=-1, keepdims=True)
    scale = lax.rsqrt(spread * (1.0 / wide) + EPSILON)
    st_ref[...] = jnp.broadcast_to(scale, st_ref.shape)
    arrive(2)
    result = mixed + db_ref[...]
    for chunk in range(chunks):
        at = pl.ds(chunk * step, step)
        hidden = ((bent[:, at] - mean) * scale * hg_ref[:, at]).astype(BF16)
        hid_ref[:, at] = hidden
    result = result + nn(hid_ref[...], wd[...])
    out_ref[...] = result.astype(BF16)


def feed(layer, sec, attended, x, pack, wo, wu, wd, tb=512):
    rows, width = x.shape
    wide = wd[0].shape[0]
    tok = lambda n: pl.BlockSpec((tb, n), lambda i: (i, 0))
    S = jax.ShapeDtypeStruct
    return pl.pallas_call(
        functools.partial(feed_kernel, layer),
        grid=(rows // tb,),
        in_specs=[SMEM, tok(width), tok(width), pack_spec(layer, pack)] + [ANY] * 6,
        out_specs=[tok(width), tok(width), tok(wide), tok(wide), tok(128)],
        out_shape=[S((rows, width), BF16), S((rows, width), F32), S((rows, wide), BF16), S((rows, wide), BF16), S((rows, 128), F32)],
        scratch_shapes=[pltpu.VMEM(wo[0].shape, BF16), pltpu.VMEM(wu[0].shape, BF16), pltpu.VMEM(wd[0].shape, BF16), pltpu.VMEM((tb, wide), F32), pltpu.SemaphoreType.DMA((3,))],
        compiler_params=pltpu.CompilerParams(vmem_limit_bytes=VLIM),
        cost_estimate=pl.CostEstimate(flops=1 * 2 * rows * width * (2 * wide + width), bytes_accessed=40 * 1024 * 1024, transcendentals=0),
        name="feed_forward",
    )(sec, attended, x, pack, *wo, *wu, *wd)


def feed_back_kernel(layer, sec_ref, c_ref, hid_ref, gp_ref, st_ref, mixed_ref, at_ref,
                     pack_ref, wo0, wo1, wu0, wu1, wd0, wd1,
                     cb_ref, cm_ref, ct_ref, cl_ref, ch_ref, n2_ref, in_ref, wide_ref, thin_ref,
                     wo, wu, wd, sloped, wide_acc, thin_acc, sem):
    now = pl.program_id(0)
    ig_ref, sg_ref, hg_ref = vectors_of(pack_ref, c_ref.shape[-1], INNER_GAIN, SECOND_GAIN, HIDDEN_GAIN)

    @pl.when(now == 0)
    def _():
        wide_acc[...] = jnp.zeros_like(wide_acc)
        thin_acc[...] = jnp.zeros_like(thin_acc)

    arrive = fetch_weights(layer, sec_ref, [(wd0, wd1, wd), (wu0, wu1, wu), (wo0, wo1, wo)], sem)
    low = c_ref[...]
    ct_ref[...] = low.T
    outer = low.astype(F32)
    thin_acc[0] += fold(outer)
    wide = hg_ref.shape[-1]
    step = 512
    chunks = wide // step

    def fall(chunk):
        return nt(low, wd[pl.ds(chunk * step, step), :])

    arrive(0)
    later = fall(0)
    sum_moved = 0.0
    sum_slope = 0.0
    for chunk in range(chunks):
        slope = later
        if chunk + 1 < chunks:
            later = fall(chunk + 1)
        at = pl.ds(chunk * step, step)
        moved = slope * hid_ref[:, at].astype(F32)
        wide_acc[0, :, at] += fold(moved)
        sum_moved = sum_moved + jnp.sum(moved, axis=-1, keepdims=True)
        slope = slope * hg_ref[:, at]
        sum_slope = sum_slope + jnp.sum(slope, axis=-1, keepdims=True)
        sloped[:, at] = slope
    scale = st_ref[:, 0:1]
    mean_moved = sum_moved * (1.0 / wide)
    mean_slope = sum_slope * (1.0 / wide)
    arrive(1)
    slope_two = 0.0
    for chunk in range(chunks):
        at = pl.ds(chunk * step, step)
        unit = hid_ref[:, at].astype(F32) * (1.0 / hg_ref[:, at])
        slope = (sloped[:, at] - mean_slope - unit * mean_moved) * scale
        before_low = (slope * gp_ref[:, at].astype(F32)).astype(BF16)
        cb_ref[:, at] = before_low
        wide_acc[1, :, at] += fold(before_low.astype(F32))
        slope_two = slope_two + nt(before_low, wu[:, at])
    unit, scale = normalize(mixed_ref[...])
    n2_ref[...] = (unit * sg_ref[...]).astype(BF16)
    thin_acc[1] += fold(slope_two * unit)
    mixed = outer + norm_back(slope_two * sg_ref[...], unit, scale)
    cm_ref[...] = mixed
    mixed_low = mixed.astype(BF16)
    cl_ref[...] = mixed_low.T
    thin_acc[2] += fold(mixed_low.astype(F32))
    arrive(2)
    slope = nt(mixed_low, wo[...])
    unit, scale = normalize(at_ref[...])
    in_ref[...] = (unit * ig_ref[...]).astype(BF16)
    thin_acc[3] += fold(slope * unit)
    ch_ref[...] = norm_back(slope * ig_ref[...], unit, scale).astype(BF16)

    @pl.when(now == pl.num_programs(0) - 1)
    def _():
        inverse = 1.0 / hg_ref[...]
        wide_ref[0:1, :] = jnp.sum(wide_acc[0], axis=0, keepdims=True) * inverse
        wide_ref[1:2, :] = jnp.sum(wide_acc[1], axis=0, keepdims=True)
        for index in range(4):
            thin_ref[index:index + 1, :] = jnp.sum(thin_acc[index], axis=0, keepdims=True)


def feed_back(layer, sec, c, hidden, gp, st, mixed, attended, pack, wo, wu, wd, tb=256):
    rows, width = c.shape
    wide = wd[0].shape[0]
    const = lambda n, m=1: pl.BlockSpec((m, n), lambda i: (0, 0))
    tok = lambda n: pl.BlockSpec((tb, n), lambda i: (i, 0))
    turned = pl.BlockSpec((width, tb), lambda i: (0, i))
    S = jax.ShapeDtypeStruct
    return pl.pallas_call(
        functools.partial(feed_back_kernel, layer),
        grid=(rows // tb,),
        in_specs=[SMEM, tok(width), tok(wide), tok(wide), tok(128), tok(width), tok(width), pack_spec(layer, pack)] + [ANY] * 6,
        out_specs=[tok(wide), tok(width), turned, turned, tok(width), tok(width), tok(width), const(wide, 2), const(width, 4)],
        out_shape=[S((rows, wide), BF16), S((rows, width), F32), S((width, rows), BF16), S((width, rows), BF16), S((rows, width), BF16), S((rows, width), BF16), S((rows, width), BF16), S((2, wide), F32), S((4, width), F32)],
        scratch_shapes=[pltpu.VMEM(wo[0].shape, BF16), pltpu.VMEM(wu[0].shape, BF16), pltpu.VMEM(wd[0].shape, BF16),
                        pltpu.VMEM((tb, wide), F32), pltpu.VMEM((2, 8, wide), F32), pltpu.VMEM((4, 8, width), F32), pltpu.SemaphoreType.DMA((3,))],
        compiler_params=pltpu.CompilerParams(vmem_limit_bytes=VLIM),
        cost_estimate=pl.CostEstimate(flops=1 * 2 * rows * width * (2 * wide + width), bytes_accessed=50 * 1024 * 1024, transcendentals=0),
        name="feed_backward",
    )(sec, c, hidden, gp, st, mixed, attended, pack, *wo, *wu, *wd)


def attend_back_kernel(qb, q_ref, k_ref, v_ref, ch_ref, at_ref, cos_ref, sin_ref, cj_ref, kt, vt, qs, shares_ref, slope_ref):
    rows = q_ref.shape[1]
    lane = lane_iota((rows, 128))
    is_head = lane < HEAD_DIM
    slopes = ch_ref[...].astype(F32)
    product = slopes * at_ref[...]
    incoming = []
    for head in range(2):
        mine = is_head if head == 0 else jnp.logical_not(is_head)
        weighted = jnp.sum(jnp.where(mine, product, 0.0), axis=-1, keepdims=True)
        high, middle, low = split3(-weighted)
        feat = jnp.where(lane == 64, high.astype(F32), jnp.where(lane == 65, middle.astype(F32), jnp.where(lane == 66, low.astype(F32), 0.0)))
        local = slopes if head == 0 else pltpu.roll(slopes, 64, 1)
        incoming.append(jnp.where(is_head, local, feat).astype(BF16))
    blocks = rows // qb
    work = [(head, block) for head in range(2) for block in range(blocks)]
    ready = {}

    def score(index):
        if index < len(work):
            head, block = work[index]
            at = block * qb
            ready[index] = (
                nt(q_ref[head, pl.ds(at, qb), :], k_ref[head]),
                nt(incoming[head][at:at + qb], v_ref[head]),
            )

    score(0)
    for index, (head, block) in enumerate(work):
        score(index + 1)
        scores, turned = ready.pop(index)
        shares = jnp.exp(scores)
        slope = (shares * turned).astype(BF16)
        at = pl.ds(block * qb, qb)
        slope_ref[head, at, :] = slope
        shares_ref[head, at, :] = shares.astype(BF16)
        qs[head, at, :] = nn(slope, k_ref[head])
        if block == blocks - 1:
            rng = pl.ds(head * HEAD_DIM, HEAD_DIM)
            kt[rng, :] = nn(q_ref[head].T[:HEAD_DIM], slope_ref[head])
            vt[rng, :] = nn(incoming[head].T[:HEAD_DIM], shares_ref[head])
    cosine, sine = cos_ref[...], sin_ref[...]
    first = lane % HEAD_DIM < HEAD_DIM // 2

    def back(part):
        turned = jnp.where(first, pltpu.roll(part, 96, 1), pltpu.roll(part, 32, 1))
        return (part * cosine - turned * sine).astype(BF16)

    cj_ref[0] = back(jnp.where(is_head, qs[0], pltpu.roll(qs[1], 64, 1)) * HEAD_DIM ** -0.5)
    cj_ref[1] = back(kt[...].T)
    cj_ref[2] = vt[...].T.astype(BF16)


def attend_back(q, k, v, ch, attended, cosine, sine, begin=0, count=None, into=None, qb=256):
    heads, rows, _ = q.shape
    width = heads * HEAD_DIM
    count = heads // 2 - begin if count is None else count
    hd = pl.BlockSpec((2, rows, 128), lambda i: (i + begin, 0, 0))
    col = pl.BlockSpec((rows, 128), lambda i: (0, i + begin))
    con = pl.BlockSpec((rows, 128), lambda i: (0, 0))
    body = functools.partial(attend_back_kernel, qb)
    extra = () if into is None else (into,)

    def kernel(*refs):
        body(*refs[:7], *refs[7 + len(extra):])

    return pl.pallas_call(
        kernel,
        grid=(count,),
        in_specs=[hd, hd, hd, col, col, con, con] + [ANY] * len(extra),
        out_specs=pl.BlockSpec((3, rows, 128), lambda i: (0, 0, i + begin)),
        out_shape=jax.ShapeDtypeStruct((3, rows, width), BF16),
        input_output_aliases={7: 0} if extra else {},
        scratch_shapes=[pltpu.VMEM((128, rows), F32), pltpu.VMEM((128, rows), F32), pltpu.VMEM((2, rows, 128), F32),
                        pltpu.VMEM((2, rows, rows), BF16), pltpu.VMEM((2, rows, rows), BF16)],
        compiler_params=pltpu.CompilerParams(vmem_limit_bytes=VLIM),
        cost_estimate=pl.CostEstimate(flops=1 * 80 * count * rows * rows * HEAD_DIM, bytes_accessed=3 * count * 1024 * 1024, transcendentals=0),
        name="attention_backward",
    )(q, k, v, ch, attended, cosine, sine, *extra)


def qkv_back_kernel(layer, sec_ref, cj_ref, x_ref, cm_ref, pack_ref, own_ref, other_ref,
                    ci_ref, small_ref, w_ref, acc, sem):
    step = pl.program_id(0)
    arrive = fetch_weights(layer, sec_ref, [(own_ref, other_ref, w_ref)], sem)

    @pl.when(step == 0)
    def _():
        acc[...] = jnp.zeros_like(acc)

    width = x_ref.shape[-1]
    (gain_ref,) = vectors_of(pack_ref, width, FIRST_GAIN)
    arrive(0)
    slope = nt(cj_ref[0], w_ref[:, 0:width])
    for which in range(1, 3):
        slope = slope + nt(cj_ref[which], w_ref[:, which * width:(which + 1) * width])
    unit, scale = normalize(x_ref[...].astype(F32))
    acc[0] += fold(slope * unit)
    for which in range(3):
        acc[which + 1] += fold(cj_ref[which].astype(F32))
    ci_ref[...] = (cm_ref[...] + norm_back(slope * gain_ref[...], unit, scale)).astype(BF16)

    @pl.when(step == pl.num_programs(0) - 1)
    def _():
        for index in range(4):
            small_ref[index:index + 1, :] = jnp.sum(acc[index], axis=0, keepdims=True)


def qkv_back(layer, sec, cj, x, cm, pack, own, other, tb=256):
    rows, width = x.shape
    const = lambda n, m=1: pl.BlockSpec((m, n), lambda i: (0, 0))
    tok = lambda n: pl.BlockSpec((tb, n), lambda i: (i, 0))
    S = jax.ShapeDtypeStruct
    return pl.pallas_call(
        functools.partial(qkv_back_kernel, layer),
        grid=(rows // tb,),
        in_specs=[SMEM, pl.BlockSpec((3, tb, width), lambda i: (0, i, 0)), tok(width), tok(width), pack_spec(layer, pack), ANY, ANY],
        out_specs=[tok(width), const(width, 4)],
        out_shape=[S((rows, width), BF16), S((4, width), F32)],
        scratch_shapes=[pltpu.VMEM(own.shape, BF16), pltpu.VMEM((4, 8, width), F32), pltpu.SemaphoreType.DMA((1,))],
        compiler_params=pltpu.CompilerParams(vmem_limit_bytes=VLIM),
        cost_estimate=pl.CostEstimate(flops=1 * 2 * rows * width * 3 * width, bytes_accessed=16 * 1024 * 1024, transcendentals=0),
        name="joint_backward",
    )(sec, cj, x, cm, pack, own, other)


def feed_grads_kernel(sec_ref, order_ref, cb_ref, hid_ref, c_t, n2_ref, cm_t, in_ref, wide_ref, thin_ref,
                      keep_ref, send_ref, held, sem):
    step = pl.program_id(0)
    sec = sec_ref[0]
    parts = order_ref.shape[0] // 2
    width = n2_ref.shape[-1]
    half = width // 2
    wide = wide_ref.shape[-1]
    up_rows = wide // parts
    thin = width // parts
    span = cb_ref.shape[-1]
    subs = span // up_rows
    steps = pl.num_programs(0) // 2
    outs = (keep_ref, send_ref)
    last = 2 * up_rows + thin
    sides = [pl.ds(pl.multiple_of(which * half, 128), half) for which in (sec, 1 - sec)]

    def leave(side, at, begin, count):
        rows = pl.ds(begin, count)
        pltpu.make_async_copy(held.at[side, at, rows], outs[side].at[at, rows], sem).start()

    @pl.when(step == 0)
    def _():
        for window in range(wide // half):
            at = pl.ds(window * half, half)
            far = pl.ds(window // (wide // width // 1) * half, half)
            rows = jnp.concatenate([wide_ref[:, at], thin_ref[:, far], jnp.zeros((10, half), F32)], axis=0).astype(BF16)
            for side in range(2):
                for sub in range(half // up_rows):
                    held[side, order_ref[side * parts + window * (half // up_rows) + sub], last:, :] = rows
        for side in range(2):
            out = nn(cm_t[...], in_ref[:, sides[side]]).astype(BF16)
            for part in range(parts):
                at = order_ref[side * parts + part]
                held[side, at, 2 * up_rows:last, :] = out[thin * part:thin * (part + 1)]
                leave(side, at, 2 * up_rows, thin + 16)

    for side in range(2):
        up = tn(cb_ref[...], n2_ref[:, sides[side]]).astype(BF16)
        for sub in range(subs):
            at = order_ref[side * parts + step * subs + sub]
            held[side, at, 0:up_rows, :] = up[sub * up_rows:(sub + 1) * up_rows]
            leave(side, at, 0, up_rows)

    down = nn(c_t[...], hid_ref[...]).astype(BF16)
    side = step // steps
    for which in range(span // half):
        begin = pl.multiple_of(up_rows + thin * (step % steps * (span // half) + which), 16)
        for part in range(parts):
            held[side, order_ref[side * parts + part], pl.ds(begin, thin), :] = down[thin * part:thin * (part + 1), which * half:(which + 1) * half]

    begin = pl.multiple_of(up_rows + thin * (step % steps * (span // half)), 16)
    rows = pl.ds(begin, thin * (span // half))
    for number in range(2):
        @pl.when(side == number)
        def _():
            pltpu.make_async_copy(held.at[number, :, rows], outs[number].at[:, rows], sem).start()

    @pl.when(step == pl.num_programs(0) - 1)
    def _():
        for number in range(2):
            pltpu.make_async_copy(held.at[number], outs[number], sem).wait()


def feed_grads(sec, order, cb, hidden, c_t, n2, cm_t, inner, wide_sums, thin_sums):
    rows, width = n2.shape
    wide = cb.shape[-1]
    parts = order.shape[0] // 2
    half = width // 2
    steps = wide // width
    up_rows = wide // parts
    total = 2 * up_rows + width // parts + 16
    full = lambda n, m=rows: pl.BlockSpec((m, n), lambda i, s, o: (0, 0))
    out_shape = jax.ShapeDtypeStruct((parts, total, half), BF16)
    return pl.pallas_call(
        feed_grads_kernel,
        grid_spec=pltpu.PrefetchScalarGridSpec(
            num_scalar_prefetch=2,
            grid=(steps,),
            in_specs=[
                pl.BlockSpec((rows, width), lambda i, s, o: (0, i)),
                pl.BlockSpec((rows, width), lambda i, s, o: (0, jnp.where(i < steps // 2, s[0], 1 - s[0]) * (steps // 2) + i % (steps // 2))),
                full(rows, width), full(width), full(rows, width), full(width), full(wide, 2), full(width, 4),
            ],
            out_specs=[ANY, ANY],
            scratch_shapes=[pltpu.VMEM((2, parts, total, half), BF16), pltpu.SemaphoreType.DMA],
        ),
        out_shape=[out_shape, out_shape],
        compiler_params=pltpu.CompilerParams(vmem_limit_bytes=VLIM),
        cost_estimate=pl.CostEstimate(flops=1 * 2 * rows * width * (2 * wide + width), bytes_accessed=30 * 1024 * 1024, transcendentals=0),
        name="feed_gradients",
    )(sec, order, cb, hidden, c_t, n2, cm_t, inner, wide_sums, thin_sums)


def joint_grads_kernel(sec_ref, order_ref, cj_ref, n_ref, sums_ref, keep_ref, send_ref, found):
    step = pl.program_id(0)
    sec = sec_ref[0]
    parts = order_ref.shape[0] // 2
    width = n_ref.shape[-1]
    half = width // 2
    thick = 3 * width // parts
    outs = (keep_ref, send_ref)
    found[...] = tn(cj_ref[0], n_ref[...]).astype(BF16)
    for side, which in enumerate((sec, 1 - sec)):
        columns = pl.ds(pl.multiple_of(which * half, 128), half)
        for block in range(3):
            @pl.when(step == block)
            def _():
                for part in range(parts):
                    low, high = max(thick * part, width * block), min(thick * (part + 1), width * (block + 1))
                    if low < high:
                        at = order_ref[side * parts + part]
                        outs[side][at, low - thick * part:high - thick * part, :] = found[low - width * block:high - width * block, columns]

    @pl.when(step == 0)
    def _():
        for part in range(parts):
            window = thick * part // half
            rows = [sums_ref[1 + w // 2:2 + w // 2, w % 2 * half:w % 2 * half + half] for w in (window, min(window + 1, 5))]
            far = part // (parts // 2) * half
            rows = jnp.concatenate(rows + [sums_ref[0:1, far:far + half], jnp.zeros((13, half), F32)], axis=0).astype(BF16)
            for side in range(2):
                outs[side][order_ref[side * parts + part], thick:, :] = rows


def joint_grads(sec, order, cj, normed, sums):
    rows, width = normed.shape
    parts = order.shape[0] // 2
    half = width // 2
    thick = 3 * width // parts
    out_spec = pl.BlockSpec((parts, thick + 16, half), lambda i, s, o: (0, 0, 0))
    out_shape = jax.ShapeDtypeStruct((parts, thick + 16, half), BF16)
    return pl.pallas_call(
        joint_grads_kernel,
        grid_spec=pltpu.PrefetchScalarGridSpec(
            num_scalar_prefetch=2,
            grid=(3,),
            in_specs=[
                pl.BlockSpec((1, rows, width), lambda i, s, o: (i, 0, 0)),
                pl.BlockSpec((rows, width), lambda i, s, o: (0, 0)),
                pl.BlockSpec((4, width), lambda i, s, o: (0, 0)),
            ],
            out_specs=[out_spec, out_spec],
            scratch_shapes=[pltpu.VMEM((width, width), BF16)],
        ),
        out_shape=[out_shape, out_shape],
        compiler_params=pltpu.CompilerParams(vmem_limit_bytes=VLIM),
        cost_estimate=pl.CostEstimate(flops=1 * 6 * rows * width * width, bytes_accessed=14 * 1024 * 1024, transcendentals=0),
        name="joint_gradients",
    )(sec, order, cj, normed, sums)


def prepare_kernel(lengths, mine_ref, part_ref, seg_ref, rate_ref, *refs):
    vectors, (cos_ref, sin_ref, lab_ref, pack_ref) = refs[:len(lengths)], refs[len(lengths):]
    begin = 0
    for vector, length in zip(vectors, lengths):
        pack_ref[:, begin:begin + length] = vector[...]
        begin += length
    rows = seg_ref.shape[-1]
    piece = rows // 2
    second = jnp.full((1, 1), part_ref[0]) == 1
    row = seg_ref[0].astype(F32)
    turned = jnp.where(second, jnp.concatenate([row[:, piece:], row[:, :piece]], axis=1), row)
    labels = jnp.broadcast_to(turned, (128, rows)).T
    starts = jnp.zeros_like(labels)
    for document in range(1, 5):
        count = jnp.sum(jnp.where(row < document, 1.0, 0.0), axis=1, keepdims=True)
        starts = jnp.where(labels == document, count, starts)
    time = lax.broadcasted_iota(jnp.int32, labels.shape, 0).astype(F32)
    shift = jnp.where(second, jnp.where(time < piece, piece * 1.0, -piece * 1.0), 0.0)
    angle = (time + shift - starts) * rate_ref[...]
    lane = lane_iota(labels.shape)
    cos_ref[...] = jnp.cos(angle)
    sin_ref[...] = jnp.sin(angle) * jnp.where(lane % HEAD_DIM < HEAD_DIM // 2, -1.0, 1.0)
    lab_ref[...] = labels.astype(jnp.int32)


def prepare(mine, part, segments, vectors):
    rows = segments.shape[-1]
    lengths = tuple(vector.shape[-1] for vector in vectors)
    half = HEAD_DIM // 2
    rate = jnp.tile(1.0 / 10000.0 ** (jnp.arange(half, dtype=F32) * 2.0 / HEAD_DIM), 4)[None]
    whole = lambda m, n: pl.BlockSpec((m, n), lambda i, a, b: (0, 0))
    return pl.pallas_call(
        functools.partial(prepare_kernel, lengths),
        grid_spec=pltpu.PrefetchScalarGridSpec(
            num_scalar_prefetch=2,
            grid=(1,),
            in_specs=[pl.BlockSpec((1, 1, rows), lambda i, a, b: (a[0], 0, 0)), whole(1, 128)] + [whole(1, length) for length in lengths],
            out_specs=[whole(rows, 128), whole(rows, 128), whole(rows, 128), whole(1, sum(lengths))],
        ),
        out_shape=[jax.ShapeDtypeStruct((rows, 128), F32)] * 2 + [jax.ShapeDtypeStruct((rows, 128), jnp.int32), jax.ShapeDtypeStruct((1, sum(lengths)), F32)],
        compiler_params=pltpu.CompilerParams(vmem_limit_bytes=VLIM),
        name="row_tables",
    )(mine.reshape(1).astype(jnp.int32), part.reshape(1).astype(jnp.int32), segments, rate, *vectors)


def swap_pairs(change, sizes):
    sections, dps, seqs = sizes
    pairs = []
    for section in range(sections):
        for dp in range(dps):
            for seq in range(seqs):
                a, b, c = change(section, dp, seq)
                pairs.append(((section * dps + dp) * seqs + seq, (a * dps + b) * seqs + c))
    return pairs


FEED, JOINT = range(2)


class Reduction:
    def __init__(self, kept, sent, sizes):
        self.sizes = sizes
        self.kept, self.sent = kept, sent
        self.stage = 0
        self.result = None

    def send(self):
        if self.stage == 0:
            self.arrived = lax.ppermute(self.sent, "section", [(0, 1), (1, 0)])
        else:
            moves = (
                lambda s, d, q: (s, d ^ 1, q) if s == 0 else (s, d, q ^ 1),
                lambda s, d, q: (s, d, q ^ 1) if s == 0 else (s, d ^ 1, q),
                lambda s, d, q: (s, d ^ 2, q),
                lambda s, d, q: (s, d ^ 4, q),
            )
            self.arrived = lax.ppermute(self.sent, ("section", "dp", "seq"), swap_pairs(moves[self.stage - 1], self.sizes))
        self.stage += 1

    def add(self):
        kept, arrived = self.kept, self.arrived
        middle = kept.shape[0] // 2
        if middle == 0:
            self.result = kept[0].astype(F32) + arrived[0].astype(F32)
            return
        self.sent = (kept[middle:].astype(F32) + arrived[middle:].astype(F32)).astype(BF16)
        self.kept = (kept[:middle].astype(F32) + arrived[:middle].astype(F32)).astype(BF16)

    def finish(self):
        if self.result is not None:
            return self.result
        while self.stage < 5:
            self.add()
            self.send()
        self.add()
        return self.result


def advance(value, *moving):
    for item in moving:
        if item.stage:
            item.add()
    if all(item.stage == 5 for item in moving):
        results = [item.result for item in moving]
        value, results = lax.optimization_barrier((value, results))
        for item, result in zip(moving, results):
            item.result = result
        return value
    parts = [array for item in moving for array in (item.kept, item.sent)]
    value, parts = lax.optimization_barrier((value, parts))
    for index, item in enumerate(moving):
        item.kept, item.sent = parts[2 * index:2 * index + 2]
        item.send()
    return value


def last_kernel(cj_ref, n_ref, x_ref, cm_ref, pack_ref, own_ref, other_ref, feed_keep, feed_send, done_ref,
                out_ref, mine_ref, got_ref,
                w_ref, back, cj_t, acc, j_keep, j_send, r0, r1, r2, r3, r4, k1, k2, k3, k4, s1, s2, s3, s4,
                f1, f2, f3, fk2, fk3, fs2, fs3, swap_out, landed, send_sem, recv_sem, local_sem):
    s, d, q = (lax.axis_index(name) for name in ("section", "dp", "seq"))
    x = (s, d + 1 - 2 * (d % 2), q)
    y = (s, d, 1 - q)
    first = (s, (1 - s) * x[1] + s * d, (1 - s) * q + s * y[2])
    second = (s, s * x[1] + (1 - s) * d, s * q + (1 - s) * y[2])
    near = (s, d + 2 - 4 * (d // 2 % 2), q)
    far = (s, d + 4 - 8 * (d // 4), q)
    core = (1 - s, d, q)
    parts, thick, half = j_keep.shape
    thick -= 16
    width = n_ref.shape[-1]
    piece = got_ref.shape[1]

    @pl.when(s == 0)
    def _():
        pltpu.make_async_copy(own_ref, w_ref, local_sem).start()

    @pl.when(s == 1)
    def _():
        pltpu.make_async_copy(other_ref, w_ref, local_sem).start()

    barrier = pltpu.get_barrier_semaphore()
    across = (1 - s, d, 1 - q)
    for other in (core, x, y, near, far, across):
        pl.semaphore_signal(barrier, inc=1, device_id=other, device_id_type=pl.DeviceIdType.MESH)
    pl.semaphore_wait(barrier, 6)

    def ready(number, source, target, other):
        return pltpu.make_async_remote_copy(
            src_ref=source, dst_ref=target, send_sem=send_sem.at[number], recv_sem=recv_sem.at[number],
            device_id=other, device_id_type=pl.DeviceIdType.MESH)

    def send(number, source, target, other):
        copy = ready(number, source, target, other)
        copy.start()
        return copy

    def total(one, two):
        return one.astype(F32) + two.astype(F32)

    feed_rows = feed_keep.shape[1]
    feed_blocks = [pl.ds(number * (feed_rows // 2), feed_rows // 2) for number in range(2)]
    feed_flights = [send(number, feed_send.at[:, at], f1.at[:, at], second) for number, at in enumerate(feed_blocks)]
    (gain_ref,) = vectors_of(pack_ref, width, FIRST_GAIN)
    acc[...] = jnp.zeros_like(acc)
    tb = piece // 2
    rows = x_ref.shape[0]
    order = [2, 3, 0, 1]

    def slope_of(block):
        at = pl.ds(block * tb, tb)
        slope = nt(cj_ref[0, at], w_ref[:, 0:width])
        for which in range(1, 3):
            slope = slope + nt(cj_ref[which, at], w_ref[:, which * width:(which + 1) * width])
        return slope

    pltpu.make_async_copy(own_ref, w_ref, local_sem).wait()
    to_y = ready(16, back.at[pl.ds(piece, piece)], got_ref.at[0], (0, d, 1 - q))
    to_core = ready(17, back.at[pl.ds(0, piece)], got_ref.at[1], (0, d, q))
    to_across = ready(18, back.at[pl.ds(piece, piece)], got_ref.at[2], (0, d, 1 - q))
    later = slope_of(order[0])
    for number, block in enumerate(order):
        slope = later
        if number + 1 < len(order):
            later = slope_of(order[number + 1])
        at = pl.ds(block * tb, tb)
        unit, scale = normalize(x_ref[at, :].astype(F32))
        acc[0] += fold(slope * unit)
        for which in range(3):
            acc[which + 1] += fold(cj_ref[which, at].astype(F32))
        back[at, :] = (cm_ref[at, :] + norm_back(slope * gain_ref[...], unit, scale)).astype(BF16)
        if number == 1:
            @pl.when(s == 0)
            def _():
                to_y.start()
    mine_ref[...] = back[0:piece, :]

    sums = [jnp.sum(acc[number], axis=0, keepdims=True) for number in range(4)]
    for which in range(3):
        cj_t[which] = cj_ref[which].T

    def position(part, owner):
        bx, by = (part // 2 % 2 + d % 2) % 2, (part % 2 + q) % 2
        bz, cz = (part // 4 + d // 2) % 2, (part // 8 + d // 4) % 2
        depth = bz * 2 + cz
        return (1 - owner) * ((bx * 2 + by) * 4 + depth) + owner * ((by * 2 + bx) * 4 + depth)

    def gradients(target, owner):
        for block in range(3):
            found = nn(cj_t[block], n_ref[:, pl.ds(pl.multiple_of(owner * half, 128), half)]).astype(BF16)
            for part in range(parts):
                low, high = max(thick * part, width * block), min(thick * (part + 1), width * (block + 1))
                if low < high:
                    target[position(part, owner), low - thick * part:high - thick * part, :] = found[low - width * block:high - width * block]
        for part in range(parts):
            window = thick * part // half
            lines = [sums[1 + w // 2][:, w % 2 * half:w % 2 * half + half] for w in (window, min(window + 1, 5))]
            away = part // (parts // 2) * half
            lines = jnp.concatenate(lines + [sums[0][:, away:away + half], jnp.zeros((13, half), F32)], axis=0)
            target[position(part, owner), thick:, :] = lines.astype(BF16)

    gradients(j_send, 1 - s)
    blocks = [pl.ds(number * (thick + 16) // 2, (thick + 16) // 2) for number in range(2)]
    flights = [send(2 + number, j_send.at[:, at], r0.at[:, at], core) for number, at in enumerate(blocks)]
    for number, at in enumerate(feed_blocks):
        feed_flights[number].wait()
        fs2[:, at] = total(feed_keep[2:, at], f1[2:, at]).astype(BF16)
        feed_flights[number] = send(4 + number, fs2.at[:, at], f2.at[:, at], near)
        fk2[:, at] = total(feed_keep[:2, at], f1[:2, at]).astype(BF16)
    gradients(j_keep, s)
    kept, arrived = j_keep, r0
    for stage, (sent, held, target, other) in enumerate(
        ((s1, k1, r1, first), (s2, k2, r2, second), (s3, k3, r3, near), (s4, k4, r4, far))):
        middle = kept.shape[0] // 2
        for number, at in enumerate(blocks):
            flights[number].wait()
            sent[:, at] = total(kept[middle:, at], arrived[middle:, at]).astype(BF16)
            flights[number] = send(8 + 2 * stage + number, sent.at[:, at], target.at[:, at], other)
            held[:, at] = total(kept[:middle, at], arrived[:middle, at]).astype(BF16)
        kept, arrived = held, target
        if stage == 0:
            for number, at in enumerate(feed_blocks):
                feed_flights[number].wait()
                fs3[:, at] = total(fk2[1:, at], f2[1:, at]).astype(BF16)
                feed_flights[number] = send(6 + number, fs3.at[:, at], f3.at[:, at], far)
                fk3[:, at] = total(fk2[:1, at], f2[:1, at])
        if stage == 1:
            @pl.when(s == 1)
            def _():
                to_core.start()
                to_across.start()
    own = jnp.full((1, 1), s) == 0

    def settle(at, mine):
        done = done_ref[at, :]
        swap_out[at, :] = jnp.where(own, done, mine)
        out_ref[pl.ds(s, 1), at, :] = jnp.where(own, mine, done)[None]

    for number, at in enumerate(feed_blocks):
        feed_flights[number].wait()
        settle(at, fk3[0, at] + f3[0, at].astype(F32))
    for number, at in enumerate(blocks):
        flights[number].wait()
        settle(pl.ds(feed_rows + number * (thick + 16) // 2, (thick + 16) // 2), total(kept[0, at], arrived[0, at]))
    send(19, swap_out, landed, core).wait()
    out_ref[pl.ds(1 - s, 1)] = landed[...][None]

    @pl.when(s == 0)
    def _():
        to_y.wait_send()
        for copy in (to_y, to_core, to_across):
            copy.wait_recv()

    @pl.when(s == 1)
    def _():
        to_core.wait_send()
        to_across.wait_send()


def last_step(cj, normed, state, cm, pack, own, other, feed_keep, feed_send, done, parts):
    rows, width = state.shape
    half, piece = width // 2, rows // 2
    thick = 3 * width // parts + 16
    feed_rows = feed_keep.shape[1]
    vm = pl.BlockSpec(memory_space=pltpu.VMEM)
    level = lambda n, m=thick, t=BF16: pltpu.VMEM((n, m, half), t)
    steps = [parts >> number for number in range(1, 5)]
    S = jax.ShapeDtypeStruct
    return pl.pallas_call(
        last_kernel,
        in_specs=[vm] * 5 + [ANY] * 2 + [vm] * 3,
        out_specs=[vm] * 3,
        out_shape=[S((2, feed_rows + thick, half), F32), S((piece, width), BF16), S((3, piece, width), BF16)],
        scratch_shapes=[pltpu.VMEM(own.shape, BF16), pltpu.VMEM((rows, width), BF16), pltpu.VMEM((3, width, rows), BF16),
                        pltpu.VMEM((4, 8, width), F32)]
        + [level(parts)] * 3 + [level(n) for n in steps] * 3
        + [level(4, feed_rows), level(2, feed_rows), level(1, feed_rows), level(2, feed_rows), level(1, feed_rows, F32),
           level(2, feed_rows), level(1, feed_rows)]
        + [pltpu.VMEM((feed_rows + thick, half), F32)] * 2
        + [pltpu.SemaphoreType.DMA((20,)), pltpu.SemaphoreType.DMA((20,)), pltpu.SemaphoreType.DMA],
        compiler_params=pltpu.CompilerParams(collective_id=0, has_side_effects=True, vmem_limit_bytes=VLIM),
        cost_estimate=pl.CostEstimate(flops=0, bytes_accessed=100 * 1024 * 1024, transcendentals=0),
        name="last_step",
    )(cj, normed, state, cm, pack, own, other, feed_keep, feed_send, done)


def assemble_kernel(parts, index_ref, both_ref, joint_ref, jb_ref, out_ref, ob_ref, up_ref, ub_ref, down_ref, db_ref,
                    fg_ref, ig_ref, sg_ref, hg_ref):
    half = both_ref.shape[-1]
    index = index_ref[0]
    up_rows, thin, thick = up_ref.shape[0], out_ref.shape[0], joint_ref.shape[0]
    steps = up_rows // thin
    for side in range(2):
        at = pl.ds(side * half, half)
        up_ref[:, at] = both_ref[side, 0:up_rows, :]
        for step in range(steps):
            begin = up_rows + step * thin
            down_ref[:, pl.ds((side * steps + step) * half, half)] = both_ref[side, begin:begin + thin, :]
        begin = 2 * up_rows
        out_ref[:, at] = both_ref[side, begin:begin + thin, :]
        begin = 2 * up_rows + thin + 16
        joint_ref[:, at] = both_ref[side, begin:begin + thick, :]

    def cut(row, count, target):
        begin = index * count % half
        best = row[:, 0:count]
        for number in range(1, half // count):
            best = jnp.where(jnp.full((1, 1), begin) == number * count, row[:, number * count:(number + 1) * count], best)
        target[...] = best

    at = 2 * up_rows + thin
    for number, (target, count) in enumerate(((hg_ref, up_rows), (ub_ref, up_rows), (db_ref, thin), (sg_ref, thin), (ob_ref, thin), (ig_ref, thin))):
        cut(both_ref[0, at + number:at + number + 1, :], count, target)
    at += 16 + thick
    cut(both_ref[0, at + 2:at + 3, :], thin, fg_ref)
    line = jnp.concatenate([both_ref[0, at:at + 1, :], both_ref[0, at + 1:at + 2, :]], axis=1)
    best = line[:, 0:thick]
    for part in range(1, parts):
        begin = part * thick % half
        best = jnp.where(jnp.full((1, 1), index) == part, line[:, begin:begin + thick], best)
    jb_ref[...] = best


def assemble(index, both, parts, width):
    wide = 4 * width
    S = lambda *shape: jax.ShapeDtypeStruct(shape, F32)
    vm = pl.BlockSpec(memory_space=pltpu.VMEM)
    thin, up_rows, thick = width // parts, wide // parts, 3 * width // parts
    results = pl.pallas_call(
        functools.partial(assemble_kernel, parts),
        in_specs=[SMEM, vm],
        out_specs=[vm] * 12,
        out_shape=[S(thick, width), S(1, thick), S(thin, width), S(1, thin), S(up_rows, width), S(1, up_rows),
                   S(thin, wide), S(1, thin), S(1, thin), S(1, thin), S(1, thin), S(1, up_rows)],
        compiler_params=pltpu.CompilerParams(vmem_limit_bytes=VLIM),
        name="gradient_outputs",
    )(index.reshape(1).astype(jnp.int32), both)
    return tuple(item.T[None] if number in (0, 2, 4, 6) else item for number, item in enumerate(results))


def row_step(
    sizes,
    tokens,
    segments,
    cotangent,
    joint_weight,
    joint_bias,
    output_weight,
    output_bias,
    up_weight,
    up_bias,
    down_weight,
    down_bias,
    first_gain,
    inner_gain,
    second_gain,
    hidden_gain,
):
    micro, row_count, piece, width = tokens.shape
    rows = 2 * piece
    wide = up_weight.shape[-1]
    parts = sizes[1] * sizes[2]
    half = width // 2
    section = lax.axis_index("section")
    part = lax.axis_index("seq")
    data = lax.axis_index("dp")
    sec = section.reshape(1).astype(jnp.int32)
    mine = 2 * section + part
    swap = [(0, 1), (1, 0)]

    def pick(array, index):
        return lax.dynamic_index_in_dim(array, index, 0, keepdims=False)

    flat_tokens = tokens.reshape(micro * row_count, piece, width)
    beside = lax.ppermute(pick(flat_tokens, mine ^ 1), "seq", swap)
    both = [(own[0], lax.ppermute(own[0], "section", swap)) for own in (joint_weight, output_weight, up_weight, down_weight)]
    joint_pair, output_pair, up_pair, down_pair = both
    cosine, sine, labels, own = prepare(mine, part, segments.reshape(micro * row_count, 1, rows), (
        joint_bias, output_bias, up_bias, down_bias, first_gain, inner_gain, second_gain, hidden_gain))
    other = lax.ppermute(own, "section", swap)
    pack = jnp.where(section == 0, jnp.stack([own, other]), jnp.stack([other, own]))

    mx, my, mz = data % 2, part, data // 2
    index = jnp.arange(parts, dtype=jnp.int32)
    cx, cy, cz = (index // 2) % 2 ^ mx, index % 2 ^ my, index // 4 ^ mz
    depth = cz % 2 * 2 + cz // 2
    order_x, order_y = (cx * 2 + cy) * 4 + depth, (cy * 2 + cx) * 4 + depth
    order = jnp.where(section == 0, jnp.concatenate([order_x, order_y]), jnp.concatenate([order_y, order_x]))

    kept = []
    hiddens = []
    for layer in range(2):
        if layer == 0:
            state, normed, q, k, v = qkv(layer, sec, (flat_tokens, beside), pack, *joint_pair, cosine, sine, labels, mine)
            state, cotangent = lax.optimization_barrier((state, cotangent))
            flat = cotangent.reshape(micro * row_count, piece, width)
            slope = jnp.concatenate([pick(flat, mine), lax.ppermute(pick(flat, mine ^ 1), "seq", swap)], axis=0)
        else:
            _, normed, q, k, v = qkv(layer, sec, state, pack, *joint_pair, cosine, sine, labels, mine)
        attended, query = attend(q, k, v)
        result, mixed, hidden, bend, stats = feed(layer, sec, attended, state, pack, output_pair, up_pair, down_pair)
        kept.append((state, normed, query, k, v, attended, mixed, hidden, bend, stats))
        hiddens.append(result)
        state = result

    def halves(item):
        return item[:piece], item[piece:]

    every = ("section", "seq")
    blocks = []
    for fs, fq in ((0, 1), (1, 0), (1, 1)):
        first, second = (halves(item)[fq] for item in hiddens)
        owed = jnp.where(section == fs, first, second)
        blocks.append((owed, [(2 * s + q, 2 * (s ^ fs) + (q ^ fq)) for s in range(2) for q in range(2)]))
    slope, owed = lax.optimization_barrier((slope, [block for block, pairs in blocks]))
    gathered = [lax.ppermute(block, every, pairs) for block, (_, pairs) in zip(owed, blocks)]
    own = jnp.where(section == 0, halves(hiddens[0])[0], halves(hiddens[1])[0])

    def place(blocks):
        stacked = jnp.stack(blocks)
        return jnp.stack([pick(stacked, mine ^ index) for index in range(4)]).reshape(1, micro, row_count, piece, width)

    def deliver(layer, back):
        own, other = halves(back)
        moves = (
            (other, [(2 * layer + q, 2 * layer + (q ^ 1)) for q in range(2)]),
            (own, [(2 * (1 - layer) + q, 2 * layer + q) for q in range(2)]),
            (other, [(2 * (1 - layer) + q, 2 * layer + (q ^ 1)) for q in range(2)]),
        )
        return [own] + [lax.ppermute(block, every, pairs) for block, pairs in moves]

    flights = {}
    delivered = [None, None]

    for layer in (1, 0):
        state, normed, query, k, v, attended, mixed, hidden, bend, stats = kept[layer]
        cb, cm, slope_t, mixed_t, ch, n2, inner, wide_sums, thin_sums = feed_back(
            layer, sec, slope, hidden, bend, stats, mixed, attended, pack, output_pair, up_pair, down_pair)
        if layer == 0:
            cb = advance(cb, flights[FEED, 1], flights[JOINT, 1])
        flights[FEED, layer] = Reduction(*feed_grads(sec, order, cb, hidden, slope_t, n2, mixed_t, inner, wide_sums, thin_sums), sizes)
        if layer == 1:
            ch = advance(ch, flights[FEED, 1])
            cj = attend_back(query, k, v, ch, attended, cosine, sine)
            cj, gathered = lax.optimization_barrier((cj, gathered))
            cj = advance(cj, flights[FEED, 1])
        else:
            ch, delivered[1] = lax.optimization_barrier((ch, delivered[1]))
            ch = advance(ch, flights[FEED, 0], flights[FEED, 1], flights[JOINT, 1])
            count = query.shape[0] // 4
            cj = attend_back(query, k, v, ch, attended, cosine, sine, 0, count)
            cj = advance(cj, flights[FEED, 0], flights[FEED, 1], flights[JOINT, 1])
            cj = attend_back(query, k, v, ch, attended, cosine, sine, count, None, cj)
            cj = advance(cj, flights[FEED, 1])
            flights[JOINT, 1].add()
            flights[JOINT, 1].send()
            flights[FEED, 0].add()
        if layer == 0:
            break
        back, sums = qkv_back(layer, sec, cj, state, cm, pack, *joint_pair)
        delivered[layer] = deliver(layer, back)
        flights[JOINT, layer] = Reduction(*joint_grads(sec, order, cj, normed, sums), sizes)
        if layer == 1:
            back = advance(back, flights[JOINT, 1])
        slope = back
    before = flights[FEED, 0]
    done = jnp.concatenate([flights[FEED, 1].finish(), flights[JOINT, 1].finish()], axis=0)
    both, ours, got = last_step(cj, normed, state, cm, pack, *joint_pair, before.kept, before.sent, done, parts)
    hiddens = place([own] + gathered)
    input_gradients = place([jnp.where(section == 0, a, b) for a, b in zip((ours, got[0], got[1], got[2]), delivered[1])]).astype(F32)

    return (hiddens, input_gradients) + tuple(assemble(2 * data + part, both, parts, width))


def choose(sizes, *arrays):
    micro, row_count, piece, width = arrays[0].shape
    if sizes == (2, 8, 2) and micro * row_count == 4:
        return row_step(sizes, *arrays)
    return shards(*arrays)


def solution(mesh):
    axes = ("section", "dp", "seq")
    return jax.shard_map(
        functools.partial(choose, tuple(mesh.shape[name] for name in axes)),
        mesh=mesh,
        in_specs=(
            P(None, "dp", "seq", None),
            P(None, "dp", None),
            P(None, "dp", "seq", None),
            P("section", None, None),
            P("section", None),
            P("section", None, None),
            P("section", None),
            P("section", None, None),
            P("section", None),
            P("section", None, None),
            P("section", None),
            P("section", None),
            P("section", None),
            P("section", None),
            P("section", None),
        ),
        out_specs=(
            P("section", None, "dp", "seq", None),
            P("section", None, "dp", "seq", None),
            P("section", None, ("dp", "seq")),
            P("section", ("dp", "seq")),
            P("section", None, ("dp", "seq")),
            P("section", ("dp", "seq")),
            P("section", None, ("dp", "seq")),
            P("section", ("dp", "seq")),
            P("section", None, ("dp", "seq")),
            P("section", ("dp", "seq")),
            P("section", ("dp", "seq")),
            P("section", ("dp", "seq")),
            P("section", ("dp", "seq")),
            P("section", ("dp", "seq")),
        ),
        check_vma=False,
    )
```

```python
import functools
import math

import jax
import jax.numpy as jnp
from jax import lax
from jax.experimental import pallas as pl
from jax.experimental.pallas import tpu as pltpu
from jax.sharding import PartitionSpec as P

HEAD_DIM = 64


EPSILON = 1e-05
MASKED = -1e30


def passed_along(value, axis, by):
    devices = lax.axis_size(axis)
    pairs = [(i, i + by) for i in range(devices) if 0 <= i + by < devices]
    return lax.ppermute(value, axis, pairs)


def layer_norm(value, gain):
    centered = value - jnp.mean(value, axis=-1, keepdims=True)
    spread = jnp.mean(centered * centered, axis=-1, keepdims=True)
    return centered * lax.rsqrt(spread + EPSILON) * gain


def feed_norm(before, gain):
    return layer_norm(jax.nn.gelu(before, approximate=False), gain)


def rotate(value, cosine, sine):
    middle = value.shape[-1] // 2
    first, second = (value[..., :middle], value[..., middle:])
    return jnp.concatenate(
        [first * cosine - second * sine, second * cosine + first * sine], axis=-1
    )


def rotate_back(incoming, cosine, sine):
    middle = incoming.shape[-1] // 2
    first, second = (incoming[..., :middle], incoming[..., middle:])
    return jnp.concatenate(
        [first * cosine + second * sine, second * cosine - first * sine], axis=-1
    )


def layer_forward(state, labels, weights, part):
    (
        joint_weight,
        joint_bias,
        output_weight,
        output_bias,
        up_weight,
        up_bias,
        down_weight,
        down_bias,
        first_gain,
        inner_gain,
        second_gain,
        hidden_gain,
    ) = weights
    row_count, piece_len, model_width = state.shape
    head_count = model_width // HEAD_DIM
    shape_heads = (row_count, piece_len, head_count, HEAD_DIM)
    offset = part * piece_len
    local_labels = lax.dynamic_slice_in_dim(labels, offset, piece_len, 1)
    starts = jnp.sum((labels[:, None, :] < local_labels[:, :, None]).astype(jnp.int32), axis=-1)
    places = offset + jnp.arange(piece_len, dtype=jnp.int32)[None, :] - starts
    inverse_rate = 1.0 / 10000.0 ** (jnp.arange(HEAD_DIM // 2, dtype=jnp.float32) * 2.0 / HEAD_DIM)
    angle = places.astype(jnp.float32)[:, :, None, None] * inverse_rate
    cosine = jnp.cos(angle)
    sine = jnp.sin(angle)
    normed = layer_norm(state, first_gain).astype(jnp.bfloat16)
    joint = jnp.dot(normed, joint_weight, preferred_element_type=jnp.float32) + joint_bias
    query = rotate(joint[..., :model_width].reshape(shape_heads), cosine, sine).astype(jnp.bfloat16)
    key = rotate(
        joint[..., model_width : 2 * model_width].reshape(shape_heads), cosine, sine
    ).astype(jnp.bfloat16)
    value = joint[..., 2 * model_width :].reshape(shape_heads).astype(jnp.bfloat16)
    keys_all, values_all = (
        lax.all_gather(key, "seq", axis=1, tiled=True),
        lax.all_gather(value, "seq", axis=1, tiled=True),
    )
    match = local_labels[:, None, :, None] == labels[:, None, None, :]
    scores = jnp.einsum(
        "rqhd,rkhd->rhqk", query, keys_all, preferred_element_type=jnp.float32
    ) * HEAD_DIM ** (-0.5)
    scores = jnp.where(match, scores, MASKED)
    peak = jnp.max(scores, axis=-1, keepdims=True)
    raised = jnp.exp(scores - peak)
    total_raised = jnp.sum(raised, axis=-1, keepdims=True)
    shares = raised / total_raised
    log_total = peak + jnp.log(total_raised)
    attended = jnp.einsum(
        "rhqk,rkhd->rqhd",
        shares.astype(jnp.bfloat16),
        values_all,
        preferred_element_type=jnp.float32,
    ).reshape(row_count, piece_len, model_width)
    inner = layer_norm(attended, inner_gain).astype(jnp.bfloat16)
    mixed = state + jnp.dot(inner, output_weight, preferred_element_type=jnp.float32) + output_bias
    normed_two = layer_norm(mixed, second_gain).astype(jnp.bfloat16)
    before = jnp.dot(normed_two, up_weight, preferred_element_type=jnp.float32) + up_bias
    hidden = feed_norm(before, hidden_gain).astype(jnp.bfloat16)
    result = mixed + jnp.dot(hidden, down_weight, preferred_element_type=jnp.float32) + down_bias
    kept = (
        state,
        normed,
        query,
        keys_all,
        values_all,
        cosine,
        sine,
        match,
        shares,
        attended,
        inner,
        mixed,
        normed_two,
        before,
        hidden,
        log_total,
        labels,
    )
    return (result, kept)


def feed_backward(kept, slope_out, weights, totals):
    (
        state,
        normed,
        query,
        keys_all,
        values_all,
        cosine,
        sine,
        match,
        shares,
        attended,
        inner,
        mixed,
        normed_two,
        before,
        hidden,
        log_total,
        labels,
    ) = kept
    (
        joint_weight,
        joint_bias,
        output_weight,
        output_bias,
        up_weight,
        up_bias,
        down_weight,
        down_bias,
        first_gain,
        inner_gain,
        second_gain,
        hidden_gain,
    ) = weights
    slope_low = slope_out.astype(jnp.bfloat16)
    totals[6] = totals[6] + jnp.einsum(
        "rcf,rcd->fd", hidden, slope_low, preferred_element_type=jnp.float32
    )
    totals[7] = totals[7] + jnp.sum(slope_low.astype(jnp.float32), axis=(0, 1))
    slope_hidden = jnp.einsum(
        "rcd,fd->rcf", slope_low, down_weight, preferred_element_type=jnp.float32
    )
    unused, puller = jax.vjp(feed_norm, before, hidden_gain)
    slope_before, slope_gain = puller(slope_hidden)
    totals[11] = totals[11] + slope_gain
    before_low = slope_before.astype(jnp.bfloat16)
    totals[4] = totals[4] + jnp.einsum(
        "rcd,rcf->df", normed_two, before_low, preferred_element_type=jnp.float32
    )
    totals[5] = totals[5] + jnp.sum(before_low.astype(jnp.float32), axis=(0, 1))
    slope_normed = jnp.einsum(
        "rcf,df->rcd", before_low, up_weight, preferred_element_type=jnp.float32
    )
    unused, puller = jax.vjp(layer_norm, mixed, second_gain)
    slope_mixed, slope_gain = puller(slope_normed)
    totals[10] = totals[10] + slope_gain
    return (slope_out + slope_mixed, totals)


def attend_backward(kept, slope_mixed, weights, totals):
    (
        state,
        normed,
        query,
        keys_all,
        values_all,
        cosine,
        sine,
        match,
        shares,
        attended,
        inner,
        mixed,
        normed_two,
        before,
        hidden,
        log_total,
        labels,
    ) = kept
    (
        joint_weight,
        joint_bias,
        output_weight,
        output_bias,
        up_weight,
        up_bias,
        down_weight,
        down_bias,
        first_gain,
        inner_gain,
        second_gain,
        hidden_gain,
    ) = weights
    row_count, piece_len, model_width = state.shape
    head_count = model_width // HEAD_DIM
    scale = HEAD_DIM ** (-0.5)
    slope_low = slope_mixed.astype(jnp.bfloat16)
    totals[2] = totals[2] + jnp.einsum(
        "rcd,rce->de", inner, slope_low, preferred_element_type=jnp.float32
    )
    totals[3] = totals[3] + jnp.sum(slope_low.astype(jnp.float32), axis=(0, 1))
    slope_inner = jnp.einsum(
        "rce,de->rcd", slope_low, output_weight, preferred_element_type=jnp.float32
    )
    unused, puller = jax.vjp(layer_norm, attended, inner_gain)
    slope_attended, slope_gain = puller(slope_inner)
    totals[9] = totals[9] + slope_gain
    slope_heads = slope_attended.astype(jnp.bfloat16).reshape(
        row_count, piece_len, head_count, HEAD_DIM
    )
    slope_shares = jnp.einsum(
        "rqhd,rkhd->rhqk", slope_heads, values_all, preferred_element_type=jnp.float32
    )
    weighted = jnp.sum(shares * slope_shares, axis=-1, keepdims=True)
    slope_scores = (shares * (slope_shares - weighted)).astype(jnp.bfloat16)
    slope_query = (
        jnp.einsum("rhqk,rkhd->rqhd", slope_scores, keys_all, preferred_element_type=jnp.float32)
        * scale
    )
    shares_low = shares.astype(jnp.bfloat16)
    key_part = (
        jnp.einsum("rhqk,rqhd->krhd", slope_scores, query, preferred_element_type=jnp.float32)
        * scale
    )
    value_part = jnp.einsum(
        "rhqk,rqhd->krhd", shares_low, slope_heads, preferred_element_type=jnp.float32
    )
    summed = lax.psum_scatter(
        jnp.concatenate([key_part, value_part], axis=-1).astype(jnp.bfloat16),
        "seq",
        scatter_dimension=0,
        tiled=True,
    ).astype(jnp.float32)
    summed = jnp.transpose(summed, (1, 0, 2, 3))
    key_raw = summed[..., :HEAD_DIM]
    slope_value = summed[..., HEAD_DIM:]
    slope_key = rotate_back(key_raw, cosine, sine)
    slope_query = rotate_back(slope_query, cosine, sine)
    flat = (row_count, piece_len, model_width)
    slope_joint = jnp.concatenate(
        [slope_query.reshape(flat), slope_key.reshape(flat), slope_value.reshape(flat)], axis=-1
    ).astype(jnp.bfloat16)
    totals[0] = totals[0] + jnp.einsum(
        "rcd,rce->de", normed, slope_joint, preferred_element_type=jnp.float32
    )
    totals[1] = totals[1] + jnp.sum(slope_joint.astype(jnp.float32), axis=(0, 1))
    slope_normed = jnp.einsum(
        "rce,de->rcd", slope_joint, joint_weight, preferred_element_type=jnp.float32
    )
    unused, puller = jax.vjp(layer_norm, state, first_gain)
    slope_state, slope_gain = puller(slope_normed)
    totals[8] = totals[8] + slope_gain
    return (slope_mixed + slope_state, totals)


def lift(vector):
    return vector.reshape(1, vector.shape[0])


def shards(
    tokens,
    segments,
    cotangent,
    joint_weight,
    joint_bias,
    output_weight,
    output_bias,
    up_weight,
    up_bias,
    down_weight,
    down_bias,
    first_gain,
    inner_gain,
    second_gain,
    hidden_gain,
):
    weights = tuple(
        (
            item[0]
            for item in (
                joint_weight,
                joint_bias,
                output_weight,
                output_bias,
                up_weight,
                up_bias,
                down_weight,
                down_bias,
                first_gain,
                inner_gain,
                second_gain,
                hidden_gain,
            )
        )
    )
    micro, row_count, piece_len, model_width = tokens.shape
    leading = lax.axis_index("section") == 0
    part = lax.axis_index("seq")
    received = jnp.zeros((row_count, piece_len, model_width), jnp.bfloat16)
    saved = []
    results = []
    for moment in range(micro + 1):
        labels = jnp.where(leading, segments[min(moment, micro - 1)], segments[max(moment - 1, 0)])
        source = jnp.where(leading, tokens[min(moment, micro - 1)], received)
        state = source.astype(jnp.float32)
        result, kept = layer_forward(state, labels, weights, part)
        sent = result.astype(jnp.bfloat16)
        results.append(sent)
        saved.append((state, labels))
        if moment < micro:
            received = passed_along(sent, "section", 1)
    totals = [jnp.zeros(item.shape, jnp.float32) for item in weights]
    back_received = jnp.zeros((row_count, piece_len, model_width), jnp.bfloat16)
    back_results = []
    for moment in range(micro + 1):
        earlier = max(moment - 1, 0)
        later = min(moment + 1, micro)
        state = jnp.where(leading, saved[earlier][0], saved[later][0])
        labels = jnp.where(leading, saved[earlier][1], saved[later][1])
        kept = layer_forward(state, labels, weights, part)[1]
        if moment < micro:
            outer = cotangent[moment].astype(jnp.float32)
        else:
            outer = jnp.zeros((row_count, piece_len, model_width), jnp.float32)
        slope_out = jnp.where(leading, back_received.astype(jnp.float32), outer)
        slope_mixed, totals = feed_backward(kept, slope_out, weights, totals)
        slope_input, totals = attend_backward(kept, slope_mixed, weights, totals)
        back_results.append(slope_input)
        if moment < micro:
            back_received = passed_along(slope_input.astype(jnp.bfloat16), "section", -1)
    reduced = (
        lax.psum_scatter(totals[0], ("dp", "seq"), scatter_dimension=1, tiled=True),
        lax.psum_scatter(lift(totals[1]), ("dp", "seq"), scatter_dimension=1, tiled=True),
        lax.psum_scatter(totals[2], ("dp", "seq"), scatter_dimension=1, tiled=True),
        lax.psum_scatter(lift(totals[3]), ("dp", "seq"), scatter_dimension=1, tiled=True),
        lax.psum_scatter(totals[4], ("dp", "seq"), scatter_dimension=1, tiled=True),
        lax.psum_scatter(lift(totals[5]), ("dp", "seq"), scatter_dimension=1, tiled=True),
        lax.psum_scatter(totals[6], ("dp", "seq"), scatter_dimension=1, tiled=True),
        lax.psum_scatter(lift(totals[7]), ("dp", "seq"), scatter_dimension=1, tiled=True),
        lax.psum_scatter(lift(totals[8]), ("dp", "seq"), scatter_dimension=1, tiled=True),
        lax.psum_scatter(lift(totals[9]), ("dp", "seq"), scatter_dimension=1, tiled=True),
        lax.psum_scatter(lift(totals[10]), ("dp", "seq"), scatter_dimension=1, tiled=True),
        lax.psum_scatter(lift(totals[11]), ("dp", "seq"), scatter_dimension=1, tiled=True),
    )
    hiddens = jnp.stack(
        [jnp.where(leading, results[index], results[index + 1]) for index in range(micro)]
    )[None]
    input_gradients = jnp.stack(
        [jnp.where(leading, back_results[index + 1], back_results[index]) for index in range(micro)]
    )[None]
    return (
        hiddens,
        input_gradients,
        reduced[0][None],
        reduced[1],
        reduced[2][None],
        reduced[3],
        reduced[4][None],
        reduced[5],
        reduced[6][None],
        reduced[7],
        reduced[8],
        reduced[9],
        reduced[10],
        reduced[11],
    )


F32 = jnp.float32
BF16 = jnp.bfloat16
ANY = pl.BlockSpec(memory_space=pl.ANY)
SMEM = pl.BlockSpec(memory_space=pltpu.SMEM)
VLIM = 60 * 1024 * 1024


def lane_iota(shape):
    return lax.broadcasted_iota(jnp.int32, shape, len(shape) - 1)


def nn(a, b):
    return lax.dot_general(a, b, (((1,), (0,)), ((), ())), preferred_element_type=F32)


def nt(a, b):
    return lax.dot_general(a, b, (((1,), (1,)), ((), ())), preferred_element_type=F32)


def tn(a, b):
    return lax.dot_general(a, b, (((0,), (0,)), ((), ())), preferred_element_type=F32)


def normalize(value):
    centered = value - jnp.mean(value, axis=-1, keepdims=True)
    scale = lax.rsqrt(jnp.mean(centered * centered, axis=-1, keepdims=True) + EPSILON)
    return centered * scale, scale


def norm_back(slope, unit, scale):
    return scale * (
        slope
        - jnp.mean(slope, axis=-1, keepdims=True)
        - unit * jnp.mean(slope * unit, axis=-1, keepdims=True)
    )


def fold(value):
    rows, columns = value.shape
    return jnp.sum(value.reshape(rows // 8, 8, columns), axis=0)


def split3(value):
    high = value.astype(BF16)
    rest = value - high.astype(F32)
    middle = rest.astype(BF16)
    low = (rest - middle.astype(F32)).astype(BF16)
    return high, middle, low


JOINT_BIAS, OUTPUT_BIAS, UP_BIAS, DOWN_BIAS, FIRST_GAIN, INNER_GAIN, SECOND_GAIN, HIDDEN_GAIN = range(8)


def vectors_of(pack_ref, width, *numbers):
    wide = 4 * width
    lengths = (3 * width, width, wide, width, width, width, width, wide)
    views = []
    for number in numbers:
        views.append(pack_ref.at[0, :, pl.ds(sum(lengths[:number]), lengths[number])])
    return views


def pack_spec(layer, pack):
    return pl.BlockSpec((1, 1, pack.shape[-1]), lambda *_: (layer, 0, 0))


def fetch_weights(layer, sec_ref, pairs, sem):
    first = pl.program_id(0) == 0

    @pl.when(first & (sec_ref[0] == layer))
    def _():
        for index, (own, other, here) in enumerate(pairs):
            pltpu.make_async_copy(own, here, sem.at[index]).start()

    @pl.when(first & (sec_ref[0] != layer))
    def _():
        for index, (own, other, here) in enumerate(pairs):
            pltpu.make_async_copy(other, here, sem.at[index]).start()

    def arrive(index):
        @pl.when(first)
        def _():
            own, other, here = pairs[index]
            pltpu.make_async_copy(own, here, sem.at[index]).wait()

    return arrive


def gelu_parts(value):
    share = 0.5 + 0.5 * lax.erf(value * 0.5 ** 0.5)
    bell = jnp.exp2(value * value * (-0.5 * math.log2(math.e)))
    return value * share, share + value * bell * (1.0 / math.sqrt(2.0 * math.pi))


def qkv_kernel(layer, blocks, sec_ref, mine_ref, x_ref, y_ref, pack_ref, own_ref, other_ref, cos_ref, sin_ref,
               lab_ref, s_ref, n_ref, q_ref, k_ref, v_ref, w_ref, sem):
    arrive = fetch_weights(layer, sec_ref, [(own_ref, other_ref, w_ref)], sem)
    width = x_ref.shape[-1]
    gain_ref, bias_ref = vectors_of(pack_ref, width, FIRST_GAIN, JOINT_BIAS)
    state = jnp.where(jnp.full((1, 1), pl.program_id(0)) < blocks, x_ref[0], y_ref[...])
    s_ref[...] = state
    unit, scale = normalize(state.astype(F32))
    normed = (unit * gain_ref[...]).astype(BF16)
    n_ref[...] = normed
    cosine, sine = cos_ref[...], sin_ref[...]
    lane = lane_iota(cosine.shape)
    first = lane % HEAD_DIM < HEAD_DIM // 2
    head = lane < HEAD_DIM
    labels = lab_ref[...]
    document = lane - HEAD_DIM
    known = (document >= 0) & (document < 5)
    q_feat = jnp.where(known & (document != labels), MASKED, 0.0)
    ones = (document >= 5) & (document < 8)
    k_feat = jnp.where((known & (document == labels)) | ones, 1.0, 0.0)
    v_feat = jnp.where((document >= 0) & (document < 3), 1.0, 0.0)
    kinds = ((q_ref, q_feat), (k_ref, k_feat), (v_ref, v_feat))
    step = 256
    chunks = 3 * width // step

    def product(chunk):
        at = pl.ds(chunk * step, step)
        return nn(normed, w_ref[:, at]) + bias_ref[:, at]

    arrive(0)
    later = product(0)
    for chunk in range(chunks):
        joint = later
        if chunk + 1 < chunks:
            later = product(chunk + 1)
        for sub in range(step // 128):
            pair = chunk * step // 128 + sub
            which = pair * 128 // width
            out, feat = kinds[which]
            pair = pair - which * width // 128
            part = joint[:, sub * 128:(sub + 1) * 128]
            if which < 2:
                turned = jnp.where(first, pltpu.roll(part, 96, 1), pltpu.roll(part, 32, 1))
                part = part * cosine + turned * sine
            if which == 0:
                part = part * HEAD_DIM ** -0.5
            out[2 * pair] = jnp.where(head, part, feat).astype(BF16)
            out[2 * pair + 1] = jnp.where(head, pltpu.roll(part, 64, 1), feat).astype(BF16)


def qkv(layer, sec, x, pack, own, other, cosine, sine, labels, mine, tb=256):
    if isinstance(x, tuple):
        x, y = x
        blocks = x.shape[1] // tb
        rows, width = 2 * x.shape[1], x.shape[2]
    else:
        rows, width = x.shape
        blocks = rows // tb
        x, y = x[None], x
        mine = jnp.int32(0)
    heads = width // HEAD_DIM
    const = lambda shape: pl.BlockSpec(shape, lambda i, s, m: (0,) * len(shape))
    tok = lambda n: pl.BlockSpec((tb, n), lambda i, s, m: (i, 0))
    hd = pl.BlockSpec((heads, tb, 128), lambda i, s, m: (0, i, 0))
    return pl.pallas_call(
        functools.partial(qkv_kernel, layer, blocks),
        grid_spec=pltpu.PrefetchScalarGridSpec(
            num_scalar_prefetch=2,
            grid=(rows // tb,),
            in_specs=[pl.BlockSpec((1, tb, width), lambda i, s, m: (m[0], jnp.minimum(i, blocks - 1), 0)),
                      pl.BlockSpec((tb, width), lambda i, s, m: (jnp.maximum(i - blocks, 0), 0)),
                      pack_spec(layer, pack), ANY, ANY, tok(128), tok(128), tok(128)],
            out_specs=[tok(width), tok(width), hd, hd, hd],
            scratch_shapes=[pltpu.VMEM(own.shape, BF16), pltpu.SemaphoreType.DMA((1,))],
        ),
        out_shape=[jax.ShapeDtypeStruct((rows, width), BF16)] * 2 + [jax.ShapeDtypeStruct((heads, rows, 128), BF16)] * 3,
        compiler_params=pltpu.CompilerParams(vmem_limit_bytes=VLIM),
        cost_estimate=pl.CostEstimate(flops=1 * 2 * rows * width * 3 * width, bytes_accessed=16 * 1024 * 1024, transcendentals=0),
        name="joint_projection",
    )(sec, mine.reshape(1).astype(jnp.int32), x, y, pack, own, other, cosine, sine, labels)


def attend_kernel(qb, q_ref, k_ref, v_ref, o_ref, ql_ref):
    rows = q_ref.shape[1]
    lane = lane_iota((qb, 128))
    inside = (lane >= 69) & (lane < 72)
    work = [(head, block) for block in range(rows // qb) for head in range(2)]
    ready = {}

    def score(index):
        if index < len(work):
            head, block = work[index]
            ready[index] = nt(q_ref[head, pl.ds(block * qb, qb), :], k_ref[head])

    score(0)
    score(1)
    done = []
    for index, (head, block) in enumerate(work):
        score(index + 2)
        scores = ready.pop(index)
        at = pl.ds(block * qb, qb)
        peak = jnp.max(scores, axis=-1, keepdims=True)
        raised = jnp.exp(scores - peak).astype(BF16)
        sums = nn(raised, v_ref[head])
        total = sums[:, HEAD_DIM:HEAD_DIM + 1]
        done.append(sums * (1.0 / total))
        high, middle, low = split3(-(peak + jnp.log(total)))
        feat = jnp.where(lane == 69, high.astype(F32), jnp.where(lane == 70, middle.astype(F32), low.astype(F32)))
        ql_ref[head, at, :] = jnp.where(inside, feat, q_ref[head, at, :].astype(F32)).astype(BF16)
        if head == 1:
            o_ref[at, :] = jnp.where(lane < HEAD_DIM, done[0], pltpu.roll(done[1], 64, 1))
            done = []


def attend(q, k, v, qb=256):
    heads, rows, _ = q.shape
    hd = pl.BlockSpec((2, rows, 128), lambda i: (i, 0, 0))
    return pl.pallas_call(
        functools.partial(attend_kernel, qb),
        grid=(heads // 2,),
        in_specs=[hd, hd, hd],
        out_specs=[pl.BlockSpec((rows, 128), lambda i: (0, i)), hd],
        out_shape=[jax.ShapeDtypeStruct((rows, heads * HEAD_DIM), F32), jax.ShapeDtypeStruct(q.shape, BF16)],
        compiler_params=pltpu.CompilerParams(vmem_limit_bytes=VLIM),
        cost_estimate=pl.CostEstimate(flops=1 * 16 * heads * rows * rows * HEAD_DIM, bytes_accessed=16 * 1024 * 1024, transcendentals=0),
        name="attention_forward",
    )(q, k, v)


def feed_kernel(layer, sec_ref, at_ref, x_ref, pack_ref,
                wo0, wo1, wu0, wu1, wd0, wd1,
                out_ref, mixed_ref, hid_ref, gp_ref, st_ref, wo, wu, wd, bent, sem):
    arrive = fetch_weights(layer, sec_ref, [(wo0, wo1, wo), (wu0, wu1, wu), (wd0, wd1, wd)], sem)
    ig_ref, ob_ref, sg_ref, ub_ref, hg_ref, db_ref = vectors_of(
        pack_ref, x_ref.shape[-1], INNER_GAIN, OUTPUT_BIAS, SECOND_GAIN, UP_BIAS, HIDDEN_GAIN, DOWN_BIAS)
    wide = hg_ref.shape[-1]
    unit, _ = normalize(at_ref[...])
    inner = (unit * ig_ref[...]).astype(BF16)
    arrive(0)
    mixed = x_ref[...].astype(F32) + nn(inner, wo[...]) + ob_ref[...]
    mixed_ref[...] = mixed
    unit, _ = normalize(mixed)
    normed = (unit * sg_ref[...]).astype(BF16)
    step = 512
    chunks = wide // step

    def rise(chunk):
        at = pl.ds(chunk * step, step)
        return nn(normed, wu[:, at]) + ub_ref[:, at]

    arrive(1)
    later = rise(0)
    total = 0.0
    for chunk in range(chunks):
        before = later
        if chunk + 1 < chunks:
            later = rise(chunk + 1)
        at = pl.ds(chunk * step, step)
        value, bend = gelu_parts(before)
        gp_ref[:, at] = bend.astype(BF16)
        bent[:, at] = value
        total = total + jnp.sum(value, axis=-1, keepdims=True)
    mean = total * (1.0 / wide)
    spread = 0.0
    for chunk in range(chunks):
        centered = bent[:, pl.ds(chunk * step, step)] - mean
        spread = spread + jnp.sum(centered * centered, axis=-1, keepdims=True)
    scale = lax.rsqrt(spread * (1.0 / wide) + EPSILON)
    st_ref[...] = jnp.broadcast_to(scale, st_ref.shape)
    arrive(2)
    result = mixed + db_ref[...]
    for chunk in range(chunks):
        at = pl.ds(chunk * step, step)
        hidden = ((bent[:, at] - mean) * scale * hg_ref[:, at]).astype(BF16)
        hid_ref[:, at] = hidden
    result = result + nn(hid_ref[...], wd[...])
    out_ref[...] = result.astype(BF16)


def feed(layer, sec, attended, x, pack, wo, wu, wd, tb=512):
    rows, width = x.shape
    wide = wd[0].shape[0]
    tok = lambda n: pl.BlockSpec((tb, n), lambda i: (i, 0))
    S = jax.ShapeDtypeStruct
    return pl.pallas_call(
        functools.partial(feed_kernel, layer),
        grid=(rows // tb,),
        in_specs=[SMEM, tok(width), tok(width), pack_spec(layer, pack)] + [ANY] * 6,
        out_specs=[tok(width), tok(width), tok(wide), tok(wide), tok(128)],
        out_shape=[S((rows, width), BF16), S((rows, width), F32), S((rows, wide), BF16), S((rows, wide), BF16), S((rows, 128), F32)],
        scratch_shapes=[pltpu.VMEM(wo[0].shape, BF16), pltpu.VMEM(wu[0].shape, BF16), pltpu.VMEM(wd[0].shape, BF16), pltpu.VMEM((tb, wide), F32), pltpu.SemaphoreType.DMA((3,))],
        compiler_params=pltpu.CompilerParams(vmem_limit_bytes=VLIM),
        cost_estimate=pl.CostEstimate(flops=1 * 2 * rows * width * (2 * wide + width), bytes_accessed=40 * 1024 * 1024, transcendentals=0),
        name="feed_forward",
    )(sec, attended, x, pack, *wo, *wu, *wd)


def feed_back_kernel(layer, sec_ref, c_ref, hid_ref, gp_ref, st_ref, mixed_ref, at_ref,
                     pack_ref, wo0, wo1, wu0, wu1, wd0, wd1,
                     cb_ref, cm_ref, ct_ref, cl_ref, ch_ref, n2_ref, in_ref, wide_ref, thin_ref,
                     wo, wu, wd, sloped, wide_acc, thin_acc, sem):
    now = pl.program_id(0)
    ig_ref, sg_ref, hg_ref = vectors_of(pack_ref, c_ref.shape[-1], INNER_GAIN, SECOND_GAIN, HIDDEN_GAIN)

    @pl.when(now == 0)
    def _():
        wide_acc[...] = jnp.zeros_like(wide_acc)
        thin_acc[...] = jnp.zeros_like(thin_acc)

    arrive = fetch_weights(layer, sec_ref, [(wd0, wd1, wd), (wu0, wu1, wu), (wo0, wo1, wo)], sem)
    low = c_ref[...]
    ct_ref[...] = low.T
    outer = low.astype(F32)
    thin_acc[0] += fold(outer)
    wide = hg_ref.shape[-1]
    step = 512
    chunks = wide // step

    def fall(chunk):
        return nt(low, wd[pl.ds(chunk * step, step), :])

    arrive(0)
    later = fall(0)
    sum_moved = 0.0
    sum_slope = 0.0
    for chunk in range(chunks):
        slope = later
        if chunk + 1 < chunks:
            later = fall(chunk + 1)
        at = pl.ds(chunk * step, step)
        moved = slope * hid_ref[:, at].astype(F32)
        wide_acc[0, :, at] += fold(moved)
        sum_moved = sum_moved + jnp.sum(moved, axis=-1, keepdims=True)
        slope = slope * hg_ref[:, at]
        sum_slope = sum_slope + jnp.sum(slope, axis=-1, keepdims=True)
        sloped[:, at] = slope
    scale = st_ref[:, 0:1]
    mean_moved = sum_moved * (1.0 / wide)
    mean_slope = sum_slope * (1.0 / wide)
    arrive(1)
    slope_two = 0.0
    for chunk in range(chunks):
        at = pl.ds(chunk * step, step)
        unit = hid_ref[:, at].astype(F32) * (1.0 / hg_ref[:, at])
        slope = (sloped[:, at] - mean_slope - unit * mean_moved) * scale
        before_low = (slope * gp_ref[:, at].astype(F32)).astype(BF16)
        cb_ref[:, at] = before_low
        wide_acc[1, :, at] += fold(before_low.astype(F32))
        slope_two = slope_two + nt(before_low, wu[:, at])
    unit, scale = normalize(mixed_ref[...])
    n2_ref[...] = (unit * sg_ref[...]).astype(BF16)
    thin_acc[1] += fold(slope_two * unit)
    mixed = outer + norm_back(slope_two * sg_ref[...], unit, scale)
    cm_ref[...] = mixed
    mixed_low = mixed.astype(BF16)
    cl_ref[...] = mixed_low.T
    thin_acc[2] += fold(mixed_low.astype(F32))
    arrive(2)
    slope = nt(mixed_low, wo[...])
    unit, scale = normalize(at_ref[...])
    in_ref[...] = (unit * ig_ref[...]).astype(BF16)
    thin_acc[3] += fold(slope * unit)
    ch_ref[...] = norm_back(slope * ig_ref[...], unit, scale).astype(BF16)

    @pl.when(now == pl.num_programs(0) - 1)
    def _():
        inverse = 1.0 / hg_ref[...]
        wide_ref[0:1, :] = jnp.sum(wide_acc[0], axis=0, keepdims=True) * inverse
        wide_ref[1:2, :] = jnp.sum(wide_acc[1], axis=0, keepdims=True)
        for index in range(4):
            thin_ref[index:index + 1, :] = jnp.sum(thin_acc[index], axis=0, keepdims=True)


def feed_back(layer, sec, c, hidden, gp, st, mixed, attended, pack, wo, wu, wd, tb=256):
    rows, width = c.shape
    wide = wd[0].shape[0]
    const = lambda n, m=1: pl.BlockSpec((m, n), lambda i: (0, 0))
    tok = lambda n: pl.BlockSpec((tb, n), lambda i: (i, 0))
    turned = pl.BlockSpec((width, tb), lambda i: (0, i))
    S = jax.ShapeDtypeStruct
    return pl.pallas_call(
        functools.partial(feed_back_kernel, layer),
        grid=(rows // tb,),
        in_specs=[SMEM, tok(width), tok(wide), tok(wide), tok(128), tok(width), tok(width), pack_spec(layer, pack)] + [ANY] * 6,
        out_specs=[tok(wide), tok(width), turned, turned, tok(width), tok(width), tok(width), const(wide, 2), const(width, 4)],
        out_shape=[S((rows, wide), BF16), S((rows, width), F32), S((width, rows), BF16), S((width, rows), BF16), S((rows, width), BF16), S((rows, width), BF16), S((rows, width), BF16), S((2, wide), F32), S((4, width), F32)],
        scratch_shapes=[pltpu.VMEM(wo[0].shape, BF16), pltpu.VMEM(wu[0].shape, BF16), pltpu.VMEM(wd[0].shape, BF16),
                        pltpu.VMEM((tb, wide), F32), pltpu.VMEM((2, 8, wide), F32), pltpu.VMEM((4, 8, width), F32), pltpu.SemaphoreType.DMA((3,))],
        compiler_params=pltpu.CompilerParams(vmem_limit_bytes=VLIM),
        cost_estimate=pl.CostEstimate(flops=1 * 2 * rows * width * (2 * wide + width), bytes_accessed=50 * 1024 * 1024, transcendentals=0),
        name="feed_backward",
    )(sec, c, hidden, gp, st, mixed, attended, pack, *wo, *wu, *wd)


def attend_back_kernel(qb, q_ref, k_ref, v_ref, ch_ref, at_ref, cos_ref, sin_ref, cj_ref, kt, vt, qs, shares_ref, slope_ref):
    rows = q_ref.shape[1]
    lane = lane_iota((rows, 128))
    is_head = lane < HEAD_DIM
    slopes = ch_ref[...].astype(F32)
    product = slopes * at_ref[...]
    incoming = []
    for head in range(2):
        mine = is_head if head == 0 else jnp.logical_not(is_head)
        weighted = jnp.sum(jnp.where(mine, product, 0.0), axis=-1, keepdims=True)
        high, middle, low = split3(-weighted)
        feat = jnp.where(lane == 64, high.astype(F32), jnp.where(lane == 65, middle.astype(F32), jnp.where(lane == 66, low.astype(F32), 0.0)))
        local = slopes if head == 0 else pltpu.roll(slopes, 64, 1)
        incoming.append(jnp.where(is_head, local, feat).astype(BF16))
    blocks = rows // qb
    work = [(head, block) for head in range(2) for block in range(blocks)]
    ready = {}

    def score(index):
        if index < len(work):
            head, block = work[index]
            at = block * qb
            ready[index] = (
                nt(q_ref[head, pl.ds(at, qb), :], k_ref[head]),
                nt(incoming[head][at:at + qb], v_ref[head]),
            )

    score(0)
    for index, (head, block) in enumerate(work):
        score(index + 1)
        scores, turned = ready.pop(index)
        shares = jnp.exp(scores)
        slope = (shares * turned).astype(BF16)
        at = pl.ds(block * qb, qb)
        slope_ref[head, at, :] = slope
        shares_ref[head, at, :] = shares.astype(BF16)
        qs[head, at, :] = nn(slope, k_ref[head])
        if block == blocks - 1:
            rng = pl.ds(head * HEAD_DIM, HEAD_DIM)
            kt[rng, :] = nn(q_ref[head].T[:HEAD_DIM], slope_ref[head])
            vt[rng, :] = nn(incoming[head].T[:HEAD_DIM], shares_ref[head])
    cosine, sine = cos_ref[...], sin_ref[...]
    first = lane % HEAD_DIM < HEAD_DIM // 2

    def back(part):
        turned = jnp.where(first, pltpu.roll(part, 96, 1), pltpu.roll(part, 32, 1))
        return (part * cosine - turned * sine).astype(BF16)

    cj_ref[0] = back(jnp.where(is_head, qs[0], pltpu.roll(qs[1], 64, 1)) * HEAD_DIM ** -0.5)
    cj_ref[1] = back(kt[...].T)
    cj_ref[2] = vt[...].T.astype(BF16)


def attend_back(q, k, v, ch, attended, cosine, sine, begin=0, count=None, into=None, qb=256):
    heads, rows, _ = q.shape
    width = heads * HEAD_DIM
    count = heads // 2 - begin if count is None else count
    hd = pl.BlockSpec((2, rows, 128), lambda i: (i + begin, 0, 0))
    col = pl.BlockSpec((rows, 128), lambda i: (0, i + begin))
    con = pl.BlockSpec((rows, 128), lambda i: (0, 0))
    body = functools.partial(attend_back_kernel, qb)
    extra = () if into is None else (into,)

    def kernel(*refs):
        body(*refs[:7], *refs[7 + len(extra):])

    return pl.pallas_call(
        kernel,
        grid=(count,),
        in_specs=[hd, hd, hd, col, col, con, con] + [ANY] * len(extra),
        out_specs=pl.BlockSpec((3, rows, 128), lambda i: (0, 0, i + begin)),
        out_shape=jax.ShapeDtypeStruct((3, rows, width), BF16),
        input_output_aliases={7: 0} if extra else {},
        scratch_shapes=[pltpu.VMEM((128, rows), F32), pltpu.VMEM((128, rows), F32), pltpu.VMEM((2, rows, 128), F32),
                        pltpu.VMEM((2, rows, rows), BF16), pltpu.VMEM((2, rows, rows), BF16)],
        compiler_params=pltpu.CompilerParams(vmem_limit_bytes=VLIM),
        cost_estimate=pl.CostEstimate(flops=1 * 80 * count * rows * rows * HEAD_DIM, bytes_accessed=3 * count * 1024 * 1024, transcendentals=0),
        name="attention_backward",
    )(q, k, v, ch, attended, cosine, sine, *extra)


def qkv_back_kernel(layer, sec_ref, cj_ref, x_ref, cm_ref, pack_ref, own_ref, other_ref,
                    ci_ref, small_ref, w_ref, acc, sem):
    step = pl.program_id(0)
    arrive = fetch_weights(layer, sec_ref, [(own_ref, other_ref, w_ref)], sem)

    @pl.when(step == 0)
    def _():
        acc[...] = jnp.zeros_like(acc)

    width = x_ref.shape[-1]
    (gain_ref,) = vectors_of(pack_ref, width, FIRST_GAIN)
    arrive(0)
    slope = nt(cj_ref[0], w_ref[:, 0:width])
    for which in range(1, 3):
        slope = slope + nt(cj_ref[which], w_ref[:, which * width:(which + 1) * width])
    unit, scale = normalize(x_ref[...].astype(F32))
    acc[0] += fold(slope * unit)
    for which in range(3):
        acc[which + 1] += fold(cj_ref[which].astype(F32))
    ci_ref[...] = (cm_ref[...] + norm_back(slope * gain_ref[...], unit, scale)).astype(BF16)

    @pl.when(step == pl.num_programs(0) - 1)
    def _():
        for index in range(4):
            small_ref[index:index + 1, :] = jnp.sum(acc[index], axis=0, keepdims=True)


def qkv_back(layer, sec, cj, x, cm, pack, own, other, tb=256):
    rows, width = x.shape
    const = lambda n, m=1: pl.BlockSpec((m, n), lambda i: (0, 0))
    tok = lambda n: pl.BlockSpec((tb, n), lambda i: (i, 0))
    S = jax.ShapeDtypeStruct
    return pl.pallas_call(
        functools.partial(qkv_back_kernel, layer),
        grid=(rows // tb,),
        in_specs=[SMEM, pl.BlockSpec((3, tb, width), lambda i: (0, i, 0)), tok(width), tok(width), pack_spec(layer, pack), ANY, ANY],
        out_specs=[tok(width), const(width, 4)],
        out_shape=[S((rows, width), BF16), S((4, width), F32)],
        scratch_shapes=[pltpu.VMEM(own.shape, BF16), pltpu.VMEM((4, 8, width), F32), pltpu.SemaphoreType.DMA((1,))],
        compiler_params=pltpu.CompilerParams(vmem_limit_bytes=VLIM),
        cost_estimate=pl.CostEstimate(flops=1 * 2 * rows * width * 3 * width, bytes_accessed=16 * 1024 * 1024, transcendentals=0),
        name="joint_backward",
    )(sec, cj, x, cm, pack, own, other)


def feed_grads_kernel(sec_ref, order_ref, cb_ref, hid_ref, c_t, n2_ref, cm_t, in_ref, wide_ref, thin_ref,
                      keep_ref, send_ref, held, sem):
    step = pl.program_id(0)
    sec = sec_ref[0]
    parts = order_ref.shape[0] // 2
    width = n2_ref.shape[-1]
    half = width // 2
    wide = wide_ref.shape[-1]
    up_rows = wide // parts
    thin = width // parts
    span = cb_ref.shape[-1]
    subs = span // up_rows
    steps = pl.num_programs(0) // 2
    outs = (keep_ref, send_ref)
    last = 2 * up_rows + thin
    sides = [pl.ds(pl.multiple_of(which * half, 128), half) for which in (sec, 1 - sec)]

    def leave(side, at, begin, count):
        rows = pl.ds(begin, count)
        pltpu.make_async_copy(held.at[side, at, rows], outs[side].at[at, rows], sem).start()

    @pl.when(step == 0)
    def _():
        for window in range(wide // half):
            at = pl.ds(window * half, half)
            far = pl.ds(window // (wide // width // 1) * half, half)
            rows = jnp.concatenate([wide_ref[:, at], thin_ref[:, far], jnp.zeros((10, half), F32)], axis=0).astype(BF16)
            for side in range(2):
                for sub in range(half // up_rows):
                    held[side, order_ref[side * parts + window * (half // up_rows) + sub], last:, :] = rows
        for side in range(2):
            out = nn(cm_t[...], in_ref[:, sides[side]]).astype(BF16)
            for part in range(parts):
                at = order_ref[side * parts + part]
                held[side, at, 2 * up_rows:last, :] = out[thin * part:thin * (part + 1)]
                leave(side, at, 2 * up_rows, thin + 16)

    for side in range(2):
        up = tn(cb_ref[...], n2_ref[:, sides[side]]).astype(BF16)
        for sub in range(subs):
            at = order_ref[side * parts + step * subs + sub]
            held[side, at, 0:up_rows, :] = up[sub * up_rows:(sub + 1) * up_rows]
            leave(side, at, 0, up_rows)

    down = nn(c_t[...], hid_ref[...]).astype(BF16)
    side = step // steps
    for which in range(span // half):
        begin = pl.multiple_of(up_rows + thin * (step % steps * (span // half) + which), 16)
        for part in range(parts):
            held[side, order_ref[side * parts + part], pl.ds(begin, thin), :] = down[thin * part:thin * (part + 1), which * half:(which + 1) * half]

    begin = pl.multiple_of(up_rows + thin * (step % steps * (span // half)), 16)
    rows = pl.ds(begin, thin * (span // half))
    for number in range(2):
        @pl.when(side == number)
        def _():
            pltpu.make_async_copy(held.at[number, :, rows], outs[number].at[:, rows], sem).start()

    @pl.when(step == pl.num_programs(0) - 1)
    def _():
        for number in range(2):
            pltpu.make_async_copy(held.at[number], outs[number], sem).wait()


def feed_grads(sec, order, cb, hidden, c_t, n2, cm_t, inner, wide_sums, thin_sums):
    rows, width = n2.shape
    wide = cb.shape[-1]
    parts = order.shape[0] // 2
    half = width // 2
    steps = wide // width
    up_rows = wide // parts
    total = 2 * up_rows + width // parts + 16
    full = lambda n, m=rows: pl.BlockSpec((m, n), lambda i, s, o: (0, 0))
    out_shape = jax.ShapeDtypeStruct((parts, total, half), BF16)
    return pl.pallas_call(
        feed_grads_kernel,
        grid_spec=pltpu.PrefetchScalarGridSpec(
            num_scalar_prefetch=2,
            grid=(steps,),
            in_specs=[
                pl.BlockSpec((rows, width), lambda i, s, o: (0, i)),
                pl.BlockSpec((rows, width), lambda i, s, o: (0, jnp.where(i < steps // 2, s[0], 1 - s[0]) * (steps // 2) + i % (steps // 2))),
                full(rows, width), full(width), full(rows, width), full(width), full(wide, 2), full(width, 4),
            ],
            out_specs=[ANY, ANY],
            scratch_shapes=[pltpu.VMEM((2, parts, total, half), BF16), pltpu.SemaphoreType.DMA],
        ),
        out_shape=[out_shape, out_shape],
        compiler_params=pltpu.CompilerParams(vmem_limit_bytes=VLIM),
        cost_estimate=pl.CostEstimate(flops=1 * 2 * rows * width * (2 * wide + width), bytes_accessed=30 * 1024 * 1024, transcendentals=0),
        name="feed_gradients",
    )(sec, order, cb, hidden, c_t, n2, cm_t, inner, wide_sums, thin_sums)


def joint_grads_kernel(sec_ref, order_ref, cj_ref, n_ref, sums_ref, keep_ref, send_ref, found):
    step = pl.program_id(0)
    sec = sec_ref[0]
    parts = order_ref.shape[0] // 2
    width = n_ref.shape[-1]
    half = width // 2
    thick = 3 * width // parts
    outs = (keep_ref, send_ref)
    found[...] = tn(cj_ref[0], n_ref[...]).astype(BF16)
    for side, which in enumerate((sec, 1 - sec)):
        columns = pl.ds(pl.multiple_of(which * half, 128), half)
        for block in range(3):
            @pl.when(step == block)
            def _():
                for part in range(parts):
                    low, high = max(thick * part, width * block), min(thick * (part + 1), width * (block + 1))
                    if low < high:
                        at = order_ref[side * parts + part]
                        outs[side][at, low - thick * part:high - thick * part, :] = found[low - width * block:high - width * block, columns]

    @pl.when(step == 0)
    def _():
        for part in range(parts):
            window = thick * part // half
            rows = [sums_ref[1 + w // 2:2 + w // 2, w % 2 * half:w % 2 * half + half] for w in (window, min(window + 1, 5))]
            far = part // (parts // 2) * half
            rows = jnp.concatenate(rows + [sums_ref[0:1, far:far + half], jnp.zeros((13, half), F32)], axis=0).astype(BF16)
            for side in range(2):
                outs[side][order_ref[side * parts + part], thick:, :] = rows


def joint_grads(sec, order, cj, normed, sums):
    rows, width = normed.shape
    parts = order.shape[0] // 2
    half = width // 2
    thick = 3 * width // parts
    out_spec = pl.BlockSpec((parts, thick + 16, half), lambda i, s, o: (0, 0, 0))
    out_shape = jax.ShapeDtypeStruct((parts, thick + 16, half), BF16)
    return pl.pallas_call(
        joint_grads_kernel,
        grid_spec=pltpu.PrefetchScalarGridSpec(
            num_scalar_prefetch=2,
            grid=(3,),
            in_specs=[
                pl.BlockSpec((1, rows, width), lambda i, s, o: (i, 0, 0)),
                pl.BlockSpec((rows, width), lambda i, s, o: (0, 0)),
                pl.BlockSpec((4, width), lambda i, s, o: (0, 0)),
            ],
            out_specs=[out_spec, out_spec],
            scratch_shapes=[pltpu.VMEM((width, width), BF16)],
        ),
        out_shape=[out_shape, out_shape],
        compiler_params=pltpu.CompilerParams(vmem_limit_bytes=VLIM),
        cost_estimate=pl.CostEstimate(flops=1 * 6 * rows * width * width, bytes_accessed=14 * 1024 * 1024, transcendentals=0),
        name="joint_gradients",
    )(sec, order, cj, normed, sums)


def prepare_kernel(lengths, mine_ref, part_ref, seg_ref, rate_ref, *refs):
    vectors, (cos_ref, sin_ref, lab_ref, pack_ref) = refs[:len(lengths)], refs[len(lengths):]
    begin = 0
    for vector, length in zip(vectors, lengths):
        pack_ref[:, begin:begin + length] = vector[...]
        begin += length
    rows = seg_ref.shape[-1]
    piece = rows // 2
    second = jnp.full((1, 1), part_ref[0]) == 1
    row = seg_ref[0].astype(F32)
    turned = jnp.where(second, jnp.concatenate([row[:, piece:], row[:, :piece]], axis=1), row)
    labels = jnp.broadcast_to(turned, (128, rows)).T
    starts = jnp.zeros_like(labels)
    for document in range(1, 5):
        count = jnp.sum(jnp.where(row < document, 1.0, 0.0), axis=1, keepdims=True)
        starts = jnp.where(labels == document, count, starts)
    time = lax.broadcasted_iota(jnp.int32, labels.shape, 0).astype(F32)
    shift = jnp.where(second, jnp.where(time < piece, piece * 1.0, -piece * 1.0), 0.0)
    angle = (time + shift - starts) * rate_ref[...]
    lane = lane_iota(labels.shape)
    cos_ref[...] = jnp.cos(angle)
    sin_ref[...] = jnp.sin(angle) * jnp.where(lane % HEAD_DIM < HEAD_DIM // 2, -1.0, 1.0)
    lab_ref[...] = labels.astype(jnp.int32)


def prepare(mine, part, segments, vectors):
    rows = segments.shape[-1]
    lengths = tuple(vector.shape[-1] for vector in vectors)
    half = HEAD_DIM // 2
    rate = jnp.tile(1.0 / 10000.0 ** (jnp.arange(half, dtype=F32) * 2.0 / HEAD_DIM), 4)[None]
    whole = lambda m, n: pl.BlockSpec((m, n), lambda i, a, b: (0, 0))
    return pl.pallas_call(
        functools.partial(prepare_kernel, lengths),
        grid_spec=pltpu.PrefetchScalarGridSpec(
            num_scalar_prefetch=2,
            grid=(1,),
            in_specs=[pl.BlockSpec((1, 1, rows), lambda i, a, b: (a[0], 0, 0)), whole(1, 128)] + [whole(1, length) for length in lengths],
            out_specs=[whole(rows, 128), whole(rows, 128), whole(rows, 128), whole(1, sum(lengths))],
        ),
        out_shape=[jax.ShapeDtypeStruct((rows, 128), F32)] * 2 + [jax.ShapeDtypeStruct((rows, 128), jnp.int32), jax.ShapeDtypeStruct((1, sum(lengths)), F32)],
        compiler_params=pltpu.CompilerParams(vmem_limit_bytes=VLIM),
        name="row_tables",
    )(mine.reshape(1).astype(jnp.int32), part.reshape(1).astype(jnp.int32), segments, rate, *vectors)


def swap_pairs(change, sizes):
    sections, dps, seqs = sizes
    pairs = []
    for section in range(sections):
        for dp in range(dps):
            for seq in range(seqs):
                a, b, c = change(section, dp, seq)
                pairs.append(((section * dps + dp) * seqs + seq, (a * dps + b) * seqs + c))
    return pairs


FEED, JOINT = range(2)


class Reduction:
    def __init__(self, kept, sent, sizes):
        self.sizes = sizes
        self.kept, self.sent = kept, sent
        self.stage = 0
        self.result = None

    def send(self):
        if self.stage == 0:
            self.arrived = lax.ppermute(self.sent, "section", [(0, 1), (1, 0)])
        else:
            moves = (
                lambda s, d, q: (s, d ^ 1, q) if s == 0 else (s, d, q ^ 1),
                lambda s, d, q: (s, d, q ^ 1) if s == 0 else (s, d ^ 1, q),
                lambda s, d, q: (s, d ^ 2, q),
                lambda s, d, q: (s, d ^ 4, q),
            )
            self.arrived = lax.ppermute(self.sent, ("section", "dp", "seq"), swap_pairs(moves[self.stage - 1], self.sizes))
        self.stage += 1

    def add(self):
        kept, arrived = self.kept, self.arrived
        middle = kept.shape[0] // 2
        if middle == 0:
            self.result = kept[0].astype(F32) + arrived[0].astype(F32)
            return
        self.sent = (kept[middle:].astype(F32) + arrived[middle:].astype(F32)).astype(BF16)
        self.kept = (kept[:middle].astype(F32) + arrived[:middle].astype(F32)).astype(BF16)

    def finish(self):
        if self.result is not None:
            return self.result
        while self.stage < 5:
            self.add()
            self.send()
        self.add()
        return self.result


def advance(value, *moving):
    for item in moving:
        if item.stage:
            item.add()
    if all(item.stage == 5 for item in moving):
        results = [item.result for item in moving]
        value, results = lax.optimization_barrier((value, results))
        for item, result in zip(moving, results):
            item.result = result
        return value
    parts = [array for item in moving for array in (item.kept, item.sent)]
    value, parts = lax.optimization_barrier((value, parts))
    for index, item in enumerate(moving):
        item.kept, item.sent = parts[2 * index:2 * index + 2]
        item.send()
    return value


def last_kernel(cj_ref, n_ref, x_ref, cm_ref, pack_ref, own_ref, other_ref, feed_keep, feed_send, done_ref,
                out_ref, mine_ref, got_ref,
                w_ref, back, cj_t, acc, j_keep, j_send, r0, r1, r2, r3, r4, k1, k2, k3, k4, s1, s2, s3, s4,
                f1, f2, f3, fk2, fk3, fs2, fs3, swap_out, landed, send_sem, recv_sem, local_sem):
    s, d, q = (lax.axis_index(name) for name in ("section", "dp", "seq"))
    x = (s, d + 1 - 2 * (d % 2), q)
    y = (s, d, 1 - q)
    first = (s, (1 - s) * x[1] + s * d, (1 - s) * q + s * y[2])
    second = (s, s * x[1] + (1 - s) * d, s * q + (1 - s) * y[2])
    near = (s, d + 2 - 4 * (d // 2 % 2), q)
    far = (s, d + 4 - 8 * (d // 4), q)
    core = (1 - s, d, q)
    parts, thick, half = j_keep.shape
    thick -= 16
    width = n_ref.shape[-1]
    piece = got_ref.shape[1]

    @pl.when(s == 0)
    def _():
        pltpu.make_async_copy(own_ref, w_ref, local_sem).start()

    @pl.when(s == 1)
    def _():
        pltpu.make_async_copy(other_ref, w_ref, local_sem).start()

    barrier = pltpu.get_barrier_semaphore()
    across = (1 - s, d, 1 - q)
    for other in (core, x, y, near, far, across):
        pl.semaphore_signal(barrier, inc=1, device_id=other, device_id_type=pl.DeviceIdType.MESH)
    pl.semaphore_wait(barrier, 6)

    def ready(number, source, target, other):
        return pltpu.make_async_remote_copy(
            src_ref=source, dst_ref=target, send_sem=send_sem.at[number], recv_sem=recv_sem.at[number],
            device_id=other, device_id_type=pl.DeviceIdType.MESH)

    def send(number, source, target, other):
        copy = ready(number, source, target, other)
        copy.start()
        return copy

    def total(one, two):
        return one.astype(F32) + two.astype(F32)

    feed_rows = feed_keep.shape[1]
    feed_blocks = [pl.ds(number * (feed_rows // 2), feed_rows // 2) for number in range(2)]
    feed_flights = [send(number, feed_send.at[:, at], f1.at[:, at], second) for number, at in enumerate(feed_blocks)]
    (gain_ref,) = vectors_of(pack_ref, width, FIRST_GAIN)
    acc[...] = jnp.zeros_like(acc)
    tb = piece // 2
    rows = x_ref.shape[0]
    order = [2, 3, 0, 1]

    def slope_of(block):
        at = pl.ds(block * tb, tb)
        slope = nt(cj_ref[0, at], w_ref[:, 0:width])
        for which in range(1, 3):
            slope = slope + nt(cj_ref[which, at], w_ref[:, which * width:(which + 1) * width])
        return slope

    pltpu.make_async_copy(own_ref, w_ref, local_sem).wait()
    to_y = ready(16, back.at[pl.ds(piece, piece)], got_ref.at[0], (0, d, 1 - q))
    to_core = ready(17, back.at[pl.ds(0, piece)], got_ref.at[1], (0, d, q))
    to_across = ready(18, back.at[pl.ds(piece, piece)], got_ref.at[2], (0, d, 1 - q))
    later = slope_of(order[0])
    for number, block in enumerate(order):
        slope = later
        if number + 1 < len(order):
            later = slope_of(order[number + 1])
        at = pl.ds(block * tb, tb)
        unit, scale = normalize(x_ref[at, :].astype(F32))
        acc[0] += fold(slope * unit)
        for which in range(3):
            acc[which + 1] += fold(cj_ref[which, at].astype(F32))
        back[at, :] = (cm_ref[at, :] + norm_back(slope * gain_ref[...], unit, scale)).astype(BF16)
        if number == 1:
            @pl.when(s == 0)
            def _():
                to_y.start()
    mine_ref[...] = back[0:piece, :]

    sums = [jnp.sum(acc[number], axis=0, keepdims=True) for number in range(4)]
    for which in range(3):
        cj_t[which] = cj_ref[which].T

    def position(part, owner):
        bx, by = (part // 2 % 2 + d % 2) % 2, (part % 2 + q) % 2
        bz, cz = (part // 4 + d // 2) % 2, (part // 8 + d // 4) % 2
        depth = bz * 2 + cz
        return (1 - owner) * ((bx * 2 + by) * 4 + depth) + owner * ((by * 2 + bx) * 4 + depth)

    def gradients(target, owner):
        for block in range(3):
            found = nn(cj_t[block], n_ref[:, pl.ds(pl.multiple_of(owner * half, 128), half)]).astype(BF16)
            for part in range(parts):
                low, high = max(thick * part, width * block), min(thick * (part + 1), width * (block + 1))
                if low < high:
                    target[position(part, owner), low - thick * part:high - thick * part, :] = found[low - width * block:high - width * block]
        for part in range(parts):
            window = thick * part // half
            lines = [sums[1 + w // 2][:, w % 2 * half:w % 2 * half + half] for w in (window, min(window + 1, 5))]
            away = part // (parts // 2) * half
            lines = jnp.concatenate(lines + [sums[0][:, away:away + half], jnp.zeros((13, half), F32)], axis=0)
            target[position(part, owner), thick:, :] = lines.astype(BF16)

    gradients(j_send, 1 - s)
    blocks = [pl.ds(number * (thick + 16) // 2, (thick + 16) // 2) for number in range(2)]
    flights = [send(2 + number, j_send.at[:, at], r0.at[:, at], core) for number, at in enumerate(blocks)]
    for number, at in enumerate(feed_blocks):
        feed_flights[number].wait()
        fs2[:, at] = total(feed_keep[2:, at], f1[2:, at]).astype(BF16)
        feed_flights[number] = send(4 + number, fs2.at[:, at], f2.at[:, at], near)
        fk2[:, at] = total(feed_keep[:2, at], f1[:2, at]).astype(BF16)
    gradients(j_keep, s)
    kept, arrived = j_keep, r0
    for stage, (sent, held, target, other) in enumerate(
        ((s1, k1, r1, first), (s2, k2, r2, second), (s3, k3, r3, near), (s4, k4, r4, far))):
        middle = kept.shape[0] // 2
        for number, at in enumerate(blocks):
            flights[number].wait()
            sent[:, at] = total(kept[middle:, at], arrived[middle:, at]).astype(BF16)
            flights[number] = send(8 + 2 * stage + number, sent.at[:, at], target.at[:, at], other)
            held[:, at] = total(kept[:middle, at], arrived[:middle, at]).astype(BF16)
        kept, arrived = held, target
        if stage == 0:
            for number, at in enumerate(feed_blocks):
                feed_flights[number].wait()
                fs3[:, at] = total(fk2[1:, at], f2[1:, at]).astype(BF16)
                feed_flights[number] = send(6 + number, fs3.at[:, at], f3.at[:, at], far)
                fk3[:, at] = total(fk2[:1, at], f2[:1, at])
        if stage == 1:
            @pl.when(s == 1)
            def _():
                to_core.start()
                to_across.start()
    own = jnp.full((1, 1), s) == 0

    def settle(at, mine):
        done = done_ref[at, :]
        swap_out[at, :] = jnp.where(own, done, mine)
        out_ref[pl.ds(s, 1), at, :] = jnp.where(own, mine, done)[None]

    for number, at in enumerate(feed_blocks):
        feed_flights[number].wait()
        settle(at, fk3[0, at] + f3[0, at].astype(F32))
    for number, at in enumerate(blocks):
        flights[number].wait()
        settle(pl.ds(feed_rows + number * (thick + 16) // 2, (thick + 16) // 2), total(kept[0, at], arrived[0, at]))
    send(19, swap_out, landed, core).wait()
    out_ref[pl.ds(1 - s, 1)] = landed[...][None]

    @pl.when(s == 0)
    def _():
        to_y.wait_send()
        for copy in (to_y, to_core, to_across):
            copy.wait_recv()

    @pl.when(s == 1)
    def _():
        to_core.wait_send()
        to_across.wait_send()


def last_step(cj, normed, state, cm, pack, own, other, feed_keep, feed_send, done, parts):
    rows, width = state.shape
    half, piece = width // 2, rows // 2
    thick = 3 * width // parts + 16
    feed_rows = feed_keep.shape[1]
    vm = pl.BlockSpec(memory_space=pltpu.VMEM)
    level = lambda n, m=thick, t=BF16: pltpu.VMEM((n, m, half), t)
    steps = [parts >> number for number in range(1, 5)]
    S = jax.ShapeDtypeStruct
    return pl.pallas_call(
        last_kernel,
        in_specs=[vm] * 5 + [ANY] * 2 + [vm] * 3,
        out_specs=[vm] * 3,
        out_shape=[S((2, feed_rows + thick, half), F32), S((piece, width), BF16), S((3, piece, width), BF16)],
        scratch_shapes=[pltpu.VMEM(own.shape, BF16), pltpu.VMEM((rows, width), BF16), pltpu.VMEM((3, width, rows), BF16),
                        pltpu.VMEM((4, 8, width), F32)]
        + [level(parts)] * 3 + [level(n) for n in steps] * 3
        + [level(4, feed_rows), level(2, feed_rows), level(1, feed_rows), level(2, feed_rows), level(1, feed_rows, F32),
           level(2, feed_rows), level(1, feed_rows)]
        + [pltpu.VMEM((feed_rows + thick, half), F32)] * 2
        + [pltpu.SemaphoreType.DMA((20,)), pltpu.SemaphoreType.DMA((20,)), pltpu.SemaphoreType.DMA],
        compiler_params=pltpu.CompilerParams(collective_id=0, has_side_effects=True, vmem_limit_bytes=VLIM),
        cost_estimate=pl.CostEstimate(flops=0, bytes_accessed=100 * 1024 * 1024, transcendentals=0),
        name="last_step",
    )(cj, normed, state, cm, pack, own, other, feed_keep, feed_send, done)


def assemble_kernel(parts, index_ref, both_ref, joint_ref, jb_ref, out_ref, ob_ref, up_ref, ub_ref, down_ref, db_ref,
                    fg_ref, ig_ref, sg_ref, hg_ref):
    half = both_ref.shape[-1]
    index = index_ref[0]
    up_rows, thin, thick = up_ref.shape[0], out_ref.shape[0], joint_ref.shape[0]
    steps = up_rows // thin
    for side in range(2):
        at = pl.ds(side * half, half)
        up_ref[:, at] = both_ref[side, 0:up_rows, :]
        for step in range(steps):
            begin = up_rows + step * thin
            down_ref[:, pl.ds((side * steps + step) * half, half)] = both_ref[side, begin:begin + thin, :]
        begin = 2 * up_rows
        out_ref[:, at] = both_ref[side, begin:begin + thin, :]
        begin = 2 * up_rows + thin + 16
        joint_ref[:, at] = both_ref[side, begin:begin + thick, :]

    def cut(row, count, target):
        begin = index * count % half
        best = row[:, 0:count]
        for number in range(1, half // count):
            best = jnp.where(jnp.full((1, 1), begin) == number * count, row[:, number * count:(number + 1) * count], best)
        target[...] = best

    at = 2 * up_rows + thin
    for number, (target, count) in enumerate(((hg_ref, up_rows), (ub_ref, up_rows), (db_ref, thin), (sg_ref, thin), (ob_ref, thin), (ig_ref, thin))):
        cut(both_ref[0, at + number:at + number + 1, :], count, target)
    at += 16 + thick
    cut(both_ref[0, at + 2:at + 3, :], thin, fg_ref)
    line = jnp.concatenate([both_ref[0, at:at + 1, :], both_ref[0, at + 1:at + 2, :]], axis=1)
    best = line[:, 0:thick]
    for part in range(1, parts):
        begin = part * thick % half
        best = jnp.where(jnp.full((1, 1), index) == part, line[:, begin:begin + thick], best)
    jb_ref[...] = best


def assemble(index, both, parts, width):
    wide = 4 * width
    S = lambda *shape: jax.ShapeDtypeStruct(shape, F32)
    vm = pl.BlockSpec(memory_space=pltpu.VMEM)
    thin, up_rows, thick = width // parts, wide // parts, 3 * width // parts
    results = pl.pallas_call(
        functools.partial(assemble_kernel, parts),
        in_specs=[SMEM, vm],
        out_specs=[vm] * 12,
        out_shape=[S(thick, width), S(1, thick), S(thin, width), S(1, thin), S(up_rows, width), S(1, up_rows),
                   S(thin, wide), S(1, thin), S(1, thin), S(1, thin), S(1, thin), S(1, up_rows)],
        compiler_params=pltpu.CompilerParams(vmem_limit_bytes=VLIM),
        name="gradient_outputs",
    )(index.reshape(1).astype(jnp.int32), both)
    return tuple(item.T[None] if number in (0, 2, 4, 6) else item for number, item in enumerate(results))


def row_step(
    sizes,
    tokens,
    segments,
    cotangent,
    joint_weight,
    joint_bias,
    output_weight,
    output_bias,
    up_weight,
    up_bias,
    down_weight,
    down_bias,
    first_gain,
    inner_gain,
    second_gain,
    hidden_gain,
):
    micro, row_count, piece, width = tokens.shape
    rows = 2 * piece
    wide = up_weight.shape[-1]
    parts = sizes[1] * sizes[2]
    half = width // 2
    section = lax.axis_index("section")
    part = lax.axis_index("seq")
    data = lax.axis_index("dp")
    sec = section.reshape(1).astype(jnp.int32)
    mine = 2 * section + part
    swap = [(0, 1), (1, 0)]

    def pick(array, index):
        return lax.dynamic_index_in_dim(array, index, 0, keepdims=False)

    flat_tokens = tokens.reshape(micro * row_count, piece, width)
    beside = lax.ppermute(pick(flat_tokens, mine ^ 1), "seq", swap)
    both = [(own[0], lax.ppermute(own[0], "section", swap)) for own in (joint_weight, output_weight, up_weight, down_weight)]
    joint_pair, output_pair, up_pair, down_pair = both
    cosine, sine, labels, own = prepare(mine, part, segments.reshape(micro * row_count, 1, rows), (
        joint_bias, output_bias, up_bias, down_bias, first_gain, inner_gain, second_gain, hidden_gain))
    other = lax.ppermute(own, "section", swap)
    pack = jnp.where(section == 0, jnp.stack([own, other]), jnp.stack([other, own]))

    mx, my, mz = data % 2, part, data // 2
    index = jnp.arange(parts, dtype=jnp.int32)
    cx, cy, cz = (index // 2) % 2 ^ mx, index % 2 ^ my, index // 4 ^ mz
    depth = cz % 2 * 2 + cz // 2
    order_x, order_y = (cx * 2 + cy) * 4 + depth, (cy * 2 + cx) * 4 + depth
    order = jnp.where(section == 0, jnp.concatenate([order_x, order_y]), jnp.concatenate([order_y, order_x]))

    kept = []
    hiddens = []
    for layer in range(2):
        if layer == 0:
            state, normed, q, k, v = qkv(layer, sec, (flat_tokens, beside), pack, *joint_pair, cosine, sine, labels, mine)
            state, cotangent = lax.optimization_barrier((state, cotangent))
            flat = cotangent.reshape(micro * row_count, piece, width)
            slope = jnp.concatenate([pick(flat, mine), lax.ppermute(pick(flat, mine ^ 1), "seq", swap)], axis=0)
        else:
            _, normed, q, k, v = qkv(layer, sec, state, pack, *joint_pair, cosine, sine, labels, mine)
        attended, query = attend(q, k, v)
        result, mixed, hidden, bend, stats = feed(layer, sec, attended, state, pack, output_pair, up_pair, down_pair)
        kept.append((state, normed, query, k, v, attended, mixed, hidden, bend, stats))
        hiddens.append(result)
        state = result

    def halves(item):
        return item[:piece], item[piece:]

    every = ("section", "seq")
    blocks = []
    for fs, fq in ((0, 1), (1, 0), (1, 1)):
        first, second = (halves(item)[fq] for item in hiddens)
        owed = jnp.where(section == fs, first, second)
        blocks.append((owed, [(2 * s + q, 2 * (s ^ fs) + (q ^ fq)) for s in range(2) for q in range(2)]))
    slope, owed = lax.optimization_barrier((slope, [block for block, pairs in blocks]))
    gathered = [lax.ppermute(block, every, pairs) for block, (_, pairs) in zip(owed, blocks)]
    own = jnp.where(section == 0, halves(hiddens[0])[0], halves(hiddens[1])[0])

    def place(blocks):
        stacked = jnp.stack(blocks)
        return jnp.stack([pick(stacked, mine ^ index) for index in range(4)]).reshape(1, micro, row_count, piece, width)

    def deliver(layer, back):
        own, other = halves(back)
        moves = (
            (other, [(2 * layer + q, 2 * layer + (q ^ 1)) for q in range(2)]),
            (own, [(2 * (1 - layer) + q, 2 * layer + q) for q in range(2)]),
            (other, [(2 * (1 - layer) + q, 2 * layer + (q ^ 1)) for q in range(2)]),
        )
        return [own] + [lax.ppermute(block, every, pairs) for block, pairs in moves]

    flights = {}
    delivered = [None, None]

    for layer in (1, 0):
        state, normed, query, k, v, attended, mixed, hidden, bend, stats = kept[layer]
        cb, cm, slope_t, mixed_t, ch, n2, inner, wide_sums, thin_sums = feed_back(
            layer, sec, slope, hidden, bend, stats, mixed, attended, pack, output_pair, up_pair, down_pair)
        if layer == 0:
            cb = advance(cb, flights[FEED, 1], flights[JOINT, 1])
        flights[FEED, layer] = Reduction(*feed_grads(sec, order, cb, hidden, slope_t, n2, mixed_t, inner, wide_sums, thin_sums), sizes)
        if layer == 1:
            ch = advance(ch, flights[FEED, 1])
            cj = attend_back(query, k, v, ch, attended, cosine, sine)
            cj, gathered = lax.optimization_barrier((cj, gathered))
            cj = advance(cj, flights[FEED, 1])
        else:
            ch, delivered[1] = lax.optimization_barrier((ch, delivered[1]))
            ch = advance(ch, flights[FEED, 0], flights[FEED, 1], flights[JOINT, 1])
            count = 2
            cj = attend_back(query, k, v, ch, attended, cosine, sine, 0, count)
            cj = advance(cj, flights[FEED, 0], flights[FEED, 1], flights[JOINT, 1])
            cj = attend_back(query, k, v, ch, attended, cosine, sine, count, None, cj)
            cj = advance(cj, flights[FEED, 1])
            flights[JOINT, 1].add()
            flights[JOINT, 1].send()
            flights[FEED, 0].add()
        if layer == 0:
            break
        back, sums = qkv_back(layer, sec, cj, state, cm, pack, *joint_pair)
        delivered[layer] = deliver(layer, back)
        flights[JOINT, layer] = Reduction(*joint_grads(sec, order, cj, normed, sums), sizes)
        if layer == 1:
            back = advance(back, flights[JOINT, 1])
        slope = back
    before = flights[FEED, 0]
    done = jnp.concatenate([flights[FEED, 1].finish(), flights[JOINT, 1].finish()], axis=0)
    both, ours, got = last_step(cj, normed, state, cm, pack, *joint_pair, before.kept, before.sent, done, parts)
    hiddens = place([own] + gathered)
    input_gradients = place([jnp.where(section == 0, a, b) for a, b in zip((ours, got[0], got[1], got[2]), delivered[1])]).astype(F32)

    return (hiddens, input_gradients) + tuple(assemble(2 * data + part, both, parts, width))


def choose(sizes, *arrays):
    micro, row_count, piece, width = arrays[0].shape
    if sizes == (2, 8, 2) and micro * row_count == 4:
        return row_step(sizes, *arrays)
    return shards(*arrays)


def solution(mesh):
    axes = ("section", "dp", "seq")
    return jax.shard_map(
        functools.partial(choose, tuple(mesh.shape[name] for name in axes)),
        mesh=mesh,
        in_specs=(
            P(None, "dp", "seq", None),
            P(None, "dp", None),
            P(None, "dp", "seq", None),
            P("section", None, None),
            P("section", None),
            P("section", None, None),
            P("section", None),
            P("section", None, None),
            P("section", None),
            P("section", None, None),
            P("section", None),
            P("section", None),
            P("section", None),
            P("section", None),
            P("section", None),
        ),
        out_specs=(
            P("section", None, "dp", "seq", None),
            P("section", None, "dp", "seq", None),
            P("section", None, ("dp", "seq")),
            P("section", ("dp", "seq")),
            P("section", None, ("dp", "seq")),
            P("section", ("dp", "seq")),
            P("section", None, ("dp", "seq")),
            P("section", ("dp", "seq")),
            P("section", None, ("dp", "seq")),
            P("section", ("dp", "seq")),
            P("section", ("dp", "seq")),
            P("section", ("dp", "seq")),
            P("section", ("dp", "seq")),
            P("section", ("dp", "seq")),
        ),
        check_vma=False,
    )
```
